32 devices in a mesh: dp: 16 (over z, x, core), tensor: 2 (over y).
Axes of the slice: x: 2, y: 2, z: 4, core: 2. Of those that a mesh axis runs over, the one named last changes fastest.
Arguments:
- tokens: bfloat16 [16384, 768], P(('dp', 'tensor')), may hold values from -6 to 6
- lengths: int32 [32], P('dp'), may hold values from 224 to 512, as said below
- cotangent: bfloat16 [16384, 768], P(('dp', 'tensor')), may hold values from -6 to 6
- norm_gain: float32 [2, 2, 768], replicated, may hold values from 0.25 to 1.75
- norm_shift: float32 [2, 2, 768], replicated, may hold values from -1.75 to 1.75
- qkv_weight: bfloat16 [2, 768, 3, 768], P(None, 'dp', None, 'tensor'), may hold values from -0.21875 to 0.21875
- qv_bias: float32 [2, 2, 768], P(None, None, 'tensor'), may hold values from -1.75 to 1.75
- out_weight: bfloat16 [2, 768, 768], P(None, 'tensor', 'dp'), may hold values from -2 to 2
- up_weight: bfloat16 [2, 768, 3072], P(None, 'dp', 'tensor'), may hold values from -0.21875 to 0.21875
- up_bias: float32 [2, 3072], P(None, 'tensor'), may hold values from -1.75 to 1.75
- down_weight: bfloat16 [2, 3072, 768], P(None, 'tensor', 'dp'), may hold values from -0.109375 to 0.109375
- out_bias: float32 [2, 2, 768], replicated, may hold values from -1.75 to 1.75
Outputs:
- final: bfloat16 [16384, 768], P(('dp', 'tensor'))
- token_grad: float32 [16384, 768], P(('dp', 'tensor'))
- grad_norm_gain: float32 [2, 2, 768], replicated
- grad_norm_shift: float32 [2, 2, 768], replicated
- grad_qkv_weight: float32 [2, 768, 3, 768], P(None, 'dp', None, 'tensor')
- grad_qv_bias: float32 [2, 2, 768], P(None, None, 'tensor')
- grad_out_weight: float32 [2, 768, 768], P(None, 'tensor', 'dp')
- grad_up_weight: float32 [2, 768, 3072], P(None, 'dp', 'tensor')
- grad_up_bias: float32 [2, 3072], P(None, 'tensor')
- grad_down_weight: float32 [2, 3072, 768], P(None, 'tensor', 'dp')
- grad_out_bias: float32 [2, 2, 768], replicated
The draws below stay inside these ranges and needn't reach their ends.
Inputs may be any that keep to these rules, and one draw needn't show every extreme that they name: `lengths`: each clip holds 224 to 512 patches; clip 0 holds exactly 512.
All inputs are finite; a program needn't handle non-finite values.
Results may differ from the reference program's by a relative error of at most 0.015.
Values may be sent and summed in bfloat16 or wider, within the bound.
A program may use at most 192 MiB of HBM per device.

```python
import math
import jax
import jax.numpy as jnp
from jax import lax

D = 768
HEAD_DIM = 64
FF = 3072
LAYERS = 2
SLOT = 512
MINLEN = 224
CLIPS = 32
TOKENS = 16384


def draw_lengths(key, part):
    values = jax.random.randint(key, (CLIPS,), MINLEN, SLOT + 1)
    return values.at[0].set(SLOT).astype(jnp.int32)


def block_levels(rng, shape, split, low, high):
    def one(position, shards_of):
        steps = jax.random.uniform(jax.random.fold_in(jax.random.fold_in(rng, 6), position), (shards_of,), jnp.float32, low / len(split), high / len(split))
        return jnp.repeat(jnp.exp(steps), shape[position] // shards_of).reshape((-1,) + (1,) * (len(shape) - position - 1))

    loudness = one(*split[0])
    for cut in split[1:]:
        loudness = loudness * one(*cut)
    return loudness


def gaussian(key, extent, scale, bound, split=(), kind=jnp.bfloat16):
    loudness = block_levels(key, extent, split, -0.22, 0.18) if split else 1.0
    values = jax.random.normal(key, extent, jnp.float32) * scale * loudness
    return jnp.minimum(jnp.maximum(values, -bound), bound).astype(kind)


def setup_inputs(seed: int = 0) -> dict:
    splits = jax.random.split(jax.random.key(seed), 13)
    return {
        "tokens": gaussian(splits[0], (TOKENS, D), 1.0, 6.0, ((0, 32),)),
        "lengths": draw_lengths(jax.random.fold_in(splits[12], 71), 0),
        "cotangent": gaussian(splits[2], (TOKENS, D), 1.0, 6.0, ((0, 32),)),
        "norm_gain": jnp.clip(1.0 + 0.15 * jax.random.normal(splits[3], (LAYERS, 2, D), jnp.float32), 0.25, 1.75),
        "norm_shift": gaussian(splits[4], (LAYERS, 2, D), 0.3, 1.75, (), jnp.float32),
        "qkv_weight": gaussian(splits[5], (LAYERS, D, 3, D), D ** -0.5, 0.21875, ((1, 16), (3, 2))),
        "qv_bias": gaussian(splits[6], (LAYERS, 2, D), 0.3, 1.75, ((2, 2),), jnp.float32),
        "out_weight": gaussian(splits[7], (LAYERS, D, D), 8 ** -0.5, 2.0, ((1, 2), (2, 16))),
        "up_weight": gaussian(splits[8], (LAYERS, D, FF), D ** -0.5, 0.21875, ((1, 16), (2, 2))),
        "up_bias": gaussian(splits[9], (LAYERS, FF), 0.3, 1.75, ((1, 2),), jnp.float32),
        "down_weight": gaussian(splits[10], (LAYERS, FF, D), FF ** -0.5, 0.109375, ((1, 2), (2, 16))),
        "out_bias": gaussian(splits[11], (LAYERS, 2, D), 0.3, 1.75, (), jnp.float32),
    }


EPSILON = 1e-06
HIGHEST = lax.Precision.HIGHEST

@jax.custom_vjp
def low(v):
    return lax.optimization_barrier(v.astype(jnp.bfloat16)).astype(jnp.float32)

@jax.custom_vjp
def low_back(v):
    return v

def low_keep(v):
    return (low(v), None)

def low_pass(kept, grad):
    return (grad,)

def back_keep(v):
    return (v, None)

def back_low(kept, grad):
    return (low(grad),)
low.defvjp(low_keep, low_pass)
low_back.defvjp(back_keep, back_low)

def layer_norm(inputs, gain_row, shift_row):
    centered = inputs - lax.optimization_barrier(jnp.mean(inputs, axis=-1, keepdims=True))
    variance = lax.optimization_barrier(jnp.mean(centered * centered, axis=-1, keepdims=True))
    return centered * lax.rsqrt(variance + EPSILON) * gain_row + shift_row

def encoder_layer(params, index, inputs, key_mask):
    norm_gain, norm_shift, qkv_weight, qv_bias, out_weight, up_weight, up_bias, down_weight, out_bias = params
    clip_count = key_mask.shape[0]
    model_width = qkv_weight.shape[3]
    head_count = model_width // HEAD_DIM
    normed = low(layer_norm(inputs, norm_gain[index, 0], norm_shift[index, 0]))
    zeros_row = jnp.zeros_like(qv_bias[index, 0])
    bias_rows = jnp.stack([qv_bias[index, 0], zeros_row, qv_bias[index, 1]])
    project = jnp.einsum('nd,dtc->ntc', normed, qkv_weight[index], precision=HIGHEST) + bias_rows
    project = low_back(low(project))
    blocks = project.reshape(clip_count, SLOT, 3, head_count, HEAD_DIM)
    scores = jnp.einsum('cqhd,ckhd->chqk', blocks[:, :, 0], blocks[:, :, 1], precision=HIGHEST) * HEAD_DIM ** (-0.5)
    scores = low_back(scores)
    scores = jnp.where(key_mask[:, None, None, :], scores, -1e+30)
    probs_low = low(jax.nn.softmax(scores, axis=-1))
    attended = jnp.einsum('chqk,ckhd->cqhd', probs_low, blocks[:, :, 2], precision=HIGHEST)
    attended = low_back(low(attended.reshape(clip_count * SLOT, model_width)))
    branch = low_back(jnp.dot(attended, out_weight[index], precision=HIGHEST))
    middle = inputs + branch + out_bias[index, 0]
    normed_mid = low(layer_norm(middle, norm_gain[index, 1], norm_shift[index, 1]))
    hidden = low_back(jnp.dot(normed_mid, up_weight[index], precision=HIGHEST) + up_bias[index])
    activated = low(jax.nn.gelu(hidden, approximate=False))
    branch_mlp = low_back(jnp.dot(activated, down_weight[index], precision=HIGHEST))
    return middle + branch_mlp + out_bias[index, 1]

def reference(tokens, lengths, cotangent, norm_gain, norm_shift, qkv_weight, qv_bias, out_weight, up_weight, up_bias, down_weight, out_bias):
    params = tuple((array.astype(jnp.float32) for array in (norm_gain, norm_shift, qkv_weight, qv_bias, out_weight, up_weight, up_bias, down_weight, out_bias)))
    group_size = math.gcd(CLIPS, max(1, 4096 // SLOT))
    group_count = CLIPS // group_size
    inputs = tokens.astype(jnp.float32).reshape(group_count, group_size * SLOT, D)
    cotangents = cotangent.astype(jnp.float32).reshape(group_count, group_size * SLOT, D)
    clip_lengths = lengths.reshape(group_count, group_size)

    def one_group(totals, group_item):
        block_in, block_cot, block_len = group_item
        key_mask = jnp.arange(SLOT, dtype=jnp.int32)[None, :] < block_len[:, None]
        row_mask = key_mask.reshape(-1, 1).astype(jnp.float32)

        def forward(weights, stream):
            for index in range(LAYERS):
                stream = encoder_layer(weights, index, stream, key_mask)
            return stream
        output, pullback = jax.vjp(forward, params, block_in)
        grad_params, grad_in = pullback(block_cot * row_mask)
        totals = jax.tree.map(lambda left, right: left + right, totals, grad_params)
        return (totals, (output.astype(jnp.bfloat16), grad_in))
    start = jax.tree.map(jnp.zeros_like, params)
    totals, (outputs, grads) = lax.scan(one_group, start, (inputs, cotangents, clip_lengths))
    return (outputs.reshape(TOKENS, D), grads.reshape(TOKENS, D), totals[0], totals[1], totals[2], totals[3], totals[4], totals[5], totals[6], totals[7], totals[8])
```

```python
import functools

import jax
import jax.numpy as jnp
from jax import lax
from jax.experimental import pallas as pl
from jax.experimental.pallas import tpu as pltpu
from jax.sharding import PartitionSpec as P

HEAD_DIM = 64
EPSILON = 1e-06
MESH = pl.DeviceIdType.MESH
VMEM_LIMIT = 60 * 2**20
BF16 = jnp.bfloat16
F32 = jnp.float32
ITEM_COUNT = 8
GATHER_ORDER = (0, 1, 2, 3, 4, 5, 6, 7)
REDUCE_ORDER = (7, 6, 5, 4, 3, 2, 1, 0)


def places():
    dp = lax.axis_index("dp")
    y = lax.axis_index("tensor")
    return dp // 4, (dp // 2) % 2, dp % 2, y


def partners(z, x, k, y):
    def at(z_, x_, k_, y_):
        return {"dp": (z_ * 2 + x_) * 2 + k_, "tensor": y_}

    along_z = [at((z + step) % 4, x, k, y) for step in (1, 2, 3)]
    return along_z + [at(z, 1 - x, k, y), at(z, x, k, 1 - y), at(z, x, 1 - k, y)]


def greet(peers):
    barrier = pltpu.get_barrier_semaphore()
    for peer in peers:
        pl.semaphore_signal(barrier, inc=1, device_id=peer, device_id_type=MESH)
    pl.semaphore_wait(barrier, len(peers))


def gather_kernel(*refs):
    own, out = refs[:ITEM_COUNT], refs[ITEM_COUNT : 2 * ITEM_COUNT]
    held = refs[2 * ITEM_COUNT : 3 * ITEM_COUNT]
    send, recv, local = refs[3 * ITEM_COUNT :]
    z, x, k, y = places()
    peers = partners(z, x, k, y)
    mine = [
        pltpu.make_async_copy(own[i], held[i].at[y, z, x, k], local.at[i])
        for i in range(ITEM_COUNT)
    ]
    for copy in mine:
        copy.start()
    greet(peers)

    def remote(i, ref, slot, peer):
        return pltpu.make_async_remote_copy(
            ref, ref, send.at[i, slot], recv.at[i, slot], device_id=peers[peer], device_id_type=MESH
        )

    def copies(i, phase):
        b = held[i]
        if phase == 0:
            return [remote(i, b.at[y, z, x, k], j, j) for j in range(3)]
        if phase == 1:
            return [remote(i, b.at[y, 0:2, x, k], 3, 3), remote(i, b.at[y, 2:4, x, k], 4, 4)]
        if phase == 2:
            return [remote(i, b.at[y, 0:2, :, k], 5, 4), remote(i, b.at[:, 2:4, x, k], 6, 3)]
        return [remote(i, b.at[:, :, :, k], 7, 5)]

    live = {}

    def begin(i, phase):
        if phase == 0:
            mine[i].wait()
        live[i, phase] = copies(i, phase)
        for copy in live[i, phase]:
            copy.start()

    def finish(i, phase):
        for copy in live.pop((i, phase)):
            copy.wait()

    order = GATHER_ORDER
    begin(order[0], 0)
    begin(order[1], 0)
    back = []
    for turn in range(ITEM_COUNT + 3):
        for phase in (3, 2, 1, 0):
            spot = turn - phase
            if 0 <= spot < ITEM_COUNT:
                finish(order[spot], phase)
                if phase < 3:
                    begin(order[spot], phase + 1)
                else:
                    i = order[spot]
                    copy = pltpu.make_async_copy(held[i], out[i], local.at[i])
                    copy.start()
                    back.append(copy)
                if phase == 0 and spot + 2 < ITEM_COUNT:
                    begin(order[spot + 2], 0)
    for copy in back:
        copy.wait()


def gather_weights(shards):
    widths = [s.shape[-1] for s in shards]
    full = [(2, 4, 2, 2, 48, w) for w in widths]
    return pl.pallas_call(
        gather_kernel,
        out_shape=[jax.ShapeDtypeStruct(f, BF16) for f in full],
        in_specs=[pl.BlockSpec(memory_space=pl.ANY)] * ITEM_COUNT,
        out_specs=[pl.BlockSpec(memory_space=pl.ANY)] * ITEM_COUNT,
        scratch_shapes=[pltpu.VMEM(f, BF16) for f in full]
        + [
            pltpu.SemaphoreType.DMA((ITEM_COUNT, 8)),
            pltpu.SemaphoreType.DMA((ITEM_COUNT, 8)),
            pltpu.SemaphoreType.DMA((ITEM_COUNT,)),
        ],
        compiler_params=pltpu.CompilerParams(
            collective_id=0, has_side_effects=True, vmem_limit_bytes=VMEM_LIMIT
        ),
        name="gather_weights",
    )(*shards)


def add_into(target, source, blocks, width):
    for at_target, at_source in blocks:
        for start in range(0, width, 384):
            stop = pl.ds(start, 384)
            total = target[(*at_target, slice(None), stop)].astype(F32) + source[
                (*at_source, slice(None), stop)
            ].astype(F32)
            target[(*at_target, slice(None), stop)] = total.astype(target.dtype)


def reduce_kernel(*refs):
    n = ITEM_COUNT
    grads, out = refs[:n], refs[n : 2 * n]
    held, from_core, from_a, from_b, from_c, from_d, from_z = (
        refs[(2 + j) * n : (3 + j) * n] for j in range(7)
    )
    send, recv, local = refs[9 * n :]
    z, x, k, y = places()
    peers = partners(z, x, k, y)
    mine = [
        pltpu.make_async_copy(grads[i].at[:, :, :, k], held[i], local.at[i]) for i in range(n)
    ]
    for copy in mine:
        copy.start()
    greet(peers)

    def remote(i, source, target, slot, peer):
        return pltpu.make_async_remote_copy(
            source, target, send.at[i, slot], recv.at[i, slot], device_id=peers[peer], device_id_type=MESH
        )

    def copies(i, phase):
        b = held[i]
        if phase == 0:
            return [remote(i, grads[i].at[:, :, :, 1 - k], from_core[i], 0, 5)]
        if phase == 1:
            return [
                remote(i, b.at[1 - y, 0:2], from_a[i], 1, 4),
                remote(i, b.at[:, 2:4, 1 - x], from_b[i], 2, 3),
            ]
        if phase == 2:
            return [
                remote(i, b.at[y, 0:2, 1 - x], from_c[i], 3, 3),
                remote(i, b.at[1 - y, 2:4, x], from_d[i], 4, 4),
            ]
        return [
            remote(i, b.at[y, (z + 1 + j) % 4, x], from_z[i].at[j], 5 + j, j) for j in range(3)
        ]

    def total(i, phase):
        b = held[i]
        width = b.shape[-1]
        if phase == 0:
            mine[i].wait()

            def block(t, carry):
                at = (t // 8, (t // 2) % 4, t % 2)
                add_into(b, from_core[i], [(at, at)], width)
                return carry

            lax.fori_loop(0, 16, block, 0)
        elif phase == 1:
            def block(t, carry):
                p, q = t // 2, t % 2
                add_into(b, from_a[i], [((y, p, q), (p, q))], width)
                add_into(b, from_b[i], [((p, 2 + q, x), (p, q))], width)
                return carry

            lax.fori_loop(0, 4, block, 0)
        elif phase == 2:
            def block(t, carry):
                add_into(b, from_c[i], [((y, t, x), (t,))], width)
                add_into(b, from_d[i], [((y, 2 + t, x), (t,))], width)
                return carry

            lax.fori_loop(0, 2, block, 0)
        else:
            for start in range(0, width, 384):
                cols = pl.ds(start, 384)
                value = b[y, z, x, :, cols].astype(F32)
                for j in range(3):
                    value += from_z[i][j, :, cols].astype(F32)
                out[i][:, cols] = value

    live = {}

    def begin(i, phase):
        live[i, phase] = copies(i, phase)
        for copy in live[i, phase]:
            copy.start()

    def finish(i, phase):
        for copy in live.pop((i, phase)):
            copy.wait()
        total(i, phase)

    order = REDUCE_ORDER
    begin(order[0], 0)
    begin(order[1], 0)
    for turn in range(n + 3):
        for phase in (3, 2, 1, 0):
            spot = turn - phase
            if 0 <= spot < n:
                finish(order[spot], phase)
                if phase < 3:
                    begin(order[spot], phase + 1)
                if phase == 0 and spot + 2 < n:
                    begin(order[spot + 2], 0)


def reduce_gradients(grads):
    widths = [g.shape[-1] for g in grads]

    def scratch(*lead):
        return [pltpu.VMEM((*lead, 48, w), BF16) for w in widths]

    return pl.pallas_call(
        reduce_kernel,
        out_shape=[jax.ShapeDtypeStruct((48, w), F32) for w in widths],
        in_specs=[pl.BlockSpec(memory_space=pl.ANY)] * ITEM_COUNT,
        out_specs=[pl.BlockSpec(memory_space=pltpu.VMEM)] * ITEM_COUNT,
        scratch_shapes=scratch(2, 4, 2)
        + scratch(2, 4, 2)
        + scratch(2, 2)
        + scratch(2, 2)
        + scratch(2)
        + scratch(2)
        + scratch(3)
        + [
            pltpu.SemaphoreType.DMA((ITEM_COUNT, 8)),
            pltpu.SemaphoreType.DMA((ITEM_COUNT, 8)),
            pltpu.SemaphoreType.DMA((ITEM_COUNT,)),
        ],
        compiler_params=pltpu.CompilerParams(
            collective_id=1, has_side_effects=True, vmem_limit_bytes=VMEM_LIMIT
        ),
        name="reduce_gradients",
    )(*grads)


def layer_norm(inputs, gain_row, shift_row):
    centered = inputs - jnp.mean(inputs, axis=-1, keepdims=True)
    variance = jnp.mean(centered * centered, axis=-1, keepdims=True)
    return centered * lax.rsqrt(variance + EPSILON) * gain_row + shift_row


def gelu_exact(values):
    return jax.nn.gelu(values, approximate=False)


def mm(left, right, contract):
    return lax.dot_general(left, right, (contract, ((), ())), preferred_element_type=F32)


def halves(array):
    return jnp.stack(jnp.split(array, 2, axis=1))


def heads(array):
    return array.reshape(array.shape[0], -1, HEAD_DIM).transpose(1, 0, 2)


def flat(array):
    return array.transpose(1, 0, 2).reshape(array.shape[1], -1)


def body(use_kernels, dp_size, tokens, lengths, cotangent, norm_gain, norm_shift, qkv_weight, qv_bias,
         out_weight, up_weight, up_bias, down_weight, out_bias):
    part = lax.axis_index("tensor")
    layers = norm_gain.shape[0]
    rows, width = tokens.shape
    length = lax.dynamic_index_in_dim(lengths, part, keepdims=False)
    keep = jnp.arange(rows, dtype=jnp.int32) < length
    own = qkv_weight.shape[1]
    shards = []
    for layer in range(layers):
        shards += [
            qkv_weight[layer].reshape(own, -1),
            out_weight[layer].T,
            up_weight[layer],
            down_weight[layer].T,
        ]
    if use_kernels:
        full = [w.reshape(2, width, -1) for w in gather_weights(shards)]
    else:
        full = [
            lax.all_gather(s, ("tensor", "dp"), axis=0).reshape(2, width, -1) for s in shards
        ]
    qv_all = lax.all_gather(qv_bias, "tensor", axis=0)
    upb_all = lax.all_gather(up_bias, "tensor", axis=0)
    scale = HEAD_DIM**-0.5
    stream = tokens.astype(F32)
    saved = []
    for layer in range(layers):
        w_qkv, w_out, w_up, w_down = full[4 * layer : 4 * layer + 4]
        normed = layer_norm(stream, norm_gain[layer, 0], norm_shift[layer, 0]).astype(BF16)
        project = []
        for t in range(2):
            b = jnp.concatenate([qv_all[t, layer, 0], jnp.zeros_like(qv_all[t, layer, 0]), qv_all[t, layer, 1]])
            project.append((mm(normed, w_qkv[t], ((1,), (0,))) + b).astype(BF16))
        third = width // 2
        q, key, val = (
            heads(jnp.concatenate([project[t][:, j * third : (j + 1) * third] for t in range(2)], axis=1))
            for j in range(3)
        )
        scores = jnp.einsum("hqd,hkd->hqk", q, key, preferred_element_type=F32) * scale
        scores = jnp.where(keep[None, None, :], scores, -1e30)
        highest = jnp.max(scores, axis=-1, keepdims=True)
        exponent = jnp.exp(scores - highest)
        probs32 = exponent / jnp.sum(exponent, axis=-1, keepdims=True)
        probs = probs32.astype(BF16)
        attended = flat(jnp.einsum("hqk,hkd->hqd", probs, val, preferred_element_type=F32)).astype(BF16)
        branch = sum(mm(attended[:, t * third : (t + 1) * third], w_out[t], ((1,), (1,))) for t in range(2))
        middle = stream + branch + out_bias[layer, 0]
        normed_mid = layer_norm(middle, norm_gain[layer, 1], norm_shift[layer, 1]).astype(BF16)
        hidden = [mm(normed_mid, w_up[t], ((1,), (0,))) + upb_all[t, layer] for t in range(2)]
        activated = [gelu_exact(h).astype(BF16) for h in hidden]
        branch_mlp = sum(mm(activated[t], w_down[t], ((1,), (1,))) for t in range(2))
        saved.append((stream, middle, normed, q, key, val, probs, attended, normed_mid, hidden, activated))
        stream = middle + branch_mlp + out_bias[layer, 1]
    final = stream.astype(BF16)
    gradient = cotangent.astype(F32) * keep.astype(F32)[:, None]
    grads = [None] * (4 * layers)
    gain, shift, outb, qvb, upb = ([None] * layers for _ in range(5))
    for layer in reversed(range(layers)):
        stream_in, middle, normed, q, key, val, probs, attended, normed_mid, hidden, activated = saved[layer]
        w_qkv, w_out, w_up, w_down = full[4 * layer : 4 * layer + 4]
        third = width // 2
        bias_late = jnp.sum(gradient, axis=0)
        dout = gradient.astype(BF16)
        grads[4 * layer + 3] = jnp.stack([mm(dout, activated[t], ((0,), (0,))).astype(BF16) for t in range(2)])
        dhidden = []
        for t in range(2):
            dact = mm(dout, w_down[t], ((1,), (0,)))
            dhidden.append(jax.vjp(gelu_exact, hidden[t])[1](dact)[0].astype(BF16))
        upb[layer] = jnp.stack([jnp.sum(d.astype(F32), axis=0) for d in dhidden])
        grads[4 * layer + 2] = jnp.stack([mm(normed_mid, d, ((0,), (0,))).astype(BF16) for d in dhidden])
        dnormed_mid = sum(mm(dhidden[t], w_up[t], ((1,), (1,))) for t in range(2))
        pull = jax.vjp(layer_norm, middle, norm_gain[layer, 1], norm_shift[layer, 1])[1]
        dmid, gain_late, shift_late = pull(dnormed_mid)
        dmiddle = gradient + dmid
        bias_early = jnp.sum(dmiddle, axis=0)
        dbranch = dmiddle.astype(BF16)
        dout_t = mm(dbranch, attended, ((0,), (0,))).astype(BF16)
        grads[4 * layer + 1] = halves(dout_t)
        dattended = heads(jnp.concatenate([mm(dbranch, w_out[t], ((1,), (0,))) for t in range(2)], axis=1).astype(BF16))
        p = probs.astype(F32)
        dval = jnp.einsum("hqk,hqd->hkd", probs, dattended, preferred_element_type=F32)
        dprobs = jnp.einsum("hqd,hkd->hqk", dattended, val, preferred_element_type=F32)
        dscores = (p * (dprobs - jnp.sum(p * dprobs, axis=-1, keepdims=True))).astype(BF16)
        dquery = jnp.einsum("hqk,hkd->hqd", dscores, key, preferred_element_type=F32) * scale
        dkey = jnp.einsum("hqk,hqd->hkd", dscores, q, preferred_element_type=F32) * scale
        parts = [flat(a).astype(BF16) for a in (dquery, dkey, dval)]
        dproject = [
            jnp.concatenate([a[:, t * third : (t + 1) * third] for a in parts], axis=1) for t in range(2)
        ]
        qvb[layer] = jnp.stack([jnp.sum(parts[0].astype(F32), axis=0), jnp.sum(parts[2].astype(F32), axis=0)])
        grads[4 * layer] = jnp.stack([mm(normed, d, ((0,), (0,))).astype(BF16) for d in dproject])
        dnormed = sum(mm(dproject[t], w_qkv[t], ((1,), (1,))) for t in range(2))
        pull = jax.vjp(layer_norm, stream_in, norm_gain[layer, 0], norm_shift[layer, 0])[1]
        dfirst, gain_early, shift_early = pull(dnormed)
        gradient = dmiddle + dfirst
        gain[layer] = jnp.stack([gain_early, gain_late])
        shift[layer] = jnp.stack([shift_early, shift_late])
        outb[layer] = jnp.stack([bias_early, bias_late])
    if use_kernels:
        reduced = reduce_gradients([g.reshape(2, 4, 2, 2, 48, -1) for g in grads])
    else:
        reduced = [
            lax.psum_scatter(
                g.reshape(2 * dp_size, own, -1).astype(F32), ("tensor", "dp"), scatter_dimension=0
            )
            for g in grads
        ]
    g_gain, g_shift, g_outb, g_qvb, g_upb = lax.psum(
        (jnp.stack(gain), jnp.stack(shift), jnp.stack(outb), jnp.stack(qvb), jnp.stack(upb)),
        ("dp", "tensor"),
    )
    g_qvb = lax.dynamic_slice_in_dim(g_qvb, part * qv_bias.shape[2], qv_bias.shape[2], axis=2)
    g_upb = lax.dynamic_index_in_dim(g_upb, part, axis=1, keepdims=False)
    g_qkv = jnp.stack([reduced[4 * l].reshape(own, 3, -1) for l in range(layers)])
    g_out = jnp.stack([reduced[4 * l + 1].T for l in range(layers)])
    g_up = jnp.stack([reduced[4 * l + 2] for l in range(layers)])
    g_down = jnp.stack([reduced[4 * l + 3].T for l in range(layers)])
    return (final, gradient, g_gain, g_shift, g_qkv, g_qvb, g_out, g_up, g_upb, g_down, g_outb)


def solution(mesh):
    use_kernels = mesh.shape["dp"] == 16 and mesh.shape["tensor"] == 2
    return jax.shard_map(
        functools.partial(body, use_kernels, mesh.shape["dp"]),
        mesh=mesh,
        in_specs=(
            P(("dp", "tensor"), None),
            P("dp"),
            P(("dp", "tensor"), None),
            P(),
            P(),
            P(None, "dp", None, "tensor"),
            P(None, None, "tensor"),
            P(None, "tensor", "dp"),
            P(None, "dp", "tensor"),
            P(None, "tensor"),
            P(None, "tensor", "dp"),
            P(),
        ),
        out_specs=(
            P(("dp", "tensor"), None),
            P(("dp", "tensor"), None),
            P(),
            P(),
            P(None, "dp", None, "tensor"),
            P(None, None, "tensor"),
            P(None, "tensor", "dp"),
            P(None, "dp", "tensor"),
            P(None, "tensor"),
            P(None, "tensor", "dp"),
            P(),
        ),
        check_vma=False,
    )
```

```python
import functools

import jax
import jax.numpy as jnp
from jax import lax
from jax.experimental import pallas as pl
from jax.experimental.pallas import tpu as pltpu
from jax.sharding import PartitionSpec as P

HEAD_DIM = 64
EPSILON = 1e-06
MESH = pl.DeviceIdType.MESH
VMEM_LIMIT = 60 * 2**20
BF16 = jnp.bfloat16
F32 = jnp.float32
ITEM_COUNT = 8
GATHER_ORDER = (0, 1, 2, 3, 4, 5, 6, 7)
REDUCE_ORDER = (7, 6, 5, 4, 3, 2, 1, 0)


def places():
    dp = lax.axis_index("dp")
    y = lax.axis_index("tensor")
    return dp // 4, (dp // 2) % 2, dp % 2, y


def partners(z, x, k, y):
    def at(z_, x_, k_, y_):
        return {"dp": (z_ * 2 + x_) * 2 + k_, "tensor": y_}

    along_z = [at((z + step) % 4, x, k, y) for step in (1, 2, 3)]
    return along_z + [at(z, 1 - x, k, y), at(z, x, k, 1 - y), at(z, x, 1 - k, y)]


def greet(peers):
    barrier = pltpu.get_barrier_semaphore()
    for peer in peers:
        pl.semaphore_signal(barrier, inc=1, device_id=peer, device_id_type=MESH)
    pl.semaphore_wait(barrier, len(peers))


def gather_kernel(*refs):
    own, out = refs[:ITEM_COUNT], refs[ITEM_COUNT : 2 * ITEM_COUNT]
    held = refs[2 * ITEM_COUNT : 3 * ITEM_COUNT]
    send, recv, local = refs[3 * ITEM_COUNT :]
    z, x, k, y = places()
    peers = partners(z, x, k, y)
    mine = [
        pltpu.make_async_copy(own[i], held[i].at[y, z, x, k], local.at[i])
        for i in range(ITEM_COUNT)
    ]
    for copy in mine:
        copy.start()
    greet(peers)

    def remote(i, ref, slot, peer):
        return pltpu.make_async_remote_copy(
            ref, ref, send.at[i, slot], recv.at[i, slot], device_id=peers[peer], device_id_type=MESH
        )

    def copies(i, phase):
        b = held[i]
        if phase == 0:
            return [remote(i, b.at[y, z, x, k], j, j) for j in range(3)]
        if phase == 1:
            return [remote(i, b.at[y, 0:2, x, k], 3, 3), remote(i, b.at[y, 2:4, x, k], 4, 4)]
        if phase == 2:
            return [remote(i, b.at[y, 0:2, :, k], 5, 4), remote(i, b.at[:, 2:4, x, k], 6, 3)]
        return [remote(i, b.at[:, :, :, k], 7, 5)]

    live = {}

    def begin(i, phase):
        if phase == 0:
            mine[i].wait()
        live[i, phase] = copies(i, phase)
        for copy in live[i, phase]:
            copy.start()

    def finish(i, phase):
        for copy in live.pop((i, phase)):
            copy.wait()

    order = GATHER_ORDER
    begin(order[0], 0)
    begin(order[1], 0)
    back = []
    for turn in range(ITEM_COUNT + 3):
        for phase in (3, 2, 1, 0):
            spot = turn - phase
            if 0 <= spot < ITEM_COUNT:
                finish(order[spot], phase)
                if phase < 3:
                    begin(order[spot], phase + 1)
                else:
                    i = order[spot]
                    copy = pltpu.make_async_copy(held[i], out[i], local.at[i])
                    copy.start()
                    back.append(copy)
                if phase == 0 and spot + 2 < ITEM_COUNT:
                    begin(order[spot + 2], 0)
    for copy in back:
        copy.wait()


def gather_weights(shards):
    widths = [s.shape[-1] for s in shards]
    full = [(2, 4, 2, 2, 48, w) for w in widths]
    return pl.pallas_call(
        gather_kernel,
        out_shape=[jax.ShapeDtypeStruct(f, BF16) for f in full],
        in_specs=[pl.BlockSpec(memory_space=pl.ANY)] * ITEM_COUNT,
        out_specs=[pl.BlockSpec(memory_space=pl.ANY)] * ITEM_COUNT,
        scratch_shapes=[pltpu.VMEM(f, BF16) for f in full]
        + [
            pltpu.SemaphoreType.DMA((ITEM_COUNT, 8)),
            pltpu.SemaphoreType.DMA((ITEM_COUNT, 8)),
            pltpu.SemaphoreType.DMA((ITEM_COUNT,)),
        ],
        compiler_params=pltpu.CompilerParams(
            collective_id=0, has_side_effects=True, vmem_limit_bytes=VMEM_LIMIT
        ),
        name="gather_weights",
    )(*shards)


def add_into(target, source, blocks, width):
    for at_target, at_source in blocks:
        for start in range(0, width, 384):
            stop = pl.ds(start, 384)
            total = target[(*at_target, slice(None), stop)].astype(F32) + source[
                (*at_source, slice(None), stop)
            ].astype(F32)
            target[(*at_target, slice(None), stop)] = total.astype(target.dtype)


def reduce_kernel(*refs):
    n = ITEM_COUNT
    grads, out = refs[:n], refs[n : 2 * n]
    held, from_core, from_a, from_b, from_c, from_d, from_z = (
        refs[(2 + j) * n : (3 + j) * n] for j in range(7)
    )
    send, recv, local = refs[9 * n :]
    z, x, k, y = places()
    peers = partners(z, x, k, y)
    mine = [
        pltpu.make_async_copy(grads[i].at[:, :, :, k], held[i], local.at[i]) for i in range(n)
    ]
    for copy in mine:
        copy.start()
    greet(peers)

    def remote(i, source, target, slot, peer):
        return pltpu.make_async_remote_copy(
            source, target, send.at[i, slot], recv.at[i, slot], device_id=peers[peer], device_id_type=MESH
        )

    def copies(i, phase):
        b = held[i]
        if phase == 0:
            return [remote(i, grads[i].at[:, :, :, 1 - k], from_core[i], 0, 5)]
        if phase == 1:
            return [
                remote(i, b.at[1 - y, 0:2], from_a[i], 1, 4),
                remote(i, b.at[:, 2:4, 1 - x], from_b[i], 2, 3),
            ]
        if phase == 2:
            return [
                remote(i, b.at[y, 0:2, 1 - x], from_c[i], 3, 3),
                remote(i, b.at[1 - y, 2:4, x], from_d[i], 4, 4),
            ]
        return [
            remote(i, b.at[y, (z + 1 + j) % 4, x], from_z[i].at[j], 5 + j, j) for j in range(3)
        ]

    def total(i, phase):
        b = held[i]
        width = b.shape[-1]
        if phase == 0:
            mine[i].wait()

            def block(t, carry):
                at = (t // 8, (t // 2) % 4, t % 2)
                add_into(b, from_core[i], [(at, at)], width)
                return carry

            lax.fori_loop(0, 16, block, 0)
        elif phase == 1:
            def block(t, carry):
                p, q = t // 2, t % 2
                add_into(b, from_a[i], [((y, p, q), (p, q))], width)
                add_into(b, from_b[i], [((p, 2 + q, x), (p, q))], width)
                return carry

            lax.fori_loop(0, 4, block, 0)
        elif phase == 2:
            def block(t, carry):
                add_into(b, from_c[i], [((y, t, x), (t,))], width)
                add_into(b, from_d[i], [((y, 2 + t, x), (t,))], width)
                return carry

            lax.fori_loop(0, 2, block, 0)
        else:
            for start in range(0, width, 384):
                cols = pl.ds(start, 384)
                value = b[y, z, x, :, cols].astype(F32)
                for j in range(3):
                    value += from_z[i][j, :, cols].astype(F32)
                out[i][:, cols] = value

    live = {}

    def begin(i, phase):
        live[i, phase] = copies(i, phase)
        for copy in live[i, phase]:
            copy.start()

    def finish(i, phase):
        for copy in live.pop((i, phase)):
            copy.wait()
        total(i, phase)

    order = REDUCE_ORDER
    begin(order[0], 0)
    begin(order[1], 0)
    for turn in range(n + 3):
        for phase in (3, 2, 1, 0):
            spot = turn - phase
            if 0 <= spot < n:
                finish(order[spot], phase)
                if phase < 3:
                    begin(order[spot], phase + 1)
                if phase == 0 and spot + 2 < n:
                    begin(order[spot + 2], 0)


def reduce_gradients(grads):
    widths = [g.shape[-1] for g in grads]

    def scratch(*lead):
        return [pltpu.VMEM((*lead, 48, w), BF16) for w in widths]

    return pl.pallas_call(
        reduce_kernel,
        out_shape=[jax.ShapeDtypeStruct((48, w), F32) for w in widths],
        in_specs=[pl.BlockSpec(memory_space=pl.ANY)] * ITEM_COUNT,
        out_specs=[pl.BlockSpec(memory_space=pltpu.VMEM)] * ITEM_COUNT,
        scratch_shapes=scratch(2, 4, 2)
        + scratch(2, 4, 2)
        + scratch(2, 2)
        + scratch(2, 2)
        + scratch(2)
        + scratch(2)
        + scratch(3)
        + [
            pltpu.SemaphoreType.DMA((ITEM_COUNT, 8)),
            pltpu.SemaphoreType.DMA((ITEM_COUNT, 8)),
            pltpu.SemaphoreType.DMA((ITEM_COUNT,)),
        ],
        compiler_params=pltpu.CompilerParams(
            collective_id=1, has_side_effects=True, vmem_limit_bytes=VMEM_LIMIT
        ),
        name="reduce_gradients",
    )(*grads)


def layer_norm(inputs, gain_row, shift_row):
    centered = inputs - jnp.mean(inputs, axis=-1, keepdims=True)
    variance = jnp.mean(centered * centered, axis=-1, keepdims=True)
    return centered * lax.rsqrt(variance + EPSILON) * gain_row + shift_row


def gelu_exact(values):
    return jax.nn.gelu(values, approximate=False)


def mm(left, right, contract):
    return lax.dot_general(left, right, (contract, ((), ())), preferred_element_type=F32)


def halves(array):
    return jnp.stack(jnp.split(array, 2, axis=1))


def heads(array):
    return array.reshape(array.shape[0], -1, HEAD_DIM).transpose(1, 0, 2)


def flat(array):
    return array.transpose(1, 0, 2).reshape(array.shape[1], -1)


def run_pump(events):
    queue = list(events)

    def step(count):
        for _ in range(min(count, len(queue))):
            queue.pop(0)[1]()

    def need(tag):
        if any(name == tag for name, _ in queue):
            while True:
                name, act = queue.pop(0)
                act()
                if name == tag:
                    break

    return need, step


def gather_events(own, held, send, recv, local, peers, place):
    z, x, k, y = place
    n = len(held)
    mine = [
        pltpu.make_async_copy(own[i], held[i].at[y, z, x, k], local.at[i]) for i in range(n)
    ]
    for copy in mine:
        copy.start()

    def remote(i, ref, slot, peer):
        return pltpu.make_async_remote_copy(
            ref, ref, send.at[i, slot], recv.at[i, slot], device_id=peers[peer], device_id_type=MESH
        )

    def copies(i, phase):
        b = held[i]
        if phase == 0:
            return [remote(i, b.at[y, z, x, k], j, j) for j in range(3)]
        if phase == 1:
            return [remote(i, b.at[y, 0:2, x, k], 3, 3), remote(i, b.at[y, 2:4, x, k], 4, 4)]
        if phase == 2:
            return [remote(i, b.at[y, 0:2, :, k], 5, 4), remote(i, b.at[:, 2:4, x, k], 6, 3)]
        return [remote(i, b.at[:, :, :, k], 7, 5)]

    live = {}

    def begin(i, phase):
        if phase == 0:
            mine[i].wait()
        live[i, phase] = copies(i, phase)
        for copy in live[i, phase]:
            copy.start()

    def finish(i, phase):
        for copy in live.pop((i, phase)):
            copy.wait()

    order = GATHER_ORDER
    events = []

    def event(spot, phase):
        i = order[spot]

        def act():
            finish(i, phase)
            if phase < 3:
                begin(i, phase + 1)
            if phase == 0 and spot + 2 < n:
                begin(order[spot + 2], 0)

        return (("w", i) if phase == 3 else None, act)

    for turn in range(n + 3):
        for phase in (3, 2, 1, 0):
            if 0 <= turn - phase < n:
                events.append(event(turn - phase, phase))

    def start():
        begin(order[0], 0)
        begin(order[1], 0)

    return start, events


def matrix(ref, *lead):
    value = ref[lead] if lead else ref[...]
    return value.reshape(-1, value.shape[-1])


def norm_rows(source, gain_row, shift_row, target):
    def block(t, carry):
        rows = pl.ds(pl.multiple_of(t * 128, 128), 128)
        target[rows, :] = layer_norm(source[rows, :], gain_row, shift_row).astype(BF16)
        return carry

    lax.fori_loop(0, source.shape[0] // 128, block, 0)


def turn_rows(source, target, k):
    for c in range(2):
        turned = source[:, c * 384 : (c + 1) * 384].T
        for j in range(8):
            block = c * 8 + j
            target[(block + k) % 2, block // 4, (block // 2) % 2] = turned[j * 48 : (j + 1) * 48]


def forward_kernel(*refs):
    n = ITEM_COUNT
    it = iter(refs)

    def take(count):
        return [next(it) for _ in range(count)]

    own = take(n)
    tokens, lengths, gain, shift, outb, qvb, upb = take(7)
    whole = take(n)
    saved = [take(9) for _ in range(2)]
    (final,) = take(1)
    held = take(n)
    (stream, middle, normed, turned, turned_mid, project, attended, active, slope, probs, qv_all, up_all) = take(12)
    send, recv, local, out_sem, prob_sem, small_send, small_recv, whole_sem = take(8)
    place = z, x, k, y = places()
    peers = partners(z, x, k, y)
    start, events = gather_events(own, held, send, recv, local, peers, place)
    need, step = run_pump(events)
    qv_all[y] = qvb[...]
    up_all[y] = upb[...]
    greet(peers)
    start()
    small = [
        pltpu.make_async_remote_copy(
            ref.at[y], ref.at[y], small_send.at[j], small_recv.at[j], device_id=peers[4], device_id_type=MESH
        )
        for j, ref in enumerate((qv_all, up_all))
    ]
    for copy in small:
        copy.start()
    stream[...] = tokens[...].astype(F32)
    length = lengths[y]
    rows = stream.shape[0]
    outgoing = {}

    def save(layer, slot, ref):
        copy = pltpu.make_async_copy(ref, saved[layer][slot], out_sem.at[layer, slot])
        copy.start()
        outgoing[slot] = copy

    def settle(slot):
        if slot in outgoing:
            outgoing.pop(slot).wait()

    back = []

    def keep_weight(i):
        copy = pltpu.make_async_copy(held[i], whole[i], whole_sem.at[i])
        copy.start()
        back.append(copy)

    for layer in range(2):
        w_qkv, w_out, w_up, w_down = held[4 * layer : 4 * layer + 4]
        settle(2)
        norm_rows(stream, gain[layer, 0:1], shift[layer, 0:1], normed)
        turn_rows(normed, turned, k)
        save(layer, 0, stream)
        save(layer, 2, turned)
        if layer == 0:
            for copy in small:
                copy.wait()
        need(("w", 4 * layer))
        keep_weight(4 * layer)
        settle(4)
        for half in range(2):
            for t in range(3):
                part = mm(normed[...], matrix(w_qkv, half, slice(None), slice(None), slice(None), slice(None), pl.ds(t * 384, 384)), ((1,), (0,)))
                if t != 1:
                    part = part + qv_all[half, layer, t // 2 : t // 2 + 1]
                project[half, :, t * 384 : (t + 1) * 384] = part.astype(BF16)
        save(layer, 4, project)
        step(1)
        settle(5)

        def pair(j, carry):
            half = j // 3
            at = (j % 3) * 128
            lane = lax.broadcasted_iota(jnp.int32, (1, 128), 1) < 64
            query = project[half, :, pl.ds(pl.multiple_of(at, 128), 128)]
            key = project[half, :, pl.ds(pl.multiple_of(at + 384, 128), 128)]
            value = project[half, :, pl.ds(pl.multiple_of(at + 768, 128), 128)]
            value_t = value.T
            hidden_key = lax.broadcasted_iota(jnp.int32, (rows, 1), 0) >= length
            both = []
            slot = j % 2
            for h in range(2):
                here = lane if h == 0 else jnp.logical_not(lane)
                some = jnp.where(here, key, jnp.zeros_like(key)) * jnp.asarray(HEAD_DIM**-0.5, BF16)
                scores = mm(some, query, ((1,), (1,)))
                scores = jnp.where(hidden_key, -1e30, scores)
                exponent = jnp.exp(scores - jnp.max(scores, axis=0, keepdims=True))
                prob = (exponent * (1.0 / jnp.sum(exponent, axis=0, keepdims=True))).astype(BF16)
                probs[j, h] = prob
                both.append(mm(value_t[h * 64 : (h + 1) * 64], prob, ((1,), (0,))))
            block = jnp.concatenate(both, axis=0).T
            attended[:, pl.ds(pl.multiple_of(j * 128, 128), 128)] = block.astype(BF16)
            return carry

        settle(6)
        for j0 in range(0, 6, 3):
            lax.fori_loop(j0, j0 + 3, pair, 0)
            step(1)
        save(layer, 5, attended)
        save(layer, 6, probs)
        need(("w", 4 * layer + 1))
        keep_weight(4 * layer + 1)
        settle(1)
        for c in range(2):
            cols = slice(c * 384, (c + 1) * 384)
            total = stream[:, cols] + outb[layer, 0:1, cols]
            for half in range(2):
                total += mm(attended[:, half * 384 : (half + 1) * 384], matrix(w_out, half, slice(2 * c, 2 * c + 2)), ((1,), (1,)))
            middle[:, cols] = total
        save(layer, 1, middle)
        settle(3)
        norm_rows(middle, gain[layer, 1:2], shift[layer, 1:2], normed)
        turn_rows(normed, turned_mid, k)
        save(layer, 3, turned_mid)
        step(1)
        need(("w", 4 * layer + 2))
        keep_weight(4 * layer + 2)
        settle(7)
        settle(8)

        def unit(t, carry):
            half = t // 3
            cols = pl.ds(pl.multiple_of((t % 3) * 512, 128), 512)
            hidden = mm(normed[...], matrix(w_up, half, slice(None), slice(None), slice(None), slice(None), cols), ((1,), (0,)))
            hidden = hidden + up_all[half, layer : layer + 1, cols]
            cdf = 0.5 * (1.0 + lax.erf(hidden * (0.5**0.5)))
            density = jnp.exp(-0.5 * hidden * hidden) * 0.3989422804014327
            active[half, :, cols] = (hidden * cdf).astype(BF16)
            slope[half, :, cols] = (cdf + hidden * density).astype(BF16)
            return carry

        for t0 in range(0, 6, 3):
            lax.fori_loop(t0, t0 + 3, unit, 0)
            step(1)
        save(layer, 7, active)
        save(layer, 8, slope)
        need(("w", 4 * layer + 3))
        keep_weight(4 * layer + 3)
        settle(0)
        for c in range(2):
            cols = slice(c * 384, (c + 1) * 384)
            total = middle[:, cols] + outb[layer, 1:2, cols]
            for half in range(2):
                total += mm(active[half], matrix(w_down, half, slice(2 * c, 2 * c + 2)), ((1,), (1,)))
            stream[:, cols] = total
        step(1)
    final[...] = stream[...].astype(BF16)
    for slot in list(outgoing):
        settle(slot)
    for copy in back:
        copy.wait()


def forward(shards, tokens, lengths, gain, shift, outb, qvb, upb):
    rows, width = tokens.shape
    widths = [s.shape[-1] for s in shards]
    full = [(2, 4, 2, 2, 48, w) for w in widths]
    layer_saves = [
        ((rows, width), F32),
        ((rows, width), F32),
        ((2, 4, 2, 48, rows), BF16),
        ((2, 4, 2, 48, rows), BF16),
        ((2, rows, widths[0]), BF16),
        ((rows, width), BF16),
        ((6, 2, rows, rows), BF16),
        ((2, rows, widths[2]), BF16),
        ((2, rows, widths[2]), BF16),
    ]
    any_spec = pl.BlockSpec(memory_space=pl.ANY)
    vmem_spec = pl.BlockSpec(memory_space=pltpu.VMEM)
    out_shape = (
        [jax.ShapeDtypeStruct(f, BF16) for f in full]
        + [jax.ShapeDtypeStruct(s, t) for s, t in layer_saves * 2]
        + [jax.ShapeDtypeStruct((rows, width), BF16)]
    )
    by_slot = {j: pltpu.VMEM(*layer_saves[j]) for j in range(9)}
    outs = pl.pallas_call(
        forward_kernel,
        out_shape=out_shape,
        in_specs=[any_spec] * ITEM_COUNT + [vmem_spec, pl.BlockSpec(memory_space=pltpu.SMEM)] + [vmem_spec] * 5,
        out_specs=[any_spec] * (ITEM_COUNT + 18) + [vmem_spec],
        scratch_shapes=[pltpu.VMEM(f, BF16) for f in full]
        + [
            by_slot[0],
            by_slot[1],
            pltpu.VMEM((rows, width), BF16),
            by_slot[2],
            by_slot[3],
            by_slot[4],
            by_slot[5],
            by_slot[7],
            by_slot[8],
            by_slot[6],
            pltpu.VMEM((2, *qvb.shape), F32),
            pltpu.VMEM((2, *upb.shape), F32),
            pltpu.SemaphoreType.DMA((ITEM_COUNT, 8)),
            pltpu.SemaphoreType.DMA((ITEM_COUNT, 8)),
            pltpu.SemaphoreType.DMA((ITEM_COUNT,)),
            pltpu.SemaphoreType.DMA((2, 9)),
            pltpu.SemaphoreType.DMA((2,)),
            pltpu.SemaphoreType.DMA((2,)),
            pltpu.SemaphoreType.DMA((2,)),
            pltpu.SemaphoreType.DMA((ITEM_COUNT,)),
        ],
        compiler_params=pltpu.CompilerParams(
            collective_id=0, has_side_effects=True, vmem_limit_bytes=VMEM_LIMIT
        ),
        name="forward",
    )(*shards, tokens, lengths, gain, shift, outb, qvb, upb)
    return outs[:ITEM_COUNT], [outs[ITEM_COUNT + 9 * l : ITEM_COUNT + 9 * l + 9] for l in range(2)], outs[-1]


def generic_body(dp_size, tokens, lengths, cotangent, norm_gain, norm_shift, qkv_weight, qv_bias,
         out_weight, up_weight, up_bias, down_weight, out_bias):
    part = lax.axis_index("tensor")
    layers = norm_gain.shape[0]
    rows, width = tokens.shape
    length = lax.dynamic_index_in_dim(lengths, part, keepdims=False)
    keep = jnp.arange(rows, dtype=jnp.int32) < length
    own = qkv_weight.shape[1]
    shards = []
    for layer in range(layers):
        shards += [
            qkv_weight[layer].reshape(own, -1),
            out_weight[layer].T,
            up_weight[layer],
            down_weight[layer].T,
        ]
    if False:
        full = [w.reshape(2, width, -1) for w in gather_weights(shards)]
    else:
        full = [
            lax.all_gather(s, ("tensor", "dp"), axis=0).reshape(2, width, -1) for s in shards
        ]
    qv_all = lax.all_gather(qv_bias, "tensor", axis=0)
    upb_all = lax.all_gather(up_bias, "tensor", axis=0)
    scale = HEAD_DIM**-0.5
    stream = tokens.astype(F32)
    saved = []
    for layer in range(layers):
        w_qkv, w_out, w_up, w_down = full[4 * layer : 4 * layer + 4]
        normed = layer_norm(stream, norm_gain[layer, 0], norm_shift[layer, 0]).astype(BF16)
        project = []
        for t in range(2):
            b = jnp.concatenate([qv_all[t, layer, 0], jnp.zeros_like(qv_all[t, layer, 0]), qv_all[t, layer, 1]])
            project.append((mm(normed, w_qkv[t], ((1,), (0,))) + b).astype(BF16))
        third = width // 2
        q, key, val = (
            heads(jnp.concatenate([project[t][:, j * third : (j + 1) * third] for t in range(2)], axis=1))
            for j in range(3)
        )
        scores = jnp.einsum("hqd,hkd->hqk", q, key, preferred_element_type=F32) * scale
        scores = jnp.where(keep[None, None, :], scores, -1e30)
        highest = jnp.max(scores, axis=-1, keepdims=True)
        exponent = jnp.exp(scores - highest)
        probs32 = exponent / jnp.sum(exponent, axis=-1, keepdims=True)
        probs = probs32.astype(BF16)
        attended = flat(jnp.einsum("hqk,hkd->hqd", probs, val, preferred_element_type=F32)).astype(BF16)
        branch = sum(mm(attended[:, t * third : (t + 1) * third], w_out[t], ((1,), (1,))) for t in range(2))
        middle = stream + branch + out_bias[layer, 0]
        normed_mid = layer_norm(middle, norm_gain[layer, 1], norm_shift[layer, 1]).astype(BF16)
        hidden = [mm(normed_mid, w_up[t], ((1,), (0,))) + upb_all[t, layer] for t in range(2)]
        activated = [gelu_exact(h).astype(BF16) for h in hidden]
        branch_mlp = sum(mm(activated[t], w_down[t], ((1,), (1,))) for t in range(2))
        saved.append((stream, middle, normed, q, key, val, probs, attended, normed_mid, hidden, activated))
        stream = middle + branch_mlp + out_bias[layer, 1]
    final = stream.astype(BF16)
    gradient = cotangent.astype(F32) * keep.astype(F32)[:, None]
    grads = [None] * (4 * layers)
    gain, shift, outb, qvb, upb = ([None] * layers for _ in range(5))
    for layer in reversed(range(layers)):
        stream_in, middle, normed, q, key, val, probs, attended, normed_mid, hidden, activated = saved[layer]
        w_qkv, w_out, w_up, w_down = full[4 * layer : 4 * layer + 4]
        third = width // 2
        bias_late = jnp.sum(gradient, axis=0)
        dout = gradient.astype(BF16)
        grads[4 * layer + 3] = jnp.stack([mm(dout, activated[t], ((0,), (0,))).astype(BF16) for t in range(2)])
        dhidden = []
        for t in range(2):
            dact = mm(dout, w_down[t], ((1,), (0,)))
            dhidden.append(jax.vjp(gelu_exact, hidden[t])[1](dact)[0].astype(BF16))
        upb[layer] = jnp.stack([jnp.sum(d.astype(F32), axis=0) for d in dhidden])
        grads[4 * layer + 2] = jnp.stack([mm(normed_mid, d, ((0,), (0,))).astype(BF16) for d in dhidden])
        dnormed_mid = sum(mm(dhidden[t], w_up[t], ((1,), (1,))) for t in range(2))
        pull = jax.vjp(layer_norm, middle, norm_gain[layer, 1], norm_shift[layer, 1])[1]
        dmid, gain_late, shift_late = pull(dnormed_mid)
        dmiddle = gradient + dmid
        bias_early = jnp.sum(dmiddle, axis=0)
        dbranch = dmiddle.astype(BF16)
        dout_t = mm(dbranch, attended, ((0,), (0,))).astype(BF16)
        grads[4 * layer + 1] = halves(dout_t)
        dattended = heads(jnp.concatenate([mm(dbranch, w_out[t], ((1,), (0,))) for t in range(2)], axis=1).astype(BF16))
        p = probs.astype(F32)
        dval = jnp.einsum("hqk,hqd->hkd", probs, dattended, preferred_element_type=F32)
        dprobs = jnp.einsum("hqd,hkd->hqk", dattended, val, preferred_element_type=F32)
        dscores = (p * (dprobs - jnp.sum(p * dprobs, axis=-1, keepdims=True))).astype(BF16)
        dquery = jnp.einsum("hqk,hkd->hqd", dscores, key, preferred_element_type=F32) * scale
        dkey = jnp.einsum("hqk,hqd->hkd", dscores, q, preferred_element_type=F32) * scale
        parts = [flat(a).astype(BF16) for a in (dquery, dkey, dval)]
        dproject = [
            jnp.concatenate([a[:, t * third : (t + 1) * third] for a in parts], axis=1) for t in range(2)
        ]
        qvb[layer] = jnp.stack([jnp.sum(parts[0].astype(F32), axis=0), jnp.sum(parts[2].astype(F32), axis=0)])
        grads[4 * layer] = jnp.stack([mm(normed, d, ((0,), (0,))).astype(BF16) for d in dproject])
        dnormed = sum(mm(dproject[t], w_qkv[t], ((1,), (1,))) for t in range(2))
        pull = jax.vjp(layer_norm, stream_in, norm_gain[layer, 0], norm_shift[layer, 0])[1]
        dfirst, gain_early, shift_early = pull(dnormed)
        gradient = dmiddle + dfirst
        gain[layer] = jnp.stack([gain_early, gain_late])
        shift[layer] = jnp.stack([shift_early, shift_late])
        outb[layer] = jnp.stack([bias_early, bias_late])
    if False:
        reduced = reduce_gradients([g.reshape(2, 4, 2, 2, 48, -1) for g in grads])
    else:
        reduced = [
            lax.psum_scatter(
                g.reshape(2 * dp_size, own, -1).astype(F32), ("tensor", "dp"), scatter_dimension=0
            )
            for g in grads
        ]
    g_gain, g_shift, g_outb, g_qvb, g_upb = lax.psum(
        (jnp.stack(gain), jnp.stack(shift), jnp.stack(outb), jnp.stack(qvb), jnp.stack(upb)),
        ("dp", "tensor"),
    )
    g_qvb = lax.dynamic_slice_in_dim(g_qvb, part * qv_bias.shape[2], qv_bias.shape[2], axis=2)
    g_upb = lax.dynamic_index_in_dim(g_upb, part, axis=1, keepdims=False)
    g_qkv = jnp.stack([reduced[4 * l].reshape(own, 3, -1) for l in range(layers)])
    g_out = jnp.stack([reduced[4 * l + 1].T for l in range(layers)])
    g_up = jnp.stack([reduced[4 * l + 2] for l in range(layers)])
    g_down = jnp.stack([reduced[4 * l + 3].T for l in range(layers)])
    return (final, gradient, g_gain, g_shift, g_qkv, g_qvb, g_out, g_up, g_upb, g_down, g_outb)


def fused_body(tokens, lengths, cotangent, norm_gain, norm_shift, qkv_weight, qv_bias, out_weight, up_weight,
               up_bias, down_weight, out_bias):
    part = lax.axis_index("tensor")
    layers = norm_gain.shape[0]
    rows, width = tokens.shape
    third = width // 2
    own = qkv_weight.shape[1]
    length = lax.dynamic_index_in_dim(lengths, part, keepdims=False)
    keep = jnp.arange(rows, dtype=jnp.int32) < length
    shards = []
    for layer in range(layers):
        shards += [
            qkv_weight[layer].reshape(own, -1),
            out_weight[layer].T,
            up_weight[layer],
            down_weight[layer].T,
        ]
    full, saved, final = forward(shards, tokens, lengths, norm_gain, norm_shift, out_bias, qv_bias, up_bias)
    full = [w.reshape(2, width, -1) for w in full]
    gradient = cotangent.astype(F32) * keep.astype(F32)[:, None]
    grads = [None] * (4 * layers)
    gain, shift, outb, qvb, upb = ([None] * layers for _ in range(5))
    scale = HEAD_DIM**-0.5
    for layer in reversed(range(layers)):
        stream_in, middle, _, _, project, attended, probs_t, activated, slope = saved[layer]
        w_qkv, w_out, w_up, w_down = full[4 * layer : 4 * layer + 4]
        normed = layer_norm(stream_in, norm_gain[layer, 0], norm_shift[layer, 0]).astype(BF16)
        normed_mid = layer_norm(middle, norm_gain[layer, 1], norm_shift[layer, 1]).astype(BF16)
        q, key, val = (
            heads(jnp.concatenate([project[t][:, j * third : (j + 1) * third] for t in range(2)], axis=1))
            for j in range(3)
        )
        probs = probs_t.reshape(-1, rows, rows).transpose(0, 2, 1)
        bias_late = jnp.sum(gradient, axis=0)
        dout = gradient.astype(BF16)
        grads[4 * layer + 3] = jnp.stack([mm(dout, activated[t], ((0,), (0,))).astype(BF16) for t in range(2)])
        dhidden = []
        for t in range(2):
            dact = mm(dout, w_down[t], ((1,), (0,)))
            dhidden.append((dact * slope[t].astype(F32)).astype(BF16))
        upb[layer] = jnp.stack([jnp.sum(d.astype(F32), axis=0) for d in dhidden])
        grads[4 * layer + 2] = jnp.stack([mm(normed_mid, d, ((0,), (0,))).astype(BF16) for d in dhidden])
        dnormed_mid = sum(mm(dhidden[t], w_up[t], ((1,), (1,))) for t in range(2))
        pull = jax.vjp(layer_norm, middle, norm_gain[layer, 1], norm_shift[layer, 1])[1]
        dmid, gain_late, shift_late = pull(dnormed_mid)
        dmiddle = gradient + dmid
        bias_early = jnp.sum(dmiddle, axis=0)
        dbranch = dmiddle.astype(BF16)
        dout_t = mm(dbranch, attended, ((0,), (0,))).astype(BF16)
        grads[4 * layer + 1] = halves(dout_t)
        dattended = heads(jnp.concatenate([mm(dbranch, w_out[t], ((1,), (0,))) for t in range(2)], axis=1).astype(BF16))
        p = probs.astype(F32)
        dval = jnp.einsum("hqk,hqd->hkd", probs, dattended, preferred_element_type=F32)
        dprobs = jnp.einsum("hqd,hkd->hqk", dattended, val, preferred_element_type=F32)
        dscores = (p * (dprobs - jnp.sum(p * dprobs, axis=-1, keepdims=True))).astype(BF16)
        dquery = jnp.einsum("hqk,hkd->hqd", dscores, key, preferred_element_type=F32) * scale
        dkey = jnp.einsum("hqk,hqd->hkd", dscores, q, preferred_element_type=F32) * scale
        parts = [flat(a).astype(BF16) for a in (dquery, dkey, dval)]
        dproject = [
            jnp.concatenate([a[:, t * third : (t + 1) * third] for a in parts], axis=1) for t in range(2)
        ]
        qvb[layer] = jnp.stack([jnp.sum(parts[0].astype(F32), axis=0), jnp.sum(parts[2].astype(F32), axis=0)])
        grads[4 * layer] = jnp.stack([mm(normed, d, ((0,), (0,))).astype(BF16) for d in dproject])
        dnormed = sum(mm(dproject[t], w_qkv[t], ((1,), (1,))) for t in range(2))
        pull = jax.vjp(layer_norm, stream_in, norm_gain[layer, 0], norm_shift[layer, 0])[1]
        dfirst, gain_early, shift_early = pull(dnormed)
        gradient = dmiddle + dfirst
        gain[layer] = jnp.stack([gain_early, gain_late])
        shift[layer] = jnp.stack([shift_early, shift_late])
        outb[layer] = jnp.stack([bias_early, bias_late])
    if True:
        reduced = reduce_gradients([g.reshape(2, 4, 2, 2, 48, -1) for g in grads])
    else:
        reduced = [
            lax.psum_scatter(
                g.reshape(2 * 32, own, -1).astype(F32), ("tensor", "dp"), scatter_dimension=0
            )
            for g in grads
        ]
    g_gain, g_shift, g_outb, g_qvb, g_upb = lax.psum(
        (jnp.stack(gain), jnp.stack(shift), jnp.stack(outb), jnp.stack(qvb), jnp.stack(upb)),
        ("dp", "tensor"),
    )
    g_qvb = lax.dynamic_slice_in_dim(g_qvb, part * qv_bias.shape[2], qv_bias.shape[2], axis=2)
    g_upb = lax.dynamic_index_in_dim(g_upb, part, axis=1, keepdims=False)
    g_qkv = jnp.stack([reduced[4 * l].reshape(own, 3, -1) for l in range(layers)])
    g_out = jnp.stack([reduced[4 * l + 1].T for l in range(layers)])
    g_up = jnp.stack([reduced[4 * l + 2] for l in range(layers)])
    g_down = jnp.stack([reduced[4 * l + 3].T for l in range(layers)])
    return (final, gradient, g_gain, g_shift, g_qkv, g_qvb, g_out, g_up, g_upb, g_down, g_outb)


def solution(mesh):
    use_kernels = mesh.shape["dp"] == 16 and mesh.shape["tensor"] == 2
    return jax.shard_map(
        fused_body if use_kernels else functools.partial(generic_body, mesh.shape["dp"]),
        mesh=mesh,
        in_specs=(
            P(("dp", "tensor"), None),
            P("dp"),
            P(("dp", "tensor"), None),
            P(),
            P(),
            P(None, "dp", None, "tensor"),
            P(None, None, "tensor"),
            P(None, "tensor", "dp"),
            P(None, "dp", "tensor"),
            P(None, "tensor"),
            P(None, "tensor", "dp"),
            P(),
        ),
        out_specs=(
            P(("dp", "tensor"), None),
            P(("dp", "tensor"), None),
            P(),
            P(),
            P(None, "dp", None, "tensor"),
            P(None, None, "tensor"),
            P(None, "tensor", "dp"),
            P(None, "dp", "tensor"),
            P(None, "tensor"),
            P(None, "tensor", "dp"),
            P(),
        ),
        check_vma=False,
    )
```

```python
import functools

import jax
import jax.numpy as jnp
from jax import lax
from jax.experimental import pallas as pl
from jax.experimental.pallas import tpu as pltpu
from jax.sharding import PartitionSpec as P

HEAD_DIM = 64
EPSILON = 1e-06
MESH = pl.DeviceIdType.MESH
VMEM_LIMIT = 60 * 2**20
BF16 = jnp.bfloat16
F32 = jnp.float32
ITEM_COUNT = 8
GATHER_ORDER = (0, 1, 2, 3, 4, 5, 6, 7)


def places():
    dp = lax.axis_index("dp")
    y = lax.axis_index("tensor")
    return dp // 4, (dp // 2) % 2, dp % 2, y


def partners(z, x, k, y):
    def at(z_, x_, k_, y_):
        return {"dp": (z_ * 2 + x_) * 2 + k_, "tensor": y_}

    along_z = [at((z + step) % 4, x, k, y) for step in (1, 2, 3)]
    return along_z + [at(z, 1 - x, k, y), at(z, x, k, 1 - y), at(z, x, 1 - k, y)]


def greet(peers):
    barrier = pltpu.get_barrier_semaphore()
    for peer in peers:
        pl.semaphore_signal(barrier, inc=1, device_id=peer, device_id_type=MESH)
    pl.semaphore_wait(barrier, len(peers))


def layer_norm(inputs, gain_row, shift_row):
    centered = inputs - jnp.mean(inputs, axis=-1, keepdims=True)
    variance = jnp.mean(centered * centered, axis=-1, keepdims=True)
    return centered * lax.rsqrt(variance + EPSILON) * gain_row + shift_row


def gelu_exact(values):
    return jax.nn.gelu(values, approximate=False)


def mm(left, right, contract):
    return lax.dot_general(left, right, (contract, ((), ())), preferred_element_type=F32)


def halves(array):
    return jnp.stack(jnp.split(array, 2, axis=1))


def heads(array):
    return array.reshape(array.shape[0], -1, HEAD_DIM).transpose(1, 0, 2)


def flat(array):
    return array.transpose(1, 0, 2).reshape(array.shape[1], -1)


def run_pump(events):
    queue = list(events)

    def step(count):
        for _ in range(min(count, len(queue))):
            queue.pop(0)[1]()

    def need(tag):
        if any(name == tag for name, _ in queue):
            while True:
                name, act = queue.pop(0)
                act()
                if name == tag:
                    break

    return need, step


def gather_events(own, held, send, recv, local, peers, place):
    z, x, k, y = place
    n = len(held)
    mine = [
        pltpu.make_async_copy(own[i], held[i].at[y, z, x, k], local.at[i]) for i in range(n)
    ]
    for copy in mine:
        copy.start()

    def remote(i, ref, slot, peer):
        return pltpu.make_async_remote_copy(
            ref, ref, send.at[i, slot], recv.at[i, slot], device_id=peers[peer], device_id_type=MESH
        )

    def copies(i, phase):
        b = held[i]
        if phase == 0:
            return [remote(i, b.at[y, z, x, k], j, j) for j in range(3)]
        if phase == 1:
            return [remote(i, b.at[y, 0:2, x, k], 3, 3), remote(i, b.at[y, 2:4, x, k], 4, 4)]
        if phase == 2:
            return [remote(i, b.at[y, 0:2, :, k], 5, 4), remote(i, b.at[:, 2:4, x, k], 6, 3)]
        return [remote(i, b.at[:, :, :, k], 7, 5)]

    live = {}

    def begin(i, phase):
        if phase == 0:
            mine[i].wait()
        live[i, phase] = copies(i, phase)
        for copy in live[i, phase]:
            copy.start()

    def finish(i, phase):
        for copy in live.pop((i, phase)):
            copy.wait()

    order = GATHER_ORDER
    events = []

    def event(spot, phase):
        i = order[spot]

        def act():
            finish(i, phase)
            if phase < 3:
                begin(i, phase + 1)
            if phase == 0 and spot + 2 < n:
                begin(order[spot + 2], 0)

        return (("w", i) if phase == 3 else None, act)

    for turn in range(n + 3):
        for phase in (3, 2, 1, 0):
            if 0 <= turn - phase < n:
                events.append(event(turn - phase, phase))

    def start():
        begin(order[0], 0)
        begin(order[1], 0)

    return start, events


def matrix(ref, *lead):
    value = ref[lead] if lead else ref[...]
    return value.reshape(-1, value.shape[-1])


def norm_rows(source, gain_row, shift_row, target):
    def block(t, carry):
        rows = pl.ds(pl.multiple_of(t * 128, 128), 128)
        target[rows, :] = layer_norm(source[rows, :], gain_row, shift_row).astype(BF16)
        return carry

    lax.fori_loop(0, source.shape[0] // 128, block, 0)


def turn_rows(source, target, k):
    for c in range(2):
        turned = source[:, c * 384 : (c + 1) * 384].T
        for j in range(8):
            block = c * 8 + j
            target[(block + k) % 2, block // 4, (block // 2) % 2] = turned[j * 48 : (j + 1) * 48]


def forward_kernel(*refs):
    n = ITEM_COUNT
    it = iter(refs)

    def take(count):
        return [next(it) for _ in range(count)]

    own = take(n)
    tokens, lengths, gain, shift, outb, qvb, upb = take(7)
    whole = take(n)
    saved = [take(9) for _ in range(2)]
    (final,) = take(1)
    held = take(n)
    (stream, middle, normed, turned, turned_mid, project, attended, active, slope, probs, qv_all, up_all) = take(12)
    send, recv, local, out_sem, prob_sem, small_send, small_recv, whole_sem = take(8)
    place = z, x, k, y = places()
    peers = partners(z, x, k, y)
    start, events = gather_events(own, held, send, recv, local, peers, place)
    need, step = run_pump(events)
    qv_all[y] = qvb[...]
    up_all[y] = upb[...]
    greet(peers)
    start()
    small = [
        pltpu.make_async_remote_copy(
            ref.at[y], ref.at[y], small_send.at[j], small_recv.at[j], device_id=peers[4], device_id_type=MESH
        )
        for j, ref in enumerate((qv_all, up_all))
    ]
    for copy in small:
        copy.start()
    stream[...] = tokens[...].astype(F32)
    length = lengths[y]
    rows = stream.shape[0]
    outgoing = {}

    def save(layer, slot, ref):
        copy = pltpu.make_async_copy(ref, saved[layer][slot], out_sem.at[layer, slot])
        copy.start()
        outgoing[slot] = copy

    def settle(slot):
        if slot in outgoing:
            outgoing.pop(slot).wait()

    back = []

    def keep_weight(i):
        copy = pltpu.make_async_copy(held[i], whole[i], whole_sem.at[i])
        copy.start()
        back.append(copy)

    for layer in range(2):
        w_qkv, w_out, w_up, w_down = held[4 * layer : 4 * layer + 4]
        settle(2)
        norm_rows(stream, gain[layer, 0:1], shift[layer, 0:1], normed)
        turn_rows(normed, turned, k)
        save(layer, 0, stream)
        save(layer, 2, turned)
        if layer == 0:
            for copy in small:
                copy.wait()
        need(("w", 4 * layer))
        keep_weight(4 * layer)
        settle(4)
        for half in range(2):
            for t in range(3):
                part = mm(normed[...], matrix(w_qkv, half, slice(None), slice(None), slice(None), slice(None), pl.ds(t * 384, 384)), ((1,), (0,)))
                if t != 1:
                    part = part + qv_all[half, layer, t // 2 : t // 2 + 1]
                project[half, :, t * 384 : (t + 1) * 384] = part.astype(BF16)
        save(layer, 4, project)
        step(1)
        settle(5)

        def pair(j, carry):
            half = j // 3
            at = (j % 3) * 128
            lane = lax.broadcasted_iota(jnp.int32, (1, 128), 1) < 64
            query = project[half, :, pl.ds(pl.multiple_of(at, 128), 128)]
            key = project[half, :, pl.ds(pl.multiple_of(at + 384, 128), 128)]
            value = project[half, :, pl.ds(pl.multiple_of(at + 768, 128), 128)]
            value_t = value.T
            hidden_key = lax.broadcasted_iota(jnp.int32, (rows, 1), 0) >= length
            both = []
            slot = j % 2
            for h in range(2):
                here = lane if h == 0 else jnp.logical_not(lane)
                some = jnp.where(here, key, jnp.zeros_like(key)) * jnp.asarray(HEAD_DIM**-0.5, BF16)
                scores = mm(some, query, ((1,), (1,)))
                scores = jnp.where(hidden_key, -1e30, scores)
                exponent = jnp.exp(scores - jnp.max(scores, axis=0, keepdims=True))
                prob = (exponent * (1.0 / jnp.sum(exponent, axis=0, keepdims=True))).astype(BF16)
                probs[j, h] = prob
                both.append(mm(value_t[h * 64 : (h + 1) * 64], prob, ((1,), (0,))))
            block = jnp.concatenate(both, axis=0).T
            attended[:, pl.ds(pl.multiple_of(j * 128, 128), 128)] = block.astype(BF16)
            return carry

        settle(6)
        for j0 in range(0, 6, 3):
            lax.fori_loop(j0, j0 + 3, pair, 0)
            step(1)
        save(layer, 5, attended)
        save(layer, 6, probs)
        need(("w", 4 * layer + 1))
        keep_weight(4 * layer + 1)
        settle(1)
        for c in range(2):
            cols = slice(c * 384, (c + 1) * 384)
            total = stream[:, cols] + outb[layer, 0:1, cols]
            for half in range(2):
                total += mm(attended[:, half * 384 : (half + 1) * 384], matrix(w_out, half, slice(2 * c, 2 * c + 2)), ((1,), (1,)))
            middle[:, cols] = total
        save(layer, 1, middle)
        settle(3)
        norm_rows(middle, gain[layer, 1:2], shift[layer, 1:2], normed)
        turn_rows(normed, turned_mid, k)
        save(layer, 3, turned_mid)
        step(1)
        need(("w", 4 * layer + 2))
        keep_weight(4 * layer + 2)
        settle(7)
        settle(8)

        def unit(t, carry):
            half = t // 3
            cols = pl.ds(pl.multiple_of((t % 3) * 512, 128), 512)
            hidden = mm(normed[...], matrix(w_up, half, slice(None), slice(None), slice(None), slice(None), cols), ((1,), (0,)))
            hidden = hidden + up_all[half, layer : layer + 1, cols]
            cdf = 0.5 * (1.0 + lax.erf(hidden * (0.5**0.5)))
            density = jnp.exp(-0.5 * hidden * hidden) * 0.3989422804014327
            active[half, :, cols] = (hidden * cdf).astype(BF16)
            slope[half, :, cols] = (cdf + hidden * density).astype(BF16)
            return carry

        for t0 in range(0, 6, 3):
            lax.fori_loop(t0, t0 + 3, unit, 0)
            step(1)
        save(layer, 7, active)
        save(layer, 8, slope)
        need(("w", 4 * layer + 3))
        keep_weight(4 * layer + 3)
        settle(0)
        for c in range(2):
            cols = slice(c * 384, (c + 1) * 384)
            total = middle[:, cols] + outb[layer, 1:2, cols]
            for half in range(2):
                total += mm(active[half], matrix(w_down, half, slice(2 * c, 2 * c + 2)), ((1,), (1,)))
            stream[:, cols] = total
        step(1)
    final[...] = stream[...].astype(BF16)
    for slot in list(outgoing):
        settle(slot)
    for copy in back:
        copy.wait()


def forward(shards, tokens, lengths, gain, shift, outb, qvb, upb):
    rows, width = tokens.shape
    widths = [s.shape[-1] for s in shards]
    full = [(2, 4, 2, 2, 48, w) for w in widths]
    layer_saves = [
        ((rows, width), F32),
        ((rows, width), F32),
        ((2, 4, 2, 48, rows), BF16),
        ((2, 4, 2, 48, rows), BF16),
        ((2, rows, widths[0]), BF16),
        ((rows, width), BF16),
        ((6, 2, rows, rows), BF16),
        ((2, rows, widths[2]), BF16),
        ((2, rows, widths[2]), BF16),
    ]
    any_spec = pl.BlockSpec(memory_space=pl.ANY)
    vmem_spec = pl.BlockSpec(memory_space=pltpu.VMEM)
    out_shape = (
        [jax.ShapeDtypeStruct(f, BF16) for f in full]
        + [jax.ShapeDtypeStruct(s, t) for s, t in layer_saves * 2]
        + [jax.ShapeDtypeStruct((rows, width), BF16)]
    )
    by_slot = {j: pltpu.VMEM(*layer_saves[j]) for j in range(9)}
    outs = pl.pallas_call(
        forward_kernel,
        out_shape=out_shape,
        in_specs=[any_spec] * ITEM_COUNT + [vmem_spec, pl.BlockSpec(memory_space=pltpu.SMEM)] + [vmem_spec] * 5,
        out_specs=[any_spec] * (ITEM_COUNT + 18) + [vmem_spec],
        scratch_shapes=[pltpu.VMEM(f, BF16) for f in full]
        + [
            by_slot[0],
            by_slot[1],
            pltpu.VMEM((rows, width), BF16),
            by_slot[2],
            by_slot[3],
            by_slot[4],
            by_slot[5],
            by_slot[7],
            by_slot[8],
            by_slot[6],
            pltpu.VMEM((2, *qvb.shape), F32),
            pltpu.VMEM((2, *upb.shape), F32),
            pltpu.SemaphoreType.DMA((ITEM_COUNT, 8)),
            pltpu.SemaphoreType.DMA((ITEM_COUNT, 8)),
            pltpu.SemaphoreType.DMA((ITEM_COUNT,)),
            pltpu.SemaphoreType.DMA((2, 9)),
            pltpu.SemaphoreType.DMA((2,)),
            pltpu.SemaphoreType.DMA((2,)),
            pltpu.SemaphoreType.DMA((2,)),
            pltpu.SemaphoreType.DMA((ITEM_COUNT,)),
        ],
        compiler_params=pltpu.CompilerParams(
            collective_id=0, has_side_effects=True, vmem_limit_bytes=VMEM_LIMIT
        ),
        name="forward",
    )(*shards, tokens, lengths, gain, shift, outb, qvb, upb)
    return outs[:ITEM_COUNT], [outs[ITEM_COUNT + 9 * l : ITEM_COUNT + 9 * l + 9] for l in range(2)], outs[-1]


REDUCE_POINTS = (
    {
        "before_d": ((1, 3), (2, 3), (0, 4)),
        "after_d": ((4, 1), (3, 2)),
        "before_u": ((1, 4),),
        "after_u": ((5, 1),),
        "after_norm": ((3, 3),),
        "before_o": ((2, 4),),
        "after_o": ((6, 1), (4, 2)),
        "mid_attention": ((5, 2),),
        "after_attention": ((4, 3), (6, 2)),
        "before_q": ((3, 4),),
        "after_q": ((7, 1),),
    },
    {
        "after_d": ((0, 1),),
        "after_u": ((1, 1),),
        "after_norm": ((0, 2),),
        "after_o": ((2, 1),),
        "after_attention": ((1, 2), (0, 3), (2, 2)),
        "after_q": ((3, 1),),
    },
)


def norm_back(source, upstream, gain_row, gradient, rounded):
    def block(t, sums):
        rows = pl.ds(pl.multiple_of(t * 64, 64), 64)
        inputs = source[rows, :]
        centered = inputs - jnp.mean(inputs, axis=-1, keepdims=True)
        rate = lax.rsqrt(jnp.mean(centered * centered, axis=-1, keepdims=True) + EPSILON)
        unit = centered * rate
        above = upstream[rows, :]
        pull = above * gain_row
        along = jnp.mean(pull * unit, axis=-1, keepdims=True)
        total = gradient[rows, :] + rate * (pull - jnp.mean(pull, axis=-1, keepdims=True) - unit * along)
        gradient[rows, :] = total
        if rounded is not None:
            rounded[rows, :] = total.astype(BF16)
        return (
            sums[0] + jnp.sum(above * unit, axis=0, keepdims=True),
            sums[1] + jnp.sum(above, axis=0, keepdims=True),
            sums[2] + jnp.sum(total, axis=0, keepdims=True),
        )

    zero = jnp.zeros((1, source.shape[1]), F32)
    return lax.fori_loop(0, source.shape[0] // 64, block, (zero, zero, zero))


def backward_kernel(*refs):
    n = ITEM_COUNT
    it = iter(refs)

    def take(count):
        return [next(it) for _ in range(count)]

    whole = take(n)
    saved = [take(9) for _ in range(2)]
    cotangent, lengths, gain = take(3)
    out_q, out_o, out_u, out_d, token_grad, sums = take(6)
    outs = (out_q, out_o, out_u, out_d)
    (slot_a, slot_b, stream, middle, turned, turned_mid, project, attended, active, slope, probs) = take(11)
    (gradient, upstream, rounded, left, dattended, dproject) = take(6)
    held = take(4)
    (to_core, from_core) = take(2)
    from_a, from_b = take(4), take(4)
    from_c, from_d, from_z = take(8), take(8), take(8)
    small_c, small_x, small_y, small_z = take(4)
    (fetch_sem, prob_sem, send, recv, credit, small_send, small_recv, last_sem) = take(8)
    place = z, x, k, y = places()
    peers = partners(z, x, k, y)
    rows = stream.shape[0]

    fetches = {}

    def fetch(name, pairs):
        fetches[name] = [pltpu.make_async_copy(s, t, fetch_sem.at[name, j]) for j, (s, t) in enumerate(pairs)]
        for copy in fetches[name]:
            copy.start()

    def ready(name):
        for copy in fetches.pop(name):
            copy.wait()

    def weights_into(slot, layer, kind):
        w_qkv, w_out, w_up, w_down = whole[4 * layer : 4 * layer + 4]
        if kind == "d":
            return [(w_down, slot)]
        if kind == "u":
            return [(w_up, slot)]
        lead = (slice(None),) * 5
        return [(w_qkv, slot.at[(*lead, pl.ds(0, 1152))]), (w_out, slot.at[(*lead, pl.ds(1152, 384))])]

    SLOT_A, SLOT_B, STREAM, MIDDLE, TURNED, TURNED_MID, PROJECT, ATTENDED, ACTIVE, SLOPE, COT = range(11)
    buffers = {
        STREAM: (stream, 0),
        MIDDLE: (middle, 1),
        TURNED: (turned, 2),
        TURNED_MID: (turned_mid, 3),
        PROJECT: (project, 4),
        ATTENDED: (attended, 5),
        ACTIVE: (active, 7),
        SLOPE: (slope, 8),
    }

    def fetch_saved(name, layer):
        target, index = buffers[name]
        fetch(name, [(saved[layer][index], target)])

    def prob_copy(layer, j):
        return pltpu.make_async_copy(saved[layer][6].at[j], probs.at[j % 2], prob_sem.at[j % 2])

    fetch(COT, [(cotangent, rounded)])
    fetch(SLOT_A, weights_into(slot_a, 1, "d"))
    for name in (SLOPE, ACTIVE):
        fetch_saved(name, 1)
    fetch(SLOT_B, weights_into(slot_b, 1, "u"))
    for name in (TURNED_MID, MIDDLE, ATTENDED, PROJECT, TURNED, STREAM):
        fetch_saved(name, 1)
    prob_copy(1, 0).start()
    slots = {("d", 1): (SLOT_A, slot_a), ("u", 1): (SLOT_B, slot_b), ("q", 1): (SLOT_A, slot_a),
             ("d", 0): (SLOT_B, slot_b), ("u", 0): (SLOT_A, slot_a), ("q", 0): (SLOT_B, slot_b)}
    greet(peers)

    kinds = [(1, 3), (1, 2), (1, 1), (1, 0), (0, 3), (0, 2), (0, 1), (0, 0)]

    def remote(r, source, target, slot, peer):
        return pltpu.make_async_remote_copy(
            source, target, send.at[r, slot], recv.at[r, slot], device_id=peers[peer], device_id_type=MESH
        )

    live = {}

    def go(key, copies):
        live[key] = copies
        for copy in copies:
            copy.start()

    def done(key):
        for copy in live.pop(key):
            copy.wait()

    def post(r, half):
        width = held[kinds[r][1]].shape[-1]
        cols = pl.ds(0, width)
        if r > 0:
            pl.semaphore_wait(credit.at[half], 1)
        at = (half, slice(None), slice(None), slice(None), cols)
        go((r, "core", half), [remote(r, to_core.at[at], from_core.at[at], half, 5)])

    def take_core(r, half):
        done((r, "core", half))
        b = held[kinds[r][1]]
        width = b.shape[-1]

        def block(t, carry):
            at = (half, t // 2, t % 2)
            b[at] = b[at] + from_core[(*at, slice(None), pl.ds(0, width))]
            return carry

        lax.fori_loop(0, 8, block, 0)
        if r < n - 1:
            pl.semaphore_signal(credit.at[half], inc=1, device_id=peers[5], device_id_type=MESH)

    def turn_one(r):
        take_core(r, 0)
        take_core(r, 1)
        kind = kinds[r][1]
        b = held[kind]
        go((r, 1), [
            remote(r, b.at[1 - y, 0:2], from_a[kind], 2, 4),
            remote(r, b.at[:, 2:4, 1 - x], from_b[kind], 3, 3),
        ])

    def turn_two(r):
        done((r, 1))
        kind = kinds[r][1]
        b = held[kind]

        def block(t, carry):
            p, q = t // 2, t % 2
            b[y, p, q] = b[y, p, q] + from_a[kind][p, q]
            b[p, 2 + q, x] = b[p, 2 + q, x] + from_b[kind][p, q]
            return carry

        lax.fori_loop(0, 4, block, 0)
        go((r, 2), [
            remote(r, b.at[y, 0:2, 1 - x], from_c[r], 4, 3),
            remote(r, b.at[1 - y, 2:4, x], from_d[r], 5, 4),
        ])

    def turn_three(r):
        done((r, 2))
        b = held[kinds[r][1]]

        def block(t, carry):
            b[y, t, x] = b[y, t, x] + from_c[r][t]
            b[y, 2 + t, x] = b[y, 2 + t, x] + from_d[r][t]
            return carry

        lax.fori_loop(0, 2, block, 0)
        go((r, 3), [remote(r, b.at[y, (z + 1 + j) % 4, x], from_z[r].at[j], 6 + j, j) for j in range(3)])

    def turn_four(r):
        done((r, 3))
        layer, kind = kinds[r]
        b = held[kind]
        width = b.shape[-1]
        for at in range(0, width, 384):
            cols = pl.ds(at, 384)
            value = b[y, z, x, :, cols].astype(F32)
            for j in range(3):
                value += from_z[r][j, :, cols].astype(F32)
            outs[kind][layer, :, cols] = value

    turns = {1: turn_one, 2: turn_two, 3: turn_three, 4: turn_four}

    def pump(*steps):
        for r, turn in steps:
            turns[turn](r)

    def at_point(layer, point):
        pump(*REDUCE_POINTS[layer].get(point, ()))

    def weight_gradient(r, lhs, rhs, half):
        b = held[kinds[r][1]]
        width = b.shape[-1]
        size = 512 if width % 512 == 0 else 384

        def chunk(t, carry):
            cols = pl.ds(pl.multiple_of(t * size, 128), size)
            value = mm(lhs[...].reshape(768, rows), rhs(cols), ((1,), (0,))).astype(BF16)
            b[half, :, :, :, cols] = value[:384].reshape(4, 2, 48, size)
            to_core[half, :, :, :, cols] = value[384:].reshape(4, 2, 48, size)
            return carry

        lax.fori_loop(0, width // size, chunk, 0)

    ready(COT)
    keep = lax.broadcasted_iota(jnp.int32, (rows, 1), 0) < lengths[y]
    gradient[...] = jnp.where(keep, rounded[...].astype(F32), 0.0)
    rounded[...] = gradient[...].astype(BF16)
    everything = (slice(None),) * 4
    for layer in (1, 0):
        first = 0 if layer == 1 else 4
        sums[layer, 2:3, 768:1536] = jnp.sum(gradient[...], axis=0, keepdims=True)
        turn_rows(rounded, left, k)
        name, w_down = slots["d", layer]
        ready(name)
        ready(SLOPE)
        ready(ACTIVE)
        r = first
        at_point(layer, "before_d")
        for half in range(2):
            def unit(t, carry):
                cols = pl.ds(pl.multiple_of(t * 512, 128), 512)
                dact = mm(rounded[...], matrix(w_down, half, *everything, cols), ((1,), (0,)))
                dhidden = (dact * slope[half, :, cols].astype(F32)).astype(BF16)
                slope[half, :, cols] = dhidden
                sums[layer, 4 + half : 5 + half, cols] = jnp.sum(dhidden.astype(F32), axis=0, keepdims=True)
                return carry

            weight_gradient(r, left, lambda cols: active[half, :, cols], half)
            post(r, half)
            lax.fori_loop(0, 3, unit, 0)
        if layer == 1:
            fetch(SLOT_A, weights_into(slot_a, 1, "q"))
            fetch_saved(ACTIVE, 0)
        else:
            fetch(SLOT_B, weights_into(slot_b, 0, "q"))
        at_point(layer, "after_d")
        r = first + 1
        name, w_up = slots["u", layer]
        ready(name)
        ready(TURNED_MID)
        at_point(layer, "before_u")
        for half in range(2):
            weight_gradient(r, turned_mid, lambda cols: slope[half, :, cols], half)
            post(r, half)
        at_point(layer, "after_u")
        for c in range(2):
            total = jnp.zeros((rows, 384), F32)
            for half in range(2):
                total += mm(slope[half], matrix(w_up, half, slice(2 * c, 2 * c + 2)), ((1,), (1,)))
            upstream[:, c * 384 : (c + 1) * 384] = total
        if layer == 1:
            fetch(SLOT_B, weights_into(slot_b, 0, "d"))
            fetch_saved(SLOPE, 0)
            fetch_saved(TURNED_MID, 0)
        ready(MIDDLE)
        gain_sum, shift_sum, bias_sum = norm_back(middle, upstream, gain[layer, 1:2], gradient, rounded)
        sums[layer, 0:1, 768:1536] = gain_sum
        sums[layer, 1:2, 768:1536] = shift_sum
        sums[layer, 2:3, 0:768] = bias_sum
        if layer == 1:
            fetch_saved(MIDDLE, 0)
        at_point(layer, "after_norm")
        turn_rows(rounded, left, k)
        r = first + 2
        name, w_qo = slots["q", layer]
        ready(name)
        ready(ATTENDED)
        at_point(layer, "before_o")
        for half in range(2):
            weight_gradient(r, left, lambda cols: attended[:, half * 384 : (half + 1) * 384], half)
            post(r, half)
            dattended[half] = mm(rounded[...], matrix(w_qo, half, *everything, slice(1152, 1536)), ((1,), (0,))).astype(BF16)
        if layer == 1:
            fetch_saved(ATTENDED, 0)
        at_point(layer, "after_o")
        ready(PROJECT)
        scale = HEAD_DIM**-0.5

        def pair(j, carry):
            half = j // 3
            at = (j % 3) * 128
            prob_copy(layer, j).wait()

            @pl.when(j < 5)
            def _():
                prob_copy(layer, j + 1).start()

            lane = lax.broadcasted_iota(jnp.int32, (1, 128), 1) < 64
            columns = [pl.ds(pl.multiple_of(at + t * 384, 128), 128) for t in range(3)]
            query, key, value = (project[half, :, c] for c in columns)
            above = dattended[half, :, columns[0]]
            key_t = key.T
            dkeys, dvalues, dqueries = [], [], []
            for h in range(2):
                here = lane if h == 0 else jnp.logical_not(lane)
                prob = probs[j % 2, h]
                dprob = mm(jnp.where(here, value, jnp.zeros_like(value)), above, ((1,), (1,)))
                prob32 = prob.astype(F32)
                both = prob32 * dprob
                dscore = (both - prob32 * jnp.sum(both, axis=0, keepdims=True)).astype(BF16)
                dvalues.append(mm(prob, above, ((1,), (0,))))
                dkeys.append(mm(dscore, query, ((1,), (0,))))
                dqueries.append(mm(key_t[h * 64 : (h + 1) * 64], dscore, ((1,), (0,))))
            dproject[half, :, columns[0]] = (jnp.concatenate(dqueries, axis=0) * scale).T.astype(BF16)
            dproject[half, :, columns[1]] = (jnp.where(lane, dkeys[0], dkeys[1]) * scale).astype(BF16)
            dproject[half, :, columns[2]] = jnp.where(lane, dvalues[0], dvalues[1]).astype(BF16)
            return carry

        lax.fori_loop(0, 3, pair, 0)
        at_point(layer, "mid_attention")
        lax.fori_loop(3, 6, pair, 0)
        if layer == 1:
            fetch_saved(PROJECT, 0)
            prob_copy(0, 0).start()
        at_point(layer, "after_attention")
        r = first + 3
        ready(TURNED)
        at_point(layer, "before_q")
        for half in range(2):
            for t in (0, 2):
                sums[layer, 3:4, (t // 2) * 768 + half * 384 : (t // 2) * 768 + half * 384 + 384] = jnp.sum(
                    dproject[half, :, t * 384 : (t + 1) * 384].astype(F32), axis=0, keepdims=True
                )
            weight_gradient(r, turned, lambda cols: dproject[half, :, cols], half)
            post(r, half)
        at_point(layer, "after_q")
        for c in range(2):
            total = jnp.zeros((rows, 384), F32)
            for half in range(2):
                total += mm(dproject[half], matrix(w_qo, half, slice(2 * c, 2 * c + 2), slice(None), slice(None), slice(None), slice(0, 1152)), ((1,), (1,)))
            upstream[:, c * 384 : (c + 1) * 384] = total
        if layer == 1:
            fetch(SLOT_A, weights_into(slot_a, 0, "u"))
            fetch_saved(TURNED, 0)
        ready(STREAM)
        gain_sum, shift_sum, _ = norm_back(stream, upstream, gain[layer, 0:1], gradient, rounded if layer == 1 else None)
        sums[layer, 0:1, 0:768] = gain_sum
        sums[layer, 1:2, 0:768] = shift_sum
        if layer == 1:
            fetch_saved(STREAM, 0)
    last = pltpu.make_async_copy(gradient, token_grad, last_sem)
    last.start()

    sums[:, 6:8, :] = jnp.zeros((2, 2, 1536), F32)

    def exchange(slot, target, peer):
        copy = pltpu.make_async_remote_copy(
            sums, target, small_send.at[slot], small_recv.at[slot], device_id=peers[peer], device_id_type=MESH
        )
        copy.start()
        return copy

    pump((5, 3), (6, 3), (4, 4))
    copy = exchange(0, small_c, 5)
    pump((7, 2), (5, 4), (6, 4))
    copy.wait()
    sums[...] += small_c[...]
    copy = exchange(1, small_x, 3)
    copy.wait()
    sums[...] += small_x[...]
    copy = exchange(2, small_y, 4)
    copy.wait()
    sums[...] += small_y[...]
    small_z[z] = sums[...]
    copies = [exchange(3 + j, small_z.at[z], j) for j in range(3)]
    pump((n - 1, 3))
    for copy in copies:
        copy.wait()
    sums[...] = (small_z[0] + small_z[1]) + (small_z[2] + small_z[3])
    pump((n - 1, 4))
    last.wait()


def backward(whole, saved, cotangent, lengths, gain):
    rows, width = cotangent.shape
    widths = [w.shape[-1] for w in whole[:4]]
    any_spec = pl.BlockSpec(memory_space=pl.ANY)
    vmem_spec = pl.BlockSpec(memory_space=pltpu.VMEM)

    def blocks(*lead):
        return [pltpu.VMEM((*lead, 48, w), BF16) for w in widths]

    def in_order(*lead):
        return [pltpu.VMEM((*lead, 48, widths[kind]), BF16) for kind in (3, 2, 1, 0)] * 2

    wide = widths[2]
    small = (2, 8, wide)
    outs = pl.pallas_call(
        backward_kernel,
        out_shape=[jax.ShapeDtypeStruct((2, 48, w), F32) for w in widths]
        + [jax.ShapeDtypeStruct((rows, width), F32), jax.ShapeDtypeStruct(small, F32)],
        in_specs=[any_spec] * (ITEM_COUNT + 18 + 1) + [pl.BlockSpec(memory_space=pltpu.SMEM), vmem_spec],
        out_specs=[vmem_spec] * 4 + [any_spec, vmem_spec],
        scratch_shapes=[
            pltpu.VMEM((2, 4, 2, 2, 48, wide), BF16),
            pltpu.VMEM((2, 4, 2, 2, 48, wide), BF16),
            pltpu.VMEM((rows, width), F32),
            pltpu.VMEM((rows, width), F32),
            pltpu.VMEM((2, 4, 2, 48, rows), BF16),
            pltpu.VMEM((2, 4, 2, 48, rows), BF16),
            pltpu.VMEM((2, rows, widths[0]), BF16),
            pltpu.VMEM((rows, width), BF16),
            pltpu.VMEM((2, rows, wide), BF16),
            pltpu.VMEM((2, rows, wide), BF16),
            pltpu.VMEM((2, 2, rows, rows), BF16),
            pltpu.VMEM((rows, width), F32),
            pltpu.VMEM((rows, width), F32),
            pltpu.VMEM((rows, width), BF16),
            pltpu.VMEM((2, 4, 2, 48, rows), BF16),
            pltpu.VMEM((2, rows, width // 2), BF16),
            pltpu.VMEM((2, rows, widths[0]), BF16),
        ]
        + blocks(2, 4, 2)
        + [pltpu.VMEM((2, 4, 2, 48, wide), BF16), pltpu.VMEM((2, 4, 2, 48, wide), BF16)]
        + blocks(2, 2)
        + blocks(2, 2)
        + in_order(2)
        + in_order(2)
        + in_order(3)
        + [pltpu.VMEM(small, F32)] * 3
        + [pltpu.VMEM((4, *small), F32)]
        + [
            pltpu.SemaphoreType.DMA((11, 2)),
            pltpu.SemaphoreType.DMA((2,)),
            pltpu.SemaphoreType.DMA((ITEM_COUNT, 9)),
            pltpu.SemaphoreType.DMA((ITEM_COUNT, 9)),
            pltpu.SemaphoreType.REGULAR((2,)),
            pltpu.SemaphoreType.DMA((6,)),
            pltpu.SemaphoreType.DMA((6,)),
            pltpu.SemaphoreType.DMA,
        ],
        compiler_params=pltpu.CompilerParams(
            collective_id=1, has_side_effects=True, vmem_limit_bytes=63 * 2**20
        ),
        name="backward",
    )(*whole, *saved[0], *saved[1], cotangent, lengths, gain)
    return outs


def generic_body(dp_size, tokens, lengths, cotangent, norm_gain, norm_shift, qkv_weight, qv_bias,
         out_weight, up_weight, up_bias, down_weight, out_bias):
    part = lax.axis_index("tensor")
    layers = norm_gain.shape[0]
    rows, width = tokens.shape
    length = lax.dynamic_index_in_dim(lengths, part, keepdims=False)
    keep = jnp.arange(rows, dtype=jnp.int32) < length
    own = qkv_weight.shape[1]
    shards = []
    for layer in range(layers):
        shards += [
            qkv_weight[layer].reshape(own, -1),
            out_weight[layer].T,
            up_weight[layer],
            down_weight[layer].T,
        ]
    if False:
        full = [w.reshape(2, width, -1) for w in gather_weights(shards)]
    else:
        full = [
            lax.all_gather(s, ("tensor", "dp"), axis=0).reshape(2, width, -1) for s in shards
        ]
    qv_all = lax.all_gather(qv_bias, "tensor", axis=0)
    upb_all = lax.all_gather(up_bias, "tensor", axis=0)
    scale = HEAD_DIM**-0.5
    stream = tokens.astype(F32)
    saved = []
    for layer in range(layers):
        w_qkv, w_out, w_up, w_down = full[4 * layer : 4 * layer + 4]
        normed = layer_norm(stream, norm_gain[layer, 0], norm_shift[layer, 0]).astype(BF16)
        project = []
        for t in range(2):
            b = jnp.concatenate([qv_all[t, layer, 0], jnp.zeros_like(qv_all[t, layer, 0]), qv_all[t, layer, 1]])
            project.append((mm(normed, w_qkv[t], ((1,), (0,))) + b).astype(BF16))
        third = width // 2
        q, key, val = (
            heads(jnp.concatenate([project[t][:, j * third : (j + 1) * third] for t in range(2)], axis=1))
            for j in range(3)
        )
        scores = jnp.einsum("hqd,hkd->hqk", q, key, preferred_element_type=F32) * scale
        scores = jnp.where(keep[None, None, :], scores, -1e30)
        highest = jnp.max(scores, axis=-1, keepdims=True)
        exponent = jnp.exp(scores - highest)
        probs32 = exponent / jnp.sum(exponent, axis=-1, keepdims=True)
        probs = probs32.astype(BF16)
        attended = flat(jnp.einsum("hqk,hkd->hqd", probs, val, preferred_element_type=F32)).astype(BF16)
        branch = sum(mm(attended[:, t * third : (t + 1) * third], w_out[t], ((1,), (1,))) for t in range(2))
        middle = stream + branch + out_bias[layer, 0]
        normed_mid = layer_norm(middle, norm_gain[layer, 1], norm_shift[layer, 1]).astype(BF16)
        hidden = [mm(normed_mid, w_up[t], ((1,), (0,))) + upb_all[t, layer] for t in range(2)]
        activated = [gelu_exact(h).astype(BF16) for h in hidden]
        branch_mlp = sum(mm(activated[t], w_down[t], ((1,), (1,))) for t in range(2))
        saved.append((stream, middle, normed, q, key, val, probs, attended, normed_mid, hidden, activated))
        stream = middle + branch_mlp + out_bias[layer, 1]
    final = stream.astype(BF16)
    gradient = cotangent.astype(F32) * keep.astype(F32)[:, None]
    grads = [None] * (4 * layers)
    gain, shift, outb, qvb, upb = ([None] * layers for _ in range(5))
    for layer in reversed(range(layers)):
        stream_in, middle, normed, q, key, val, probs, attended, normed_mid, hidden, activated = saved[layer]
        w_qkv, w_out, w_up, w_down = full[4 * layer : 4 * layer + 4]
        third = width // 2
        bias_late = jnp.sum(gradient, axis=0)
        dout = gradient.astype(BF16)
        grads[4 * layer + 3] = jnp.stack([mm(dout, activated[t], ((0,), (0,))).astype(BF16) for t in range(2)])
        dhidden = []
        for t in range(2):
            dact = mm(dout, w_down[t], ((1,), (0,)))
            dhidden.append(jax.vjp(gelu_exact, hidden[t])[1](dact)[0].astype(BF16))
        upb[layer] = jnp.stack([jnp.sum(d.astype(F32), axis=0) for d in dhidden])
        grads[4 * layer + 2] = jnp.stack([mm(normed_mid, d, ((0,), (0,))).astype(BF16) for d in dhidden])
        dnormed_mid = sum(mm(dhidden[t], w_up[t], ((1,), (1,))) for t in range(2))
        pull = jax.vjp(layer_norm, middle, norm_gain[layer, 1], norm_shift[layer, 1])[1]
        dmid, gain_late, shift_late = pull(dnormed_mid)
        dmiddle = gradient + dmid
        bias_early = jnp.sum(dmiddle, axis=0)
        dbranch = dmiddle.astype(BF16)
        dout_t = mm(dbranch, attended, ((0,), (0,))).astype(BF16)
        grads[4 * layer + 1] = halves(dout_t)
        dattended = heads(jnp.concatenate([mm(dbranch, w_out[t], ((1,), (0,))) for t in range(2)], axis=1).astype(BF16))
        p = probs.astype(F32)
        dval = jnp.einsum("hqk,hqd->hkd", probs, dattended, preferred_element_type=F32)
        dprobs = jnp.einsum("hqd,hkd->hqk", dattended, val, preferred_element_type=F32)
        dscores = (p * (dprobs - jnp.sum(p * dprobs, axis=-1, keepdims=True))).astype(BF16)
        dquery = jnp.einsum("hqk,hkd->hqd", dscores, key, preferred_element_type=F32) * scale
        dkey = jnp.einsum("hqk,hqd->hkd", dscores, q, preferred_element_type=F32) * scale
        parts = [flat(a).astype(BF16) for a in (dquery, dkey, dval)]
        dproject = [
            jnp.concatenate([a[:, t * third : (t + 1) * third] for a in parts], axis=1) for t in range(2)
        ]
        qvb[layer] = jnp.stack([jnp.sum(parts[0].astype(F32), axis=0), jnp.sum(parts[2].astype(F32), axis=0)])
        grads[4 * layer] = jnp.stack([mm(normed, d, ((0,), (0,))).astype(BF16) for d in dproject])
        dnormed = sum(mm(dproject[t], w_qkv[t], ((1,), (1,))) for t in range(2))
        pull = jax.vjp(layer_norm, stream_in, norm_gain[layer, 0], norm_shift[layer, 0])[1]
        dfirst, gain_early, shift_early = pull(dnormed)
        gradient = dmiddle + dfirst
        gain[layer] = jnp.stack([gain_early, gain_late])
        shift[layer] = jnp.stack([shift_early, shift_late])
        outb[layer] = jnp.stack([bias_early, bias_late])
    if False:
        reduced = reduce_gradients([g.reshape(2, 4, 2, 2, 48, -1) for g in grads])
    else:
        reduced = [
            lax.psum_scatter(
                g.reshape(2 * dp_size, own, -1).astype(F32), ("tensor", "dp"), scatter_dimension=0
            )
            for g in grads
        ]
    g_gain, g_shift, g_outb, g_qvb, g_upb = lax.psum(
        (jnp.stack(gain), jnp.stack(shift), jnp.stack(outb), jnp.stack(qvb), jnp.stack(upb)),
        ("dp", "tensor"),
    )
    g_qvb = lax.dynamic_slice_in_dim(g_qvb, part * qv_bias.shape[2], qv_bias.shape[2], axis=2)
    g_upb = lax.dynamic_index_in_dim(g_upb, part, axis=1, keepdims=False)
    g_qkv = jnp.stack([reduced[4 * l].reshape(own, 3, -1) for l in range(layers)])
    g_out = jnp.stack([reduced[4 * l + 1].T for l in range(layers)])
    g_up = jnp.stack([reduced[4 * l + 2] for l in range(layers)])
    g_down = jnp.stack([reduced[4 * l + 3].T for l in range(layers)])
    return (final, gradient, g_gain, g_shift, g_qkv, g_qvb, g_out, g_up, g_upb, g_down, g_outb)


def fused_body(tokens, lengths, cotangent, norm_gain, norm_shift, qkv_weight, qv_bias, out_weight, up_weight,
               up_bias, down_weight, out_bias):
    part = lax.axis_index("tensor")
    layers = norm_gain.shape[0]
    rows, width = tokens.shape
    third = width // 2
    own = qkv_weight.shape[1]
    shards = []
    for layer in range(layers):
        shards += [
            qkv_weight[layer].reshape(own, -1),
            out_weight[layer].T,
            up_weight[layer],
            down_weight[layer].T,
        ]
    full, saved, final = forward(shards, tokens, lengths, norm_gain, norm_shift, out_bias, qv_bias, up_bias)
    g_qkv, g_out, g_up, g_down, token_grad, small = backward(full, saved, cotangent, lengths, norm_gain)
    g_gain, g_shift, g_outb, g_qvb = (small[:, j].reshape(layers, 2, width) for j in range(4))
    g_upb = lax.dynamic_index_in_dim(small, 4 + part, axis=1, keepdims=False)
    g_qvb = lax.dynamic_slice_in_dim(g_qvb, part * third, third, axis=2)
    return (
        final,
        token_grad,
        g_gain,
        g_shift,
        g_qkv.reshape(layers, own, 3, third),
        g_qvb,
        g_out.transpose(0, 2, 1),
        g_up,
        g_upb,
        g_down.transpose(0, 2, 1),
        g_outb,
    )


def solution(mesh):
    use_kernels = mesh.shape["dp"] == 16 and mesh.shape["tensor"] == 2
    return jax.shard_map(
        fused_body if use_kernels else functools.partial(generic_body, mesh.shape["dp"]),
        mesh=mesh,
        in_specs=(
            P(("dp", "tensor"), None),
            P("dp"),
            P(("dp", "tensor"), None),
            P(),
            P(),
            P(None, "dp", None, "tensor"),
            P(None, None, "tensor"),
            P(None, "tensor", "dp"),
            P(None, "dp", "tensor"),
            P(None, "tensor"),
            P(None, "tensor", "dp"),
            P(),
        ),
        out_specs=(
            P(("dp", "tensor"), None),
            P(("dp", "tensor"), None),
            P(),
            P(),
            P(None, "dp", None, "tensor"),
            P(None, None, "tensor"),
            P(None, "tensor", "dp"),
            P(None, "dp", "tensor"),
            P(None, "tensor"),
            P(None, "tensor", "dp"),
            P(),
        ),
        check_vma=False,
    )
```

```python
import functools

import jax
import jax.numpy as jnp
from jax import lax
from jax.experimental import pallas as pl
from jax.experimental.pallas import tpu as pltpu
from jax.sharding import PartitionSpec as P

HEAD_DIM = 64
EPSILON = 1e-06
MESH = pl.DeviceIdType.MESH
VMEM_LIMIT = 60 * 2**20
BF16 = jnp.bfloat16
F32 = jnp.float32
ITEM_COUNT = 8
GATHER_CHAINS = (
    (0, 0, 512, "zxy"),
    (0, 512, 640, "zyx"),
    (1, 0, 256, "yzx"),
    (1, 256, 128, "xzy"),
    (2, 0, 768, "zxy"),
    (2, 768, 768, "zyx"),
    (3, 0, 768, "zxy"),
    (3, 768, 768, "zyx"),
    (4, 0, 512, "xzy"),
    (4, 512, 640, "yzx"),
    (5, 0, 256, "zyx"),
    (5, 256, 128, "zxy"),
    (6, 0, 768, "zxy"),
    (6, 768, 768, "zyx"),
    (7, 0, 768, "xzy"),
    (7, 768, 768, "yzx"),
)
GATHER_TABLE = (
    (12, 32, 8, 36, 20, 0),
    (),
    (-13, 56, -9, 60, -33, -37, -57, -61, -21, 21, 24, -1, 1, 13, -22, 22, -2, 2, -25, 25, 4, -14, 14, 16, -5, 44, -3, 5, 3, -15, 15, -23, -4, 23, -17, 17, 28, -16, -45, 9, -24, -6, -26, 6, 26, -29, 29, 40, -18, 45, -10, 33, -41, 37, -27, 18, 27, -7, 10, 7, -28, -34, 48, -46, -8, -30, 30, 46),
    (-11, 11),
    (-12,),
    (-38, 38, 52),
    (-19, 41, 19, -49, 57, -47, 34, 47, -31, 49),
    (-20, 31, -48, -42),
    (-32, -53, 53, 61),
    (),
    (-39, 42, 39, -35, 35),
    (-40,),
    (-36, -50, 50, -54, 54, -58, 58),
    (-43, 43),
    (-44,),
    (),
    (-62, 62, -51, 51),
    (-55, 55),
    (-52, -56),
    (),
    (-59, 59, -63, 63, -60, -64),
    (),
)


REDUCE_CHAINS = (
    (0, 0, 768, "yzx"),
    (0, 768, 768, "xzy"),
    (1, 0, 768, "yxz"),
    (1, 768, 768, "xyz"),
    (2, 0, 256, "xzy"),
    (2, 256, 128, "yzx"),
    (3, 0, 512, "yxz"),
    (3, 512, 640, "xyz"),
    (4, 0, 768, "yzx"),
    (4, 768, 768, "xzy"),
    (5, 0, 768, "yxz"),
    (5, 768, 768, "xyz"),
    (6, 0, 256, "xyz"),
    (6, 256, 128, "yxz"),
    (7, 0, 512, "yxz"),
    (7, 512, 640, "xyz"),
)
REDUCE_TABLE = (
    (),
    (),
    (),
    (),
    (),
    (4, 0),
    (12, 8),
    (),
    (),
    (-1, 20, 1, -5, 16, 5),
    (),
    (),
    (-9, 24, -13, 9, -21, 13),
    (-2, 21, -17, 2),
    (),
    (-10, 28, -25, -3, 25, -6, 6, 10, -22, 17, -14, -7),
    (-29, 22, 29, -11, 14),
    (32, -26, 36, -23, -18, 26, -30, 18, -15, 30),
    (44, -27),
    (-33, 40, 33, -37, -19, -31, 37),
    (),
    (48, 52),
    (-45,),
    (-34, 34, -41, 45, -49, 41, -53, 49),
    (-35, 53),
    (-46, 56, 46, -42, 60, -50, -54, -38, 38, 54),
    (-47, 50, -55, 42, -57, 57, -39, -51, -61, 61, -58, 58, -43, -62, 62, -59, -63),
)


def places():
    dp = lax.axis_index("dp")
    y = lax.axis_index("tensor")
    return dp // 4, (dp // 2) % 2, dp % 2, y


def partners(z, x, k, y):
    def at(z_, x_, k_, y_):
        return {"dp": (z_ * 2 + x_) * 2 + k_, "tensor": y_}

    along_z = [at((z + step) % 4, x, k, y) for step in (1, 2, 3)]
    return along_z + [at(z, 1 - x, k, y), at(z, x, k, 1 - y), at(z, x, 1 - k, y)]


def greet(peers):
    barrier = pltpu.get_barrier_semaphore()
    for peer in peers:
        pl.semaphore_signal(barrier, inc=1, device_id=peer, device_id_type=MESH)
    pl.semaphore_wait(barrier, len(peers))


def layer_norm(inputs, gain_row, shift_row):
    centered = inputs - jnp.mean(inputs, axis=-1, keepdims=True)
    variance = jnp.mean(centered * centered, axis=-1, keepdims=True)
    return centered * lax.rsqrt(variance + EPSILON) * gain_row + shift_row


def gelu_exact(values):
    return jax.nn.gelu(values, approximate=False)


def mm(left, right, contract):
    return lax.dot_general(left, right, (contract, ((), ())), preferred_element_type=F32)


def halves(array):
    return jnp.stack(jnp.split(array, 2, axis=1))


def heads(array):
    return array.reshape(array.shape[0], -1, HEAD_DIM).transpose(1, 0, 2)


def flat(array):
    return array.transpose(1, 0, 2).reshape(array.shape[1], -1)


class Chains:
    def __init__(self, table, copies, arrived):
        self.table, self.copies, self.arrived = table, copies, arrived
        self.live, self.spot = {}, 0

    def act(self, code):
        if code >= 0:
            key = divmod(code, 4)
            self.live[key] = self.copies(*key)
            for copy in self.live[key]:
                copy.start()
        else:
            key = divmod(-code - 1, 4)
            for copy in self.live.pop(key):
                copy.wait()
            self.arrived(*key)

    def at(self):
        for code in self.table[self.spot]:
            self.act(code)
        self.spot += 1


def axis_index_of(axis, own, order, count):
    return slice(None) if axis in order[:count] else own


def gather_chains(own, held, send, recv, local, peers, place):
    z, x, k, y = place
    mine = {i: pltpu.make_async_copy(own[i], held[i].at[y, z, x, k], local.at[i]) for i in range(len(held))}
    for copy in mine.values():
        copy.start()

    def copies(c, phase):
        i, first, width, order = GATHER_CHAINS[c]
        b, cols = held[i], pl.ds(first, width)

        def remote(source, target, slot, peer):
            return pltpu.make_async_remote_copy(
                source, target, send.at[c, slot], recv.at[c, slot], device_id=peers[peer], device_id_type=MESH
            )

        if phase == 3:
            ref = b.at[:, :, :, k, :, cols]
            return [remote(ref, ref, 5, 5)]
        at = [axis_index_of(axis, own_at, order, phase) for axis, own_at in (("y", y), ("z", z), ("x", x))]
        target = b.at[(*at, k, slice(None), cols)]
        if phase == 0:
            source = own[i].at[:, cols]
        else:
            if i in mine:
                mine.pop(i).wait()
            source = target
        if order[phase] == "z":
            return [remote(source, target, j, j) for j in range(3)]
        return [remote(source, target, 3, 3) if order[phase] == "x" else remote(source, target, 4, 4)]

    return Chains(GATHER_TABLE, copies, lambda c, phase: None)


def matrix(ref, *lead):
    value = ref[lead] if lead else ref[...]
    return value.reshape(-1, value.shape[-1])


def norm_rows(source, gain_row, shift_row, target):
    def block(t, carry):
        rows = pl.ds(pl.multiple_of(t * 128, 128), 128)
        target[rows, :] = layer_norm(source[rows, :], gain_row, shift_row).astype(BF16)
        return carry

    lax.fori_loop(0, source.shape[0] // 128, block, 0)


def turn_rows(source, target, k):
    for c in range(2):
        turned = source[:, c * 384 : (c + 1) * 384].T
        for j in range(8):
            block = c * 8 + j
            target[(block + k) % 2, block // 4, (block // 2) % 2] = turned[j * 48 : (j + 1) * 48]


def forward_kernel(*refs):
    n = ITEM_COUNT
    it = iter(refs)

    def take(count):
        return [next(it) for _ in range(count)]

    own = take(n)
    tokens, lengths, gain, shift, outb, qvb, upb = take(7)
    whole = take(n)
    saved = [take(9) for _ in range(2)]
    (final,) = take(1)
    held = take(n)
    (stream, middle, normed, turned, turned_mid, project, attended, active, slope, probs, qv_all, up_all) = take(12)
    send, recv, local, out_sem, prob_sem, small_send, small_recv, whole_sem = take(8)
    place = z, x, k, y = places()
    peers = partners(z, x, k, y)
    chains = gather_chains(own, held, send, recv, local, peers, place)
    qv_all[y] = qvb[...]
    up_all[y] = upb[...]
    greet(peers)
    chains.at()
    small = [
        pltpu.make_async_remote_copy(
            ref.at[y], ref.at[y], small_send.at[j], small_recv.at[j], device_id=peers[4], device_id_type=MESH
        )
        for j, ref in enumerate((qv_all, up_all))
    ]
    for copy in small:
        copy.start()
    stream[...] = tokens[...].astype(F32)
    length = lengths[y]
    rows = stream.shape[0]
    outgoing = {}

    def save(layer, slot, ref):
        copy = pltpu.make_async_copy(ref, saved[layer][slot], out_sem.at[layer, slot])
        copy.start()
        outgoing[slot] = copy

    def settle(slot):
        if slot in outgoing:
            outgoing.pop(slot).wait()

    back = []

    def keep_weight(i):
        copy = pltpu.make_async_copy(held[i], whole[i], whole_sem.at[i])
        copy.start()
        back.append(copy)

    everything = (slice(None),) * 4
    for layer in range(2):
        w_qkv, w_out, w_up, w_down = held[4 * layer : 4 * layer + 4]
        chains.at()
        settle(2)
        norm_rows(stream, gain[layer, 0:1], shift[layer, 0:1], normed)
        turn_rows(normed, turned, k)
        save(layer, 0, stream)
        save(layer, 2, turned)
        if layer == 0:
            for copy in small:
                copy.wait()
        settle(4)
        for half in range(2):
            chains.at()
            if half == 0:
                keep_weight(4 * layer)

            def third(t, carry):
                cols = pl.ds(pl.multiple_of(t * 384, 128), 384)
                part = mm(normed[...], matrix(w_qkv, half, *everything, cols), ((1,), (0,)))
                bias = jnp.where(t == 1, 0.0, qv_all[half, layer, pl.ds(t // 2, 1)])
                project[half, :, cols] = (part + bias).astype(BF16)
                return carry

            lax.fori_loop(0, 3, third, 0)
        save(layer, 4, project)
        settle(5)

        def pair(j, carry):
            half = j // 3
            at = (j % 3) * 128
            lane = lax.broadcasted_iota(jnp.int32, (1, 128), 1) < 64
            query = project[half, :, pl.ds(pl.multiple_of(at, 128), 128)]
            key = project[half, :, pl.ds(pl.multiple_of(at + 384, 128), 128)]
            value = project[half, :, pl.ds(pl.multiple_of(at + 768, 128), 128)]
            value_t = value.T
            hidden_key = lax.broadcasted_iota(jnp.int32, (rows, 1), 0) >= length
            both = []
            slot = j % 2
            for h in range(2):
                here = lane if h == 0 else jnp.logical_not(lane)
                some = jnp.where(here, key, jnp.zeros_like(key)) * jnp.asarray(HEAD_DIM**-0.5, BF16)
                scores = mm(some, query, ((1,), (1,)))
                scores = jnp.where(hidden_key, -1e30, scores)
                exponent = jnp.exp(scores - jnp.max(scores, axis=0, keepdims=True))
                prob = (exponent * (1.0 / jnp.sum(exponent, axis=0, keepdims=True))).astype(BF16)
                probs[j, h] = prob
                both.append(mm(value_t[h * 64 : (h + 1) * 64], prob, ((1,), (0,))))
            block = jnp.concatenate(both, axis=0).T
            attended[:, pl.ds(pl.multiple_of(j * 128, 128), 128)] = block.astype(BF16)
            return carry

        settle(6)
        for j0 in range(0, 6, 3):
            chains.at()
            lax.fori_loop(j0, j0 + 3, pair, 0)
        save(layer, 5, attended)
        save(layer, 6, probs)
        chains.at()
        keep_weight(4 * layer + 1)
        settle(1)

        def mix(c, carry):
            cols = pl.ds(pl.multiple_of(c * 384, 128), 384)
            total = stream[:, cols] + outb[layer, 0:1, cols]
            for half in range(2):
                total += mm(attended[:, half * 384 : (half + 1) * 384], matrix(w_out, half, pl.ds(2 * c, 2)), ((1,), (1,)))
            middle[:, cols] = total
            return carry

        lax.fori_loop(0, 2, mix, 0)
        save(layer, 1, middle)
        chains.at()
        settle(3)
        norm_rows(middle, gain[layer, 1:2], shift[layer, 1:2], normed)
        turn_rows(normed, turned_mid, k)
        save(layer, 3, turned_mid)
        settle(7)
        settle(8)

        def unit(t, carry):
            half = t // 3
            cols = pl.ds(pl.multiple_of((t % 3) * 512, 128), 512)
            hidden = mm(normed[...], matrix(w_up, half, *everything, cols), ((1,), (0,)))
            hidden = hidden + up_all[half, layer : layer + 1, cols]
            cdf = 0.5 * (1.0 + lax.erf(hidden * (0.5**0.5)))
            density = jnp.exp(-0.5 * hidden * hidden) * 0.3989422804014327
            active[half, :, cols] = (hidden * cdf).astype(BF16)
            slope[half, :, cols] = (cdf + hidden * density).astype(BF16)
            return carry

        for t0 in range(0, 6, 3):
            chains.at()
            if t0 == 0:
                keep_weight(4 * layer + 2)
            lax.fori_loop(t0, t0 + 3, unit, 0)
        save(layer, 7, active)
        save(layer, 8, slope)
        chains.at()
        keep_weight(4 * layer + 3)
        settle(0)

        def close(c, carry):
            cols = pl.ds(pl.multiple_of(c * 384, 128), 384)
            total = middle[:, cols] + outb[layer, 1:2, cols]
            for half in range(2):
                total += mm(active[half], matrix(w_down, half, pl.ds(2 * c, 2)), ((1,), (1,)))
            stream[:, cols] = total
            return carry

        lax.fori_loop(0, 2, close, 0)
    chains.at()
    final[...] = stream[...].astype(BF16)
    for slot in list(outgoing):
        settle(slot)
    for copy in back:
        copy.wait()


def forward(shards, tokens, lengths, gain, shift, outb, qvb, upb):
    rows, width = tokens.shape
    widths = [s.shape[-1] for s in shards]
    full = [(2, 4, 2, 2, 48, w) for w in widths]
    layer_saves = [
        ((rows, width), F32),
        ((rows, width), F32),
        ((2, 4, 2, 48, rows), BF16),
        ((2, 4, 2, 48, rows), BF16),
        ((2, rows, widths[0]), BF16),
        ((rows, width), BF16),
        ((6, 2, rows, rows), BF16),
        ((2, rows, widths[2]), BF16),
        ((2, rows, widths[2]), BF16),
    ]
    any_spec = pl.BlockSpec(memory_space=pl.ANY)
    vmem_spec = pl.BlockSpec(memory_space=pltpu.VMEM)
    out_shape = (
        [jax.ShapeDtypeStruct(f, BF16) for f in full]
        + [jax.ShapeDtypeStruct(s, t) for s, t in layer_saves * 2]
        + [jax.ShapeDtypeStruct((rows, width), BF16)]
    )
    by_slot = {j: pltpu.VMEM(*layer_saves[j]) for j in range(9)}
    outs = pl.pallas_call(
        forward_kernel,
        out_shape=out_shape,
        in_specs=[any_spec] * ITEM_COUNT + [vmem_spec, pl.BlockSpec(memory_space=pltpu.SMEM)] + [vmem_spec] * 5,
        out_specs=[any_spec] * (ITEM_COUNT + 18) + [vmem_spec],
        scratch_shapes=[pltpu.VMEM(f, BF16) for f in full]
        + [
            by_slot[0],
            by_slot[1],
            pltpu.VMEM((rows, width), BF16),
            by_slot[2],
            by_slot[3],
            by_slot[4],
            by_slot[5],
            by_slot[7],
            by_slot[8],
            by_slot[6],
            pltpu.VMEM((2, *qvb.shape), F32),
            pltpu.VMEM((2, *upb.shape), F32),
            pltpu.SemaphoreType.DMA((len(GATHER_CHAINS), 6)),
            pltpu.SemaphoreType.DMA((len(GATHER_CHAINS), 6)),
            pltpu.SemaphoreType.DMA((ITEM_COUNT,)),
            pltpu.SemaphoreType.DMA((2, 9)),
            pltpu.SemaphoreType.DMA((2,)),
            pltpu.SemaphoreType.DMA((2,)),
            pltpu.SemaphoreType.DMA((2,)),
            pltpu.SemaphoreType.DMA((ITEM_COUNT,)),
        ],
        compiler_params=pltpu.CompilerParams(
            collective_id=0, has_side_effects=True, vmem_limit_bytes=VMEM_LIMIT
        ),
        name="forward",
    )(*shards, tokens, lengths, gain, shift, outb, qvb, upb)
    return outs[:ITEM_COUNT], [outs[ITEM_COUNT + 9 * l : ITEM_COUNT + 9 * l + 9] for l in range(2)], outs[-1]


def norm_back(source, upstream, gain_row, gradient, rounded):
    def block(t, sums):
        rows = pl.ds(pl.multiple_of(t * 64, 64), 64)
        inputs = source[rows, :]
        centered = inputs - jnp.mean(inputs, axis=-1, keepdims=True)
        rate = lax.rsqrt(jnp.mean(centered * centered, axis=-1, keepdims=True) + EPSILON)
        unit = centered * rate
        above = upstream[rows, :]
        pull = above * gain_row
        along = jnp.mean(pull * unit, axis=-1, keepdims=True)
        total = gradient[rows, :] + rate * (pull - jnp.mean(pull, axis=-1, keepdims=True) - unit * along)
        gradient[rows, :] = total
        if rounded is not None:
            rounded[rows, :] = total.astype(BF16)
        return (
            sums[0] + jnp.sum(above * unit, axis=0, keepdims=True),
            sums[1] + jnp.sum(above, axis=0, keepdims=True),
            sums[2] + jnp.sum(total, axis=0, keepdims=True),
        )

    zero = jnp.zeros((1, source.shape[1]), F32)
    return lax.fori_loop(0, source.shape[0] // 64, block, (zero, zero, zero))


def backward_kernel(*refs):
    n = ITEM_COUNT
    it = iter(refs)

    def take(count):
        return [next(it) for _ in range(count)]

    whole = take(n)
    saved = [take(9) for _ in range(2)]
    cotangent, lengths, gain = take(3)
    out_q, out_o, out_u, out_d, token_grad, sums = take(6)
    outs = (out_q, out_o, out_u, out_d)
    (slot_a, slot_b, stream, middle, turned, turned_mid, project, attended, active, slope, probs) = take(11)
    (gradient, upstream, rounded, left, dattended, dproject) = take(6)
    held = take(4)
    (to_core, from_core) = take(2)
    arrivals = [take(3) for _ in REDUCE_CHAINS]
    small_c, small_x, small_y, small_z = take(4)
    (fetch_sem, prob_sem, core_send, core_recv, send, recv, credit, small_send, small_recv, last_sem) = take(10)
    place = z, x, k, y = places()
    peers = partners(z, x, k, y)
    rows = stream.shape[0]

    fetches = {}

    def fetch(name, pairs):
        fetches[name] = [pltpu.make_async_copy(s, t, fetch_sem.at[name, j]) for j, (s, t) in enumerate(pairs)]
        for copy in fetches[name]:
            copy.start()

    def ready(name):
        for copy in fetches.pop(name):
            copy.wait()

    def weights_into(slot, layer, kind):
        w_qkv, w_out, w_up, w_down = whole[4 * layer : 4 * layer + 4]
        if kind == "d":
            return [(w_down, slot)]
        if kind == "u":
            return [(w_up, slot)]
        lead = (slice(None),) * 5
        return [(w_qkv, slot.at[(*lead, pl.ds(0, 1152))]), (w_out, slot.at[(*lead, pl.ds(1152, 384))])]

    SLOT_A, SLOT_B, STREAM, MIDDLE, TURNED, TURNED_MID, PROJECT, ATTENDED, ACTIVE, SLOPE, COT = range(11)
    buffers = {
        STREAM: (stream, 0),
        MIDDLE: (middle, 1),
        TURNED: (turned, 2),
        TURNED_MID: (turned_mid, 3),
        PROJECT: (project, 4),
        ATTENDED: (attended, 5),
        ACTIVE: (active, 7),
        SLOPE: (slope, 8),
    }

    def fetch_saved(name, layer):
        target, index = buffers[name]
        fetch(name, [(saved[layer][index], target)])

    def prob_copy(layer, j):
        return pltpu.make_async_copy(saved[layer][6].at[j], probs.at[j % 2], prob_sem.at[j % 2])

    fetch(COT, [(cotangent, rounded)])
    fetch(SLOT_A, weights_into(slot_a, 1, "d"))
    for name in (SLOPE, ACTIVE):
        fetch_saved(name, 1)
    fetch(SLOT_B, weights_into(slot_b, 1, "u"))
    for name in (TURNED_MID, MIDDLE, ATTENDED, PROJECT, TURNED, STREAM):
        fetch_saved(name, 1)
    prob_copy(1, 0).start()
    slots = {("d", 1): (SLOT_A, slot_a), ("u", 1): (SLOT_B, slot_b), ("q", 1): (SLOT_A, slot_a),
             ("d", 0): (SLOT_B, slot_b), ("u", 0): (SLOT_A, slot_a), ("q", 0): (SLOT_B, slot_b)}
    greet(peers)

    kinds = [(1, 3), (1, 2), (1, 1), (1, 0), (0, 3), (0, 2), (0, 1), (0, 0)]

    def core_copy(r, half):
        width = held[kinds[r][1]].shape[-1]
        at = (half, slice(None), slice(None), slice(None), pl.ds(0, width))
        return pltpu.make_async_remote_copy(
            to_core.at[at], from_core.at[at], core_send.at[r, half], core_recv.at[r, half],
            device_id=peers[5], device_id_type=MESH,
        )

    def take_core(r):
        b = held[kinds[r][1]]
        width = b.shape[-1]
        for half in range(2):
            core_copy(r, half).wait()

        def block(t, carry):
            at = (t // 8, (t // 2) % 4, t % 2)
            b[at] = b[at] + from_core[(*at, slice(None), pl.ds(0, width))]
            return carry

        lax.fori_loop(0, 16, block, 0)
        if r < n - 1:
            for half in range(2):
                pl.semaphore_signal(credit.at[half], inc=1, device_id=peers[5], device_id_type=MESH)

    def rest_of(order, phase):
        return [(axis, size) for axis, size in (("y", 2), ("z", 4), ("x", 2)) if axis in order[phase + 1 :]]

    def copies(c, phase):
        r, first, width, order = REDUCE_CHAINS[c]
        b, cols = held[kinds[r][1]], pl.ds(first, width)
        target = arrivals[c][phase]
        left_over = order[phase + 1 :]

        def block(axis, there):
            at = []
            for name, own_at in (("y", y), ("z", z), ("x", x)):
                at.append(there if name == axis else slice(None) if name in left_over else own_at)
            return b.at[(*at, slice(None), cols)]

        def remote(source, there, slot, peer):
            return pltpu.make_async_remote_copy(
                source, there, send.at[c, slot], recv.at[c, slot], device_id=peers[peer], device_id_type=MESH
            )

        if order[phase] == "z":
            return [remote(block("z", (z + 1 + j) % 4), target.at[j], j, j) for j in range(3)]
        if order[phase] == "x":
            return [remote(block("x", 1 - x), target, 3, 3)]
        return [remote(block("y", 1 - y), target, 4, 4)]

    def arrived(c, phase):
        r, first, width, order = REDUCE_CHAINS[c]
        layer, kind = kinds[r]
        b, cols = held[kind], pl.ds(first, width)
        source = arrivals[c][phase]
        rest = rest_of(order, phase)
        count = 1
        for _, size in rest:
            count *= size

        def total(t):
            at, inner, stride = {}, [], 1
            for axis, size in reversed(rest):
                at[axis] = (t // stride) % size
                stride *= size
            inner = [at[axis] for axis, _ in rest]
            spot = (at.get("y", y), at.get("z", z), at.get("x", x), slice(None), cols)
            value = b[spot].astype(F32)
            if order[phase] == "z":
                for j in range(3):
                    value += source[(j, *inner)].astype(F32)
            else:
                value += source[tuple(inner)].astype(F32) if inner else source[...].astype(F32)
            return spot, value

        if not rest:
            outs[kind][layer, :, cols] = total(0)[1]
        else:

            def block(t, carry):
                spot, value = total(t)
                b[spot] = value.astype(BF16)
                return carry

            lax.fori_loop(0, count, block, 0)

    chains = Chains(REDUCE_TABLE, copies, arrived)

    def weight_gradient(r, lhs, rhs):
        b = held[kinds[r][1]]
        width = b.shape[-1]
        size = 512 if width % 512 == 0 else 384

        def one(half, carry):
            def chunk(t, inner):
                cols = pl.ds(pl.multiple_of(t * size, 128), size)
                value = mm(lhs[...].reshape(768, rows), rhs(half, cols), ((1,), (0,))).astype(BF16)
                b[half, :, :, :, cols] = value[:384].reshape(4, 2, 48, size)
                to_core[half, :, :, :, cols] = value[384:].reshape(4, 2, 48, size)
                return inner

            lax.fori_loop(0, width // size, chunk, 0)
            if r > 0:
                pl.semaphore_wait(credit.at[half], 1)
            core_copy(r, half).start()
            return carry

        lax.fori_loop(0, 2, one, 0)

    chains.at()
    chains.at()
    ready(COT)
    keep = lax.broadcasted_iota(jnp.int32, (rows, 1), 0) < lengths[y]
    gradient[...] = jnp.where(keep, rounded[...].astype(F32), 0.0)
    rounded[...] = gradient[...].astype(BF16)
    everything = (slice(None),) * 4

    def place_at(*taken):
        for r in taken:
            take_core(r)
        chains.at()

    for layer in (1, 0):
        first = 0 if layer == 1 else 4
        place_at()
        sums[layer, 2:3, 768:1536] = jnp.sum(gradient[...], axis=0, keepdims=True)
        turn_rows(rounded, left, k)
        name, w_down = slots["d", layer]
        ready(ACTIVE)
        place_at()
        weight_gradient(first, left, lambda half, cols: active[half, :, cols])
        ready(name)
        ready(SLOPE)
        place_at()

        def unit(t, carry):
            half = t // 3
            cols = pl.ds(pl.multiple_of((t % 3) * 512, 128), 512)
            dact = mm(rounded[...], matrix(w_down, half, *everything, cols), ((1,), (0,)))
            dhidden = (dact * slope[half, :, cols].astype(F32)).astype(BF16)
            slope[half, :, cols] = dhidden
            sums[layer, pl.ds(4 + half, 1), cols] = jnp.sum(dhidden.astype(F32), axis=0, keepdims=True)
            return carry

        lax.fori_loop(0, 6, unit, 0)
        if layer == 1:
            fetch(SLOT_A, weights_into(slot_a, 1, "q"))
            fetch_saved(ACTIVE, 0)
        else:
            fetch(SLOT_B, weights_into(slot_b, 0, "q"))
        name, w_up = slots["u", layer]
        ready(name)
        ready(TURNED_MID)
        place_at(first)
        weight_gradient(first + 1, turned_mid, lambda half, cols: slope[half, :, cols])
        place_at(first + 1)

        def pull_up(c, carry):
            total = mm(slope[0], matrix(w_up, 0, pl.ds(2 * c, 2)), ((1,), (1,)))
            total += mm(slope[1], matrix(w_up, 1, pl.ds(2 * c, 2)), ((1,), (1,)))
            upstream[:, pl.ds(pl.multiple_of(c * 384, 128), 384)] = total
            return carry

        lax.fori_loop(0, 2, pull_up, 0)
        if layer == 1:
            fetch(SLOT_B, weights_into(slot_b, 0, "d"))
            fetch_saved(SLOPE, 0)
            fetch_saved(TURNED_MID, 0)
        ready(MIDDLE)
        place_at()
        gain_sum, shift_sum, bias_sum = norm_back(middle, upstream, gain[layer, 1:2], gradient, rounded)
        sums[layer, 0:1, 768:1536] = gain_sum
        sums[layer, 1:2, 768:1536] = shift_sum
        sums[layer, 2:3, 0:768] = bias_sum
        if layer == 1:
            fetch_saved(MIDDLE, 0)
        name, w_qo = slots["q", layer]
        ready(name)
        ready(ATTENDED)
        place_at()
        turn_rows(rounded, left, k)
        weight_gradient(first + 2, left, lambda half, cols: attended[:, pl.ds(pl.multiple_of(half * 384, 128), 384)])

        def pull_out(half, carry):
            dattended[half] = mm(rounded[...], matrix(w_qo, half, *everything, pl.ds(1152, 384)), ((1,), (0,))).astype(BF16)
            return carry

        lax.fori_loop(0, 2, pull_out, 0)
        if layer == 1:
            fetch_saved(ATTENDED, 0)
        ready(PROJECT)
        scale = HEAD_DIM**-0.5

        def pair(j, carry):
            half = j // 3
            at = (j % 3) * 128
            prob_copy(layer, j).wait()

            @pl.when(j < 5)
            def _():
                prob_copy(layer, j + 1).start()

            lane = lax.broadcasted_iota(jnp.int32, (1, 128), 1) < 64
            columns = [pl.ds(pl.multiple_of(at + t * 384, 128), 128) for t in range(3)]
            query, key, value = (project[half, :, c] for c in columns)
            above = dattended[half, :, columns[0]]
            key_t = key.T
            dkeys, dvalues, dqueries = [], [], []
            for h in range(2):
                here = lane if h == 0 else jnp.logical_not(lane)
                prob = probs[j % 2, h]
                dprob = mm(jnp.where(here, value, jnp.zeros_like(value)), above, ((1,), (1,)))
                prob32 = prob.astype(F32)
                both = prob32 * dprob
                dscore = (both - prob32 * jnp.sum(both, axis=0, keepdims=True)).astype(BF16)
                dvalues.append(mm(prob, above, ((1,), (0,))))
                dkeys.append(mm(dscore, query, ((1,), (0,))))
                dqueries.append(mm(key_t[h * 64 : (h + 1) * 64], dscore, ((1,), (0,))))
            dproject[half, :, columns[0]] = (jnp.concatenate(dqueries, axis=0) * scale).T.astype(BF16)
            dproject[half, :, columns[1]] = (jnp.where(lane, dkeys[0], dkeys[1]) * scale).astype(BF16)
            dproject[half, :, columns[2]] = jnp.where(lane, dvalues[0], dvalues[1]).astype(BF16)
            return carry

        place_at(first + 2)
        lax.fori_loop(0, 3, pair, 0)
        place_at()
        lax.fori_loop(3, 6, pair, 0)
        if layer == 1:
            fetch_saved(PROJECT, 0)
            prob_copy(0, 0).start()
        ready(TURNED)
        place_at()
        for half in range(2):
            for t in (0, 2):
                sums[layer, 3:4, (t // 2) * 768 + half * 384 : (t // 2) * 768 + half * 384 + 384] = jnp.sum(
                    dproject[half, :, t * 384 : (t + 1) * 384].astype(F32), axis=0, keepdims=True
                )
        weight_gradient(first + 3, turned, lambda half, cols: dproject[half, :, cols])
        place_at(first + 3)

        def pull_qkv(c, carry):
            rest = (slice(None),) * 3
            total = mm(dproject[0], matrix(w_qo, 0, pl.ds(2 * c, 2), *rest, pl.ds(0, 1152)), ((1,), (1,)))
            total += mm(dproject[1], matrix(w_qo, 1, pl.ds(2 * c, 2), *rest, pl.ds(0, 1152)), ((1,), (1,)))
            upstream[:, pl.ds(pl.multiple_of(c * 384, 128), 384)] = total
            return carry

        lax.fori_loop(0, 2, pull_qkv, 0)
        if layer == 1:
            fetch(SLOT_A, weights_into(slot_a, 0, "u"))
            fetch_saved(TURNED, 0)
        ready(STREAM)
        place_at()
        gain_sum, shift_sum, _ = norm_back(stream, upstream, gain[layer, 0:1], gradient, rounded if layer == 1 else None)
        sums[layer, 0:1, 0:768] = gain_sum
        sums[layer, 1:2, 0:768] = shift_sum
        if layer == 1:
            fetch_saved(STREAM, 0)
    last = pltpu.make_async_copy(gradient, token_grad, last_sem)
    last.start()

    sums[:, 6:8, :] = jnp.zeros((2, 2, 1536), F32)

    def exchange(slot, target, peer):
        copy = pltpu.make_async_remote_copy(
            sums, target, small_send.at[slot], small_recv.at[slot], device_id=peers[peer], device_id_type=MESH
        )
        copy.start()
        return copy

    tail = chains.table[chains.spot]
    parts = [tail[len(tail) * j // 4 : len(tail) * (j + 1) // 4] for j in range(4)]
    for slot, (target, peer) in enumerate(((small_c, 5), (small_x, 3), (small_y, 4))):
        copy = exchange(slot, target, peer)
        for code in parts[slot]:
            chains.act(code)
        copy.wait()
        sums[...] += target[...]
    small_z[z] = sums[...]
    across = [exchange(3 + j, small_z.at[z], j) for j in range(3)]
    for code in parts[3]:
        chains.act(code)
    for copy in across:
        copy.wait()
    sums[...] = (small_z[0] + small_z[1]) + (small_z[2] + small_z[3])
    last.wait()


def backward(whole, saved, cotangent, lengths, gain):
    rows, width = cotangent.shape
    widths = [w.shape[-1] for w in whole[:4]]
    any_spec = pl.BlockSpec(memory_space=pl.ANY)
    vmem_spec = pl.BlockSpec(memory_space=pltpu.VMEM)

    def blocks(*lead):
        return [pltpu.VMEM((*lead, 48, w), BF16) for w in widths]

    def arrival_shapes():
        sizes, shapes = {"y": 2, "z": 4, "x": 2}, []
        for _, _, columns, order in REDUCE_CHAINS:
            for phase in range(3):
                lead = [3] if order[phase] == "z" else []
                lead += [sizes[axis] for axis in "yzx" if axis in order[phase + 1 :]]
                shapes.append(pltpu.VMEM((*lead, 48, columns), BF16))
        return shapes

    wide = widths[2]
    small = (2, 8, wide)
    outs = pl.pallas_call(
        backward_kernel,
        out_shape=[jax.ShapeDtypeStruct((2, 48, w), F32) for w in widths]
        + [jax.ShapeDtypeStruct((rows, width), F32), jax.ShapeDtypeStruct(small, F32)],
        in_specs=[any_spec] * (ITEM_COUNT + 18 + 1) + [pl.BlockSpec(memory_space=pltpu.SMEM), vmem_spec],
        out_specs=[vmem_spec] * 4 + [any_spec, vmem_spec],
        scratch_shapes=[
            pltpu.VMEM((2, 4, 2, 2, 48, wide), BF16),
            pltpu.VMEM((2, 4, 2, 2, 48, wide), BF16),
            pltpu.VMEM((rows, width), F32),
            pltpu.VMEM((rows, width), F32),
            pltpu.VMEM((2, 4, 2, 48, rows), BF16),
            pltpu.VMEM((2, 4, 2, 48, rows), BF16),
            pltpu.VMEM((2, rows, widths[0]), BF16),
            pltpu.VMEM((rows, width), BF16),
            pltpu.VMEM((2, rows, wide), BF16),
            pltpu.VMEM((2, rows, wide), BF16),
            pltpu.VMEM((2, 2, rows, rows), BF16),
            pltpu.VMEM((rows, width), F32),
            pltpu.VMEM((rows, width), F32),
            pltpu.VMEM((rows, width), BF16),
            pltpu.VMEM((2, 4, 2, 48, rows), BF16),
            pltpu.VMEM((2, rows, width // 2), BF16),
            pltpu.VMEM((2, rows, widths[0]), BF16),
        ]
        + blocks(2, 4, 2)
        + [pltpu.VMEM((2, 4, 2, 48, wide), BF16), pltpu.VMEM((2, 4, 2, 48, wide), BF16)]
        + arrival_shapes()
        + [pltpu.VMEM(small, F32)] * 3
        + [pltpu.VMEM((4, *small), F32)]
        + [
            pltpu.SemaphoreType.DMA((11, 2)),
            pltpu.SemaphoreType.DMA((2,)),
            pltpu.SemaphoreType.DMA((ITEM_COUNT, 2)),
            pltpu.SemaphoreType.DMA((ITEM_COUNT, 2)),
            pltpu.SemaphoreType.DMA((len(REDUCE_CHAINS), 5)),
            pltpu.SemaphoreType.DMA((len(REDUCE_CHAINS), 5)),
            pltpu.SemaphoreType.REGULAR((2,)),
            pltpu.SemaphoreType.DMA((6,)),
            pltpu.SemaphoreType.DMA((6,)),
            pltpu.SemaphoreType.DMA,
        ],
        compiler_params=pltpu.CompilerParams(
            collective_id=1, has_side_effects=True, vmem_limit_bytes=63 * 2**20
        ),
        name="backward",
    )(*whole, *saved[0], *saved[1], cotangent, lengths, gain)
    return outs


def generic_body(dp_size, tokens, lengths, cotangent, norm_gain, norm_shift, qkv_weight, qv_bias,
         out_weight, up_weight, up_bias, down_weight, out_bias):
    part = lax.axis_index("tensor")
    layers = norm_gain.shape[0]
    rows, width = tokens.shape
    length = lax.dynamic_index_in_dim(lengths, part, keepdims=False)
    keep = jnp.arange(rows, dtype=jnp.int32) < length
    own = qkv_weight.shape[1]
    shards = []
    for layer in range(layers):
        shards += [
            qkv_weight[layer].reshape(own, -1),
            out_weight[layer].T,
            up_weight[layer],
            down_weight[layer].T,
        ]
    if False:
        full = [w.reshape(2, width, -1) for w in gather_weights(shards)]
    else:
        full = [
            lax.all_gather(s, ("tensor", "dp"), axis=0).reshape(2, width, -1) for s in shards
        ]
    qv_all = lax.all_gather(qv_bias, "tensor", axis=0)
    upb_all = lax.all_gather(up_bias, "tensor", axis=0)
    scale = HEAD_DIM**-0.5
    stream = tokens.astype(F32)
    saved = []
    for layer in range(layers):
        w_qkv, w_out, w_up, w_down = full[4 * layer : 4 * layer + 4]
        normed = layer_norm(stream, norm_gain[layer, 0], norm_shift[layer, 0]).astype(BF16)
        project = []
        for t in range(2):
            b = jnp.concatenate([qv_all[t, layer, 0], jnp.zeros_like(qv_all[t, layer, 0]), qv_all[t, layer, 1]])
            project.append((mm(normed, w_qkv[t], ((1,), (0,))) + b).astype(BF16))
        third = width // 2
        q, key, val = (
            heads(jnp.concatenate([project[t][:, j * third : (j + 1) * third] for t in range(2)], axis=1))
            for j in range(3)
        )
        scores = jnp.einsum("hqd,hkd->hqk", q, key, preferred_element_type=F32) * scale
        scores = jnp.where(keep[None, None, :], scores, -1e30)
        highest = jnp.max(scores, axis=-1, keepdims=True)
        exponent = jnp.exp(scores - highest)
        probs32 = exponent / jnp.sum(exponent, axis=-1, keepdims=True)
        probs = probs32.astype(BF16)
        attended = flat(jnp.einsum("hqk,hkd->hqd", probs, val, preferred_element_type=F32)).astype(BF16)
        branch = sum(mm(attended[:, t * third : (t + 1) * third], w_out[t], ((1,), (1,))) for t in range(2))
        middle = stream + branch + out_bias[layer, 0]
        normed_mid = layer_norm(middle, norm_gain[layer, 1], norm_shift[layer, 1]).astype(BF16)
        hidden = [mm(normed_mid, w_up[t], ((1,), (0,))) + upb_all[t, layer] for t in range(2)]
        activated = [gelu_exact(h).astype(BF16) for h in hidden]
        branch_mlp = sum(mm(activated[t], w_down[t], ((1,), (1,))) for t in range(2))
        saved.append((stream, middle, normed, q, key, val, probs, attended, normed_mid, hidden, activated))
        stream = middle + branch_mlp + out_bias[layer, 1]
    final = stream.astype(BF16)
    gradient = cotangent.astype(F32) * keep.astype(F32)[:, None]
    grads = [None] * (4 * layers)
    gain, shift, outb, qvb, upb = ([None] * layers for _ in range(5))
    for layer in reversed(range(layers)):
        stream_in, middle, normed, q, key, val, probs, attended, normed_mid, hidden, activated = saved[layer]
        w_qkv, w_out, w_up, w_down = full[4 * layer : 4 * layer + 4]
        third = width // 2
        bias_late = jnp.sum(gradient, axis=0)
        dout = gradient.astype(BF16)
        grads[4 * layer + 3] = jnp.stack([mm(dout, activated[t], ((0,), (0,))).astype(BF16) for t in range(2)])
        dhidden = []
        for t in range(2):
            dact = mm(dout, w_down[t], ((1,), (0,)))
            dhidden.append(jax.vjp(gelu_exact, hidden[t])[1](dact)[0].astype(BF16))
        upb[layer] = jnp.stack([jnp.sum(d.astype(F32), axis=0) for d in dhidden])
        grads[4 * layer + 2] = jnp.stack([mm(normed_mid, d, ((0,), (0,))).astype(BF16) for d in dhidden])
        dnormed_mid = sum(mm(dhidden[t], w_up[t], ((1,), (1,))) for t in range(2))
        pull = jax.vjp(layer_norm, middle, norm_gain[layer, 1], norm_shift[layer, 1])[1]
        dmid, gain_late, shift_late = pull(dnormed_mid)
        dmiddle = gradient + dmid
        bias_early = jnp.sum(dmiddle, axis=0)
        dbranch = dmiddle.astype(BF16)
        dout_t = mm(dbranch, attended, ((0,), (0,))).astype(BF16)
        grads[4 * layer + 1] = halves(dout_t)
        dattended = heads(jnp.concatenate([mm(dbranch, w_out[t], ((1,), (0,))) for t in range(2)], axis=1).astype(BF16))
        p = probs.astype(F32)
        dval = jnp.einsum("hqk,hqd->hkd", probs, dattended, preferred_element_type=F32)
        dprobs = jnp.einsum("hqd,hkd->hqk", dattended, val, preferred_element_type=F32)
        dscores = (p * (dprobs - jnp.sum(p * dprobs, axis=-1, keepdims=True))).astype(BF16)
        dquery = jnp.einsum("hqk,hkd->hqd", dscores, key, preferred_element_type=F32) * scale
        dkey = jnp.einsum("hqk,hqd->hkd", dscores, q, preferred_element_type=F32) * scale
        parts = [flat(a).astype(BF16) for a in (dquery, dkey, dval)]
        dproject = [
            jnp.concatenate([a[:, t * third : (t + 1) * third] for a in parts], axis=1) for t in range(2)
        ]
        qvb[layer] = jnp.stack([jnp.sum(parts[0].astype(F32), axis=0), jnp.sum(parts[2].astype(F32), axis=0)])
        grads[4 * layer] = jnp.stack([mm(normed, d, ((0,), (0,))).astype(BF16) for d in dproject])
        dnormed = sum(mm(dproject[t], w_qkv[t], ((1,), (1,))) for t in range(2))
        pull = jax.vjp(layer_norm, stream_in, norm_gain[layer, 0], norm_shift[layer, 0])[1]
        dfirst, gain_early, shift_early = pull(dnormed)
        gradient = dmiddle + dfirst
        gain[layer] = jnp.stack([gain_early, gain_late])
        shift[layer] = jnp.stack([shift_early, shift_late])
        outb[layer] = jnp.stack([bias_early, bias_late])
    if False:
        reduced = reduce_gradients([g.reshape(2, 4, 2, 2, 48, -1) for g in grads])
    else:
        reduced = [
            lax.psum_scatter(
                g.reshape(2 * dp_size, own, -1).astype(F32), ("tensor", "dp"), scatter_dimension=0
            )
            for g in grads
        ]
    g_gain, g_shift, g_outb, g_qvb, g_upb = lax.psum(
        (jnp.stack(gain), jnp.stack(shift), jnp.stack(outb), jnp.stack(qvb), jnp.stack(upb)),
        ("dp", "tensor"),
    )
    g_qvb = lax.dynamic_slice_in_dim(g_qvb, part * qv_bias.shape[2], qv_bias.shape[2], axis=2)
    g_upb = lax.dynamic_index_in_dim(g_upb, part, axis=1, keepdims=False)
    g_qkv = jnp.stack([reduced[4 * l].reshape(own, 3, -1) for l in range(layers)])
    g_out = jnp.stack([reduced[4 * l + 1].T for l in range(layers)])
    g_up = jnp.stack([reduced[4 * l + 2] for l in range(layers)])
    g_down = jnp.stack([reduced[4 * l + 3].T for l in range(layers)])
    return (final, gradient, g_gain, g_shift, g_qkv, g_qvb, g_out, g_up, g_upb, g_down, g_outb)


def fused_body(tokens, lengths, cotangent, norm_gain, norm_shift, qkv_weight, qv_bias, out_weight, up_weight,
               up_bias, down_weight, out_bias):
    part = lax.axis_index("tensor")
    layers = norm_gain.shape[0]
    rows, width = tokens.shape
    third = width // 2
    own = qkv_weight.shape[1]
    shards = []
    for layer in range(layers):
        shards += [
            qkv_weight[layer].reshape(own, -1),
            out_weight[layer].T,
            up_weight[layer],
            down_weight[layer].T,
        ]
    full, saved, final = forward(shards, tokens, lengths, norm_gain, norm_shift, out_bias, qv_bias, up_bias)
    g_qkv, g_out, g_up, g_down, token_grad, small = backward(full, saved, cotangent, lengths, norm_gain)
    g_gain, g_shift, g_outb, g_qvb = (small[:, j].reshape(layers, 2, width) for j in range(4))
    g_upb = lax.dynamic_index_in_dim(small, 4 + part, axis=1, keepdims=False)
    g_qvb = lax.dynamic_slice_in_dim(g_qvb, part * third, third, axis=2)
    return (
        final,
        token_grad,
        g_gain,
        g_shift,
        g_qkv.reshape(layers, own, 3, third),
        g_qvb,
        g_out.transpose(0, 2, 1),
        g_up,
        g_upb,
        g_down.transpose(0, 2, 1),
        g_outb,
    )


def solution(mesh):
    use_kernels = mesh.shape["dp"] == 16 and mesh.shape["tensor"] == 2
    return jax.shard_map(
        fused_body if use_kernels else functools.partial(generic_body, mesh.shape["dp"]),
        mesh=mesh,
        in_specs=(
            P(("dp", "tensor"), None),
            P("dp"),
            P(("dp", "tensor"), None),
            P(),
            P(),
            P(None, "dp", None, "tensor"),
            P(None, None, "tensor"),
            P(None, "tensor", "dp"),
            P(None, "dp", "tensor"),
            P(None, "tensor"),
            P(None, "tensor", "dp"),
            P(),
        ),
        out_specs=(
            P(("dp", "tensor"), None),
            P(("dp", "tensor"), None),
            P(),
            P(),
            P(None, "dp", None, "tensor"),
            P(None, None, "tensor"),
            P(None, "tensor", "dp"),
            P(None, "dp", "tensor"),
            P(None, "tensor"),
            P(None, "tensor", "dp"),
            P(),
        ),
        check_vma=False,
    )
```

```python
import functools

import jax
import jax.numpy as jnp
from jax import lax
from jax.experimental import pallas as pl
from jax.experimental.pallas import tpu as pltpu
from jax.sharding import PartitionSpec as P

HEAD_DIM = 64
EPSILON = 1e-06
MESH = pl.DeviceIdType.MESH
VMEM_LIMIT = 60 * 2**20
BF16 = jnp.bfloat16
F32 = jnp.float32
ITEM_COUNT = 8
GATHER_CHAINS = (
    (0, 0, 256, "zxy"),
    (0, 256, 256, "zyx"),
    (0, 512, 384, "zxy"),
    (0, 896, 256, "zyx"),
    (1, 0, 256, "zyx"),
    (1, 256, 128, "zxy"),
    (2, 0, 384, "zxy"),
    (2, 384, 384, "zyx"),
    (2, 768, 384, "zxy"),
    (2, 1152, 384, "zyx"),
    (3, 0, 384, "xzy"),
    (3, 384, 384, "yzx"),
    (3, 768, 384, "xzy"),
    (3, 1152, 384, "yzx"),
    (4, 0, 256, "zxy"),
    (4, 256, 256, "zyx"),
    (4, 512, 384, "zxy"),
    (4, 896, 256, "zyx"),
    (5, 0, 256, "yzx"),
    (5, 256, 128, "xzy"),
    (6, 0, 384, "zxy"),
    (6, 384, 384, "zyx"),
    (6, 768, 384, "xzy"),
    (6, 1152, 384, "yzx"),
    (7, 0, 384, "zxy"),
    (7, 384, 384, "zyx"),
    (7, 768, 384, "xzy"),
    (7, 1152, 384, "yzx"),
)
GATHER_TABLE = (
    (80, 96, 152, 88, 104, 144, 8, 24, 0),
    (),
    (-81, 176, -89, 184, -97, 208, -105, 216, -153, -9, 16, -145, 9, -25, 32, -177, -185, 25, -209, -217, -1, 1, 40, -10, 10, -17, 17, 48, -26, -2, 26, 2, -33, 33, 72, -41, 64, -11, 41, 11, -49, 56, -3, 3, -12, -18, 49, 18, -73, 73, 81, -34, -4, -65, 89, -27, 34, 27, -42, 65, 42, -28, -57, 97, -50, -19, 50, 19, -20, -74, 74, 57),
    (-35, 35, -82, 105, -43, 82, 43),
    (-66, -36, -44),
    (-90, 90, 112, -51, 66, 51, -75, 75),
    (-58, 58, -52, -76, -98, 98, 120),
    (-83, 83, -91, 91),
    (-84, -106, 106, 128, -92, -113, 113, 136, -67, 67, -59, 59, -121, 121, 153, -68, -60, -129, 129, 145),
    (-137, 137, 160, -99, 99, -107, 107, -154, 154, 168, -122, 122, -114, 114),
    (-100, -108, -138, 138, -130, 130, -146, 146, 177, -155, 155),
    (-161, 185, -156, -123, 161, 123, -115, 115, -169, 169, 192),
    (-124, -139, 139, -116, -131, 131, -140, -147, 147, -178, 178, 200, -132, -170, 170, -148, -162, 162),
    (),
    (-186, 186, 209),
    (-179, 179, -193, 193, 217, -171, 171, -201, 201),
    (-163, 163, -180, -172, -187, 187, -202, 202, -210, 210),
    (-194, 194, -164, -188),
    (),
    (-218, 218, -203, 203, -211, 211),
    (-204, -212),
    (-195, 195, -219, 219),
    (-196, -220),
)


REDUCE_CHAINS = (
    (0, 0, 768, "yxz"),
    (0, 768, 768, "xyz"),
    (1, 0, 768, "yxz"),
    (1, 768, 768, "xyz"),
    (2, 0, 256, "xyz"),
    (2, 256, 128, "yxz"),
    (3, 0, 512, "yxz"),
    (3, 512, 640, "xyz"),
    (4, 0, 768, "yzx"),
    (4, 768, 768, "xzy"),
    (5, 0, 768, "yxz"),
    (5, 768, 768, "xyz"),
    (6, 0, 256, "xyz"),
    (6, 256, 128, "yxz"),
    (7, 0, 512, "yxz"),
    (7, 512, 640, "xyz"),
)
REDUCE_TABLE = (
    (),
    (8, 0),
    (),
    (),
    (),
    (24, 16, -1, 1, -9, 9),
    (),
    (),
    (32, 40),
    (-17, -25, 17, 25),
    (-2, 2, -10, 10, -41, 41, -33, 33),
    (56, 48, -26, 26),
    (-18, -34, -42, -3, 42),
    (-11, 18),
    (-49, 49),
    (-57, 57, -27, 34),
    (72, 64, -43, -50, 50, -58, -19, 58),
    (88, 80, -35, -51),
    (-59, -65, 65, -73, 73),
    (),
    (96, 104),
    (-81, 81, -89, 89),
    (-105, 105, -66, -97, 66, 97),
    (112, 128, -90, 90, -82, 120, 82, -98, -106, -129, 129),
    (-67, -74, 74, 98),
    (136, -113, 113, -91, 106, -75, -137, -121, 137, 121, -130, 130, -83, -114, 114, -138, 138, -99, -122, 122, -107, -131, 131, -139, -115, 139, -123, -132, 132, -140, -133),
)


def places():
    dp = lax.axis_index("dp")
    y = lax.axis_index("tensor")
    return dp // 4, (dp // 2) % 2, dp % 2, y


def partners(z, x, k, y):
    def at(z_, x_, k_, y_):
        return {"dp": (z_ * 2 + x_) * 2 + k_, "tensor": y_}

    along_z = [at((z + step) % 4, x, k, y) for step in (1, 2, 3)]
    return along_z + [at(z, 1 - x, k, y), at(z, x, k, 1 - y), at(z, x, 1 - k, y)]


def greet(peers):
    barrier = pltpu.get_barrier_semaphore()
    for peer in peers:
        pl.semaphore_signal(barrier, inc=1, device_id=peer, device_id_type=MESH)
    pl.semaphore_wait(barrier, len(peers))


def layer_norm(inputs, gain_row, shift_row):
    centered = inputs - jnp.mean(inputs, axis=-1, keepdims=True)
    variance = jnp.mean(centered * centered, axis=-1, keepdims=True)
    return centered * lax.rsqrt(variance + EPSILON) * gain_row + shift_row


def gelu_exact(values):
    return jax.nn.gelu(values, approximate=False)


def mm(left, right, contract):
    return lax.dot_general(left, right, (contract, ((), ())), preferred_element_type=F32)


def halves(array):
    return jnp.stack(jnp.split(array, 2, axis=1))


def heads(array):
    return array.reshape(array.shape[0], -1, HEAD_DIM).transpose(1, 0, 2)


def flat(array):
    return array.transpose(1, 0, 2).reshape(array.shape[1], -1)


class Chains:
    def __init__(self, table, copies, arrived):
        self.table, self.copies, self.arrived = table, copies, arrived
        self.live, self.spot = {}, 0

    def act(self, code):
        if code >= 0:
            key = divmod(code, 8)
            self.live[key] = self.copies(*key)
            for copy in self.live[key]:
                copy.start()
        else:
            key = divmod(-code - 1, 8)
            for copy in self.live.pop(key):
                copy.wait()
            self.arrived(*key)

    def at(self):
        for code in self.table[self.spot]:
            self.act(code)
        self.spot += 1


def axis_index_of(axis, own, order, count):
    return slice(None) if axis in order[:count] else own


def gather_chains(shards, held, send, recv, local, peers, place):
    z, x, k, y = place
    mine = {}
    for layer in range(2):
        for kind in range(4):
            i = 4 * layer + kind
            target = held[i].at[y, z, x, k]
            if kind == 0:
                mine[i] = [
                    pltpu.make_async_copy(shards[0].at[layer, t], target.at[:, pl.ds(t * 384, 384)], local.at[i, t])
                    for t in range(3)
                ]
            else:
                mine[i] = [pltpu.make_async_copy(shards[kind].at[layer], target, local.at[i, 0])]
            for copy in mine[i]:
                copy.start()

    def put(i):
        for copy in mine.pop(i, ()):
            copy.wait()

    def copies(c, phase):
        i, first, width, order = GATHER_CHAINS[c]
        b, cols = held[i], pl.ds(first, width)
        put(i)

        def remote(source, target, slot, peer):
            return pltpu.make_async_remote_copy(
                source, target, send.at[c, slot], recv.at[c, slot], device_id=peers[peer], device_id_type=MESH
            )

        if phase == 3:
            ref = b.at[:, :, :, k, :, cols]
            return [remote(ref, ref, 5, 5)]
        at = [axis_index_of(axis, own_at, order, phase) for axis, own_at in (("y", y), ("z", z), ("x", x))]
        target = b.at[(*at, k, slice(None), cols)]
        if order[phase] == "z":
            return [remote(target, target, j, j) for j in range(3)]
        return [remote(target, target, 3, 3) if order[phase] == "x" else remote(target, target, 4, 4)]

    return Chains(GATHER_TABLE, copies, lambda c, phase: None)


def matrix(ref, *lead):
    value = ref[lead] if lead else ref[...]
    return value.reshape(-1, value.shape[-1])


def norm_rows(source, gain_row, shift_row, target):
    def block(t, carry):
        rows = pl.ds(pl.multiple_of(t * 128, 128), 128)
        target[rows, :] = layer_norm(source[rows, :], gain_row, shift_row).astype(BF16)
        return carry

    lax.fori_loop(0, source.shape[0] // 128, block, 0)


def turn_rows(source, target, k):
    for c in range(2):
        turned = source[:, c * 384 : (c + 1) * 384].T
        for j in range(8):
            block = c * 8 + j
            target[(block + k) % 2, block // 4, (block // 2) % 2] = turned[j * 48 : (j + 1) * 48]


def forward_kernel(*refs):
    n = ITEM_COUNT
    it = iter(refs)

    def take(count):
        return [next(it) for _ in range(count)]

    shards = take(4)
    tokens, cotangent, lengths, gain, shift, outb, qvb, upb = take(8)
    whole = take(n)
    saved = [take(9) for _ in range(2)]
    (first_grad,) = take(1)
    held = take(n)
    (stream, middle, normed, turned, turned_mid, project, attended, active, slope, probs, qv_all, up_all) = take(12)
    (grad, to_core, from_core) = take(3)
    send, recv, local, out_sem, core_send, core_recv, small_send, small_recv, whole_sem, grad_sem = take(10)
    place = z, x, k, y = places()
    peers = partners(z, x, k, y)
    chains = gather_chains(shards, held, send, recv, local, peers, place)
    qv_all[y] = qvb[...]
    up_all[y] = upb[...]
    greet(peers)
    chains.at()
    small = [
        pltpu.make_async_remote_copy(
            ref.at[y], ref.at[y], small_send.at[j], small_recv.at[j], device_id=peers[4], device_id_type=MESH
        )
        for j, ref in enumerate((qv_all, up_all))
    ]
    for copy in small:
        copy.start()
    stream[...] = tokens[...].astype(F32)
    length = lengths[y]
    rows = stream.shape[0]
    outgoing = {}

    def save(layer, slot, ref):
        copy = pltpu.make_async_copy(ref, saved[layer][slot], out_sem.at[layer, slot])
        copy.start()
        outgoing[slot] = copy

    def settle(slot):
        if slot in outgoing:
            outgoing.pop(slot).wait()

    back = []

    def keep_weight(i):
        copy = pltpu.make_async_copy(held[i], whole[i], whole_sem.at[i])
        copy.start()
        back.append(copy)

    everything = (slice(None),) * 4
    for layer in range(2):
        w_qkv, w_out, w_up, w_down = held[4 * layer : 4 * layer + 4]
        chains.at()
        settle(2)
        norm_rows(stream, gain[layer, 0:1], shift[layer, 0:1], normed)
        turn_rows(normed, turned, k)
        save(layer, 0, stream)
        save(layer, 2, turned)
        if layer == 0:
            for copy in small:
                copy.wait()
        settle(4)
        for half in range(2):
            chains.at()
            if half == 0:
                keep_weight(4 * layer)

            def third(t, carry):
                cols = pl.ds(pl.multiple_of(t * 384, 128), 384)
                part = mm(normed[...], matrix(w_qkv, half, *everything, cols), ((1,), (0,)))
                bias = jnp.where(t == 1, 0.0, qv_all[half, layer, pl.ds(t // 2, 1)])
                project[half, :, cols] = (part + bias).astype(BF16)
                return carry

            lax.fori_loop(0, 3, third, 0)
        save(layer, 4, project)
        settle(5)

        def pair(j, carry):
            half = j // 3
            at = (j % 3) * 128
            lane = lax.broadcasted_iota(jnp.int32, (1, 128), 1) < 64
            query = project[half, :, pl.ds(pl.multiple_of(at, 128), 128)]
            key = project[half, :, pl.ds(pl.multiple_of(at + 384, 128), 128)]
            value = project[half, :, pl.ds(pl.multiple_of(at + 768, 128), 128)]
            value_t = value.T
            hidden_key = lax.broadcasted_iota(jnp.int32, (rows, 1), 0) >= length
            both = []
            slot = j % 2
            for h in range(2):
                here = lane if h == 0 else jnp.logical_not(lane)
                some = jnp.where(here, key, jnp.zeros_like(key)) * jnp.asarray(HEAD_DIM**-0.5, BF16)
                scores = mm(some, query, ((1,), (1,)))
                scores = jnp.where(hidden_key, -1e30, scores)
                exponent = jnp.exp(scores - jnp.max(scores, axis=0, keepdims=True))
                prob = (exponent * (1.0 / jnp.sum(exponent, axis=0, keepdims=True))).astype(BF16)
                probs[j, h] = prob
                both.append(mm(value_t[h * 64 : (h + 1) * 64], prob, ((1,), (0,))))
            block = jnp.concatenate(both, axis=0).T
            attended[:, pl.ds(pl.multiple_of(j * 128, 128), 128)] = block.astype(BF16)
            return carry

        settle(6)
        for j0 in range(0, 6, 3):
            chains.at()
            lax.fori_loop(j0, j0 + 3, pair, 0)
        save(layer, 5, attended)
        save(layer, 6, probs)
        chains.at()
        keep_weight(4 * layer + 1)
        settle(1)

        def mix(c, carry):
            cols = pl.ds(pl.multiple_of(c * 384, 128), 384)
            total = stream[:, cols] + outb[layer, 0:1, cols]
            for half in range(2):
                total += mm(attended[:, half * 384 : (half + 1) * 384], matrix(w_out, half, pl.ds(2 * c, 2)), ((1,), (1,)))
            middle[:, cols] = total
            return carry

        lax.fori_loop(0, 2, mix, 0)
        save(layer, 1, middle)
        chains.at()
        settle(3)
        norm_rows(middle, gain[layer, 1:2], shift[layer, 1:2], normed)
        turn_rows(normed, turned_mid, k)
        save(layer, 3, turned_mid)
        settle(7)
        settle(8)

        def unit(t, carry):
            half = t // 3
            cols = pl.ds(pl.multiple_of((t % 3) * 512, 128), 512)
            hidden = mm(normed[...], matrix(w_up, half, *everything, cols), ((1,), (0,)))
            hidden = hidden + up_all[half, layer : layer + 1, cols]
            cdf = 0.5 * (1.0 + lax.erf(hidden * (0.5**0.5)))
            density = jnp.exp(-0.5 * hidden * hidden) * 0.3989422804014327
            active[half, :, cols] = (hidden * cdf).astype(BF16)
            slope[half, :, cols] = (cdf + hidden * density).astype(BF16)
            return carry

        for t0 in range(0, 6, 3):
            chains.at()
            if t0 == 0:
                keep_weight(4 * layer + 2)
            lax.fori_loop(t0, t0 + 3, unit, 0)
        save(layer, 7, active)
        save(layer, 8, slope)
        chains.at()
        if layer == 1:
            break
        keep_weight(3)
        settle(0)

        def close(c, carry):
            cols = pl.ds(pl.multiple_of(c * 384, 128), 384)
            total = middle[:, cols] + outb[layer, 1:2, cols]
            for half in range(2):
                total += mm(active[half], matrix(w_down, half, pl.ds(2 * c, 2)), ((1,), (1,)))
            stream[:, cols] = total
            return carry

        lax.fori_loop(0, 2, close, 0)

    keep = lax.broadcasted_iota(jnp.int32, (rows, 1), 0) < length
    normed[...] = jnp.where(keep, cotangent[...], jnp.zeros_like(cotangent[...]))
    settle(2)
    turn_rows(normed, turned, k)
    def across(half):
        return pltpu.make_async_remote_copy(
            to_core.at[half], from_core.at[half], core_send.at[half], core_recv.at[half],
            device_id=peers[5], device_id_type=MESH,
        )

    def first_half(half, carry):
        def chunk(t, inner):
            cols = pl.ds(pl.multiple_of(t * 512, 128), 512)
            value = mm(turned[...].reshape(768, rows), active[half, :, cols], ((1,), (0,))).astype(BF16)
            grad[half, :, :, :, cols] = value[:384].reshape(4, 2, 48, 512)
            to_core[half, :, :, :, cols] = value[384:].reshape(4, 2, 48, 512)
            return inner

        lax.fori_loop(0, 3, chunk, 0)
        across(half).start()
        return carry

    lax.fori_loop(0, 2, first_half, 0)
    chains.at()
    for half in range(2):
        across(half).wait()

    def join(t, carry):
        at = (t // 8, (t // 2) % 4, t % 2)
        grad[at] = grad[at] + from_core[at]
        return carry

    lax.fori_loop(0, 16, join, 0)
    back.append(pltpu.make_async_copy(grad, first_grad, grad_sem))
    back[-1].start()
    chains.at()
    keep_weight(7)
    for slot in list(outgoing):
        settle(slot)
    for copy in back:
        copy.wait()


def forward(shards, tokens, cotangent, lengths, gain, shift, outb, qvb, upb):
    rows, width = tokens.shape
    qkv, out, up, down = shards
    widths = [3 * qkv.shape[3], out.shape[2], up.shape[2], down.shape[2]] * 2
    full = [(2, 4, 2, 2, 48, w) for w in widths]
    layer_saves = [
        ((rows, width), F32),
        ((rows, width), F32),
        ((2, 4, 2, 48, rows), BF16),
        ((2, 4, 2, 48, rows), BF16),
        ((2, rows, widths[0]), BF16),
        ((rows, width), BF16),
        ((6, 2, rows, rows), BF16),
        ((2, rows, widths[2]), BF16),
        ((2, rows, widths[2]), BF16),
    ]
    any_spec = pl.BlockSpec(memory_space=pl.ANY)
    vmem_spec = pl.BlockSpec(memory_space=pltpu.VMEM)
    out_shape = (
        [jax.ShapeDtypeStruct(f, BF16) for f in full]
        + [jax.ShapeDtypeStruct(s, t) for s, t in layer_saves * 2]
        + [jax.ShapeDtypeStruct((2, 4, 2, 48, widths[3]), BF16)]
    )
    by_slot = {j: pltpu.VMEM(*layer_saves[j]) for j in range(9)}
    outs = pl.pallas_call(
        forward_kernel,
        out_shape=out_shape,
        in_specs=[any_spec] * 4 + [vmem_spec] * 2 + [pl.BlockSpec(memory_space=pltpu.SMEM)] + [vmem_spec] * 5,
        out_specs=[any_spec] * (ITEM_COUNT + 19),
        scratch_shapes=[pltpu.VMEM(f, BF16) for f in full]
        + [
            by_slot[0],
            by_slot[1],
            pltpu.VMEM((rows, width), BF16),
            by_slot[2],
            by_slot[3],
            by_slot[4],
            by_slot[5],
            by_slot[7],
            by_slot[8],
            by_slot[6],
            pltpu.VMEM((2, *qvb.shape), F32),
            pltpu.VMEM((2, *upb.shape), F32),
            pltpu.VMEM((2, 4, 2, 48, widths[3]), BF16),
            pltpu.VMEM((2, 4, 2, 48, widths[3]), BF16),
            pltpu.VMEM((2, 4, 2, 48, widths[3]), BF16),
            pltpu.SemaphoreType.DMA((len(GATHER_CHAINS), 6)),
            pltpu.SemaphoreType.DMA((len(GATHER_CHAINS), 6)),
            pltpu.SemaphoreType.DMA((ITEM_COUNT, 3)),
            pltpu.SemaphoreType.DMA((2, 9)),
            pltpu.SemaphoreType.DMA((2,)),
            pltpu.SemaphoreType.DMA((2,)),
            pltpu.SemaphoreType.DMA((2,)),
            pltpu.SemaphoreType.DMA((2,)),
            pltpu.SemaphoreType.DMA((ITEM_COUNT,)),
            pltpu.SemaphoreType.DMA,
        ],
        compiler_params=pltpu.CompilerParams(
            collective_id=0, has_side_effects=True, vmem_limit_bytes=VMEM_LIMIT
        ),
        name="forward",
    )(*shards, tokens, cotangent, lengths, gain, shift, outb, qvb, upb)
    return outs[:ITEM_COUNT], [outs[ITEM_COUNT + 9 * l : ITEM_COUNT + 9 * l + 9] for l in range(2)], outs[-1]


def norm_back(source, upstream, gain_row, gradient, rounded):
    def block(t, sums):
        rows = pl.ds(pl.multiple_of(t * 64, 64), 64)
        inputs = source[rows, :]
        centered = inputs - jnp.mean(inputs, axis=-1, keepdims=True)
        rate = lax.rsqrt(jnp.mean(centered * centered, axis=-1, keepdims=True) + EPSILON)
        unit = centered * rate
        above = upstream[rows, :]
        pull = above * gain_row
        along = jnp.mean(pull * unit, axis=-1, keepdims=True)
        total = gradient[rows, :] + rate * (pull - jnp.mean(pull, axis=-1, keepdims=True) - unit * along)
        gradient[rows, :] = total
        if rounded is not None:
            rounded[rows, :] = total.astype(BF16)
        return (
            sums[0] + jnp.sum(above * unit, axis=0, keepdims=True),
            sums[1] + jnp.sum(above, axis=0, keepdims=True),
            sums[2] + jnp.sum(total, axis=0, keepdims=True),
        )

    zero = jnp.zeros((1, source.shape[1]), F32)
    return lax.fori_loop(0, source.shape[0] // 64, block, (zero, zero, zero))


def backward_kernel(*refs):
    n = ITEM_COUNT
    it = iter(refs)

    def take(count):
        return [next(it) for _ in range(count)]

    whole = take(n)
    saved = [take(9) for _ in range(2)]
    first_grad, cotangent, lengths, gain, outb = take(5)
    out_q, out_o, out_u, out_d, token_grad, sums, late, final = take(8)
    outs = (out_q, out_o, out_u, out_d)
    (slot_a, slot_b, stream, middle, turned, turned_mid, project, attended, active, slope, probs) = take(11)
    (gradient, upstream, rounded, left, dattended, dproject) = take(6)
    held = take(4)
    (to_core, from_core) = take(2)
    arrivals = [take(3) for _ in REDUCE_CHAINS]
    small_c, small_x, small_y, small_b, small_z, late_in, late_z = take(7)
    (fetch_sem, prob_sem, core_send, core_recv, send, recv, credit, small_send, small_recv, last_sem, final_sem) = take(11)
    place = z, x, k, y = places()
    peers = partners(z, x, k, y)
    rows = stream.shape[0]

    fetches = {}

    def fetch(name, pairs):
        fetches[name] = [pltpu.make_async_copy(s, t, fetch_sem.at[name, j]) for j, (s, t) in enumerate(pairs)]
        for copy in fetches[name]:
            copy.start()

    def ready(name):
        for copy in fetches.pop(name):
            copy.wait()

    def weights_into(slot, layer, kind):
        w_qkv, w_out, w_up, w_down = whole[4 * layer : 4 * layer + 4]
        if kind == "d":
            return [(w_down, slot)]
        if kind == "u":
            return [(w_up, slot)]
        lead = (slice(None),) * 5
        return [(w_qkv, slot.at[(*lead, pl.ds(0, 1152))]), (w_out, slot.at[(*lead, pl.ds(1152, 384))])]

    SLOT_A, SLOT_B, STREAM, MIDDLE, TURNED, TURNED_MID, PROJECT, ATTENDED, ACTIVE, SLOPE, COT, GRAD = range(12)
    buffers = {
        STREAM: (stream, 0),
        MIDDLE: (middle, 1),
        TURNED: (turned, 2),
        TURNED_MID: (turned_mid, 3),
        PROJECT: (project, 4),
        ATTENDED: (attended, 5),
        ACTIVE: (active, 7),
        SLOPE: (slope, 8),
    }

    def fetch_saved(name, layer):
        target, index = buffers[name]
        fetch(name, [(saved[layer][index], target)])

    def prob_copy(layer, j):
        return pltpu.make_async_copy(saved[layer][6].at[j], probs.at[j % 2], prob_sem.at[j % 2])

    fetch(GRAD, [(first_grad, held[3])])
    fetch(COT, [(cotangent, rounded)])
    fetch(SLOT_A, weights_into(slot_a, 1, "d"))
    for name in (SLOPE, ACTIVE, MIDDLE, TURNED_MID):
        fetch_saved(name, 1)
    fetch(SLOT_B, weights_into(slot_b, 1, "u"))
    for name in (ATTENDED, PROJECT, TURNED, STREAM):
        fetch_saved(name, 1)
    prob_copy(1, 0).start()
    slots = {("d", 1): (SLOT_A, slot_a), ("u", 1): (SLOT_B, slot_b), ("q", 1): (SLOT_A, slot_a),
             ("d", 0): (SLOT_B, slot_b), ("u", 0): (SLOT_A, slot_a), ("q", 0): (SLOT_B, slot_b)}
    greet(peers)

    kinds = [(1, 3), (1, 2), (1, 1), (1, 0), (0, 3), (0, 2), (0, 1), (0, 0)]

    def core_copy(r, half):
        width = held[kinds[r][1]].shape[-1]
        at = (half, slice(None), slice(None), slice(None), pl.ds(0, width))
        return pltpu.make_async_remote_copy(
            to_core.at[at], from_core.at[at], core_send.at[r, half], core_recv.at[r, half],
            device_id=peers[5], device_id_type=MESH,
        )

    def take_core(r):
        b = held[kinds[r][1]]
        width = b.shape[-1]
        for half in range(2):
            core_copy(r, half).wait()

        def block(t, carry):
            at = (t // 8, (t // 2) % 4, t % 2)
            b[at] = b[at] + from_core[(*at, slice(None), pl.ds(0, width))]
            return carry

        lax.fori_loop(0, 16, block, 0)
        if r < n - 1:
            for half in range(2):
                pl.semaphore_signal(credit.at[half], inc=1, device_id=peers[5], device_id_type=MESH)

    def rest_of(order, phase):
        return [(axis, size) for axis, size in (("y", 2), ("z", 4), ("x", 2)) if axis in order[phase + 1 :]]

    def copies(c, phase):
        r, first, width, order = REDUCE_CHAINS[c]
        b, cols = held[kinds[r][1]], pl.ds(first, width)
        target = arrivals[c][phase]
        left_over = order[phase + 1 :]

        def block(axis, there):
            at = []
            for name, own_at in (("y", y), ("z", z), ("x", x)):
                at.append(there if name == axis else slice(None) if name in left_over else own_at)
            return b.at[(*at, slice(None), cols)]

        def remote(source, there, slot, peer):
            return pltpu.make_async_remote_copy(
                source, there, send.at[c, slot], recv.at[c, slot], device_id=peers[peer], device_id_type=MESH
            )

        if order[phase] == "z":
            return [remote(block("z", (z + 1 + j) % 4), target.at[j], j, j) for j in range(3)]
        if order[phase] == "x":
            return [remote(block("x", 1 - x), target, 3, 3)]
        return [remote(block("y", 1 - y), target, 4, 4)]

    def arrived(c, phase):
        r, first, width, order = REDUCE_CHAINS[c]
        layer, kind = kinds[r]
        b, cols = held[kind], pl.ds(first, width)
        source = arrivals[c][phase]
        rest = rest_of(order, phase)
        count = 1
        for _, size in rest:
            count *= size

        def total(t):
            at, inner, stride = {}, [], 1
            for axis, size in reversed(rest):
                at[axis] = (t // stride) % size
                stride *= size
            inner = [at[axis] for axis, _ in rest]
            spot = (at.get("y", y), at.get("z", z), at.get("x", x), slice(None), cols)
            value = b[spot].astype(F32)
            if order[phase] == "z":
                for j in range(3):
                    value += source[(j, *inner)].astype(F32)
            else:
                value += source[tuple(inner)].astype(F32) if inner else source[...].astype(F32)
            return spot, value

        if not rest:
            outs[kind][layer, :, cols] = total(0)[1]
        else:

            def block(t, carry):
                spot, value = total(t)
                b[spot] = value.astype(BF16)
                return carry

            lax.fori_loop(0, count, block, 0)

    early, late_at = len(REDUCE_CHAINS), len(REDUCE_CHAINS) + 1

    def small_copies(c, phase):
        def remote(source, target, slot, peer):
            return pltpu.make_async_remote_copy(
                source, target, small_send.at[slot], small_recv.at[slot], device_id=peers[peer], device_id_type=MESH
            )

        if c == early:
            if phase == 0:
                return [remote(sums.at[1 - k], small_c, 0, 5)]
            if phase == 3:
                small_z[z] = sums[k]
                return [remote(sums.at[k], small_z.at[z], 3 + j, j) for j in range(3)]
            target, slot, peer = ((small_x, 1, 3), (small_y, 2, 4), None, (small_b, 6, 5))[phase - 1]
            return [remote(sums.at[k], target, slot, peer)]
        if phase == 3:
            late_z[z] = late[...]
            return [remote(late, late_z.at[z], 10 + j, j) for j in range(3)]
        return [remote(late, late_in.at[phase], 7 + phase, (5, 3, 4)[phase])]

    def small_arrived(c, phase):
        if c == early:
            if phase == 4:
                sums[1 - k] = small_b[...]
            elif phase == 3:
                sums[k] = (small_z[0] + small_z[1]) + (small_z[2] + small_z[3])
            else:
                sums[k] += (small_c, small_x, small_y)[phase][...]
        elif phase == 3:
            late[...] = (late_z[0] + late_z[1]) + (late_z[2] + late_z[3])
        else:
            late[...] += late_in[phase]

    def any_copies(c, phase):
        return copies(c, phase) if c < early else small_copies(c, phase)

    def any_arrived(c, phase):
        return arrived(c, phase) if c < early else small_arrived(c, phase)

    chains = Chains(REDUCE_TABLE, any_copies, any_arrived)

    def weight_gradient(r, lhs, rhs):
        b = held[kinds[r][1]]
        width = b.shape[-1]
        size = 512 if width % 512 == 0 else 384

        def one(half, carry):
            def chunk(t, inner):
                cols = pl.ds(pl.multiple_of(t * size, 128), size)
                value = mm(lhs[...].reshape(768, rows), rhs(half, cols), ((1,), (0,))).astype(BF16)
                b[half, :, :, :, cols] = value[:384].reshape(4, 2, 48, size)
                to_core[half, :, :, :, cols] = value[384:].reshape(4, 2, 48, size)
                return inner

            lax.fori_loop(0, width // size, chunk, 0)
            if r > 1:
                pl.semaphore_wait(credit.at[half], 1)
            core_copy(r, half).start()
            return carry

        lax.fori_loop(0, 2, one, 0)

    sums[0, 0:2, 0:768] = jnp.zeros((2, 768), F32)
    sums[:, 6:8, :] = jnp.zeros((2, 2, 1536), F32)
    chains.at()
    ready(GRAD)
    chains.at()
    ready(COT)
    keep = lax.broadcasted_iota(jnp.int32, (rows, 1), 0) < lengths[y]
    gradient[...] = jnp.where(keep, rounded[...].astype(F32), 0.0)
    rounded[...] = gradient[...].astype(BF16)
    everything = (slice(None),) * 4

    def place_at(*taken):
        for r in taken:
            take_core(r)
        chains.at()

    for layer in (1, 0):
        first = 0 if layer == 1 else 4
        place_at()
        sums[layer, 2:3, 768:1536] = jnp.sum(gradient[...], axis=0, keepdims=True)
        name, w_down = slots["d", layer]
        if layer == 0:
            turn_rows(rounded, left, k)
            ready(ACTIVE)
            place_at()
            weight_gradient(first, left, lambda half, cols: active[half, :, cols])
        ready(name)
        ready(SLOPE)
        place_at()

        def unit(t, carry):
            half = t // 3
            cols = pl.ds(pl.multiple_of((t % 3) * 512, 128), 512)
            dact = mm(rounded[...], matrix(w_down, half, *everything, cols), ((1,), (0,)))
            dhidden = (dact * slope[half, :, cols].astype(F32)).astype(BF16)
            slope[half, :, cols] = dhidden
            sums[layer, pl.ds(4 + half, 1), cols] = jnp.sum(dhidden.astype(F32), axis=0, keepdims=True)
            return carry

        lax.fori_loop(0, 6, unit, 0)
        if layer == 1:
            ready(ACTIVE)
            ready(MIDDLE)

            def close(c, carry):
                cols = pl.ds(pl.multiple_of(c * 384, 128), 384)
                total = middle[:, cols] + outb[1, 1:2, cols]
                for half in range(2):
                    total += mm(active[half], matrix(w_down, half, pl.ds(2 * c, 2)), ((1,), (1,)))
                dattended[c] = total.astype(BF16)
                return carry

            lax.fori_loop(0, 2, close, 0)
            finals = [
                pltpu.make_async_copy(dattended.at[c], final.at[:, pl.ds(c * 384, 384)], final_sem.at[c])
                for c in range(2)
            ]
            for copy in finals:
                copy.start()
            fetch(SLOT_A, weights_into(slot_a, 1, "q"))
            fetch_saved(ACTIVE, 0)
        else:
            fetch(SLOT_B, weights_into(slot_b, 0, "q"))
        name, w_up = slots["u", layer]
        ready(name)
        ready(TURNED_MID)
        place_at(*([first] if first else []))
        weight_gradient(first + 1, turned_mid, lambda half, cols: slope[half, :, cols])
        place_at(first + 1)

        def pull_up(c, carry):
            total = mm(slope[0], matrix(w_up, 0, pl.ds(2 * c, 2)), ((1,), (1,)))
            total += mm(slope[1], matrix(w_up, 1, pl.ds(2 * c, 2)), ((1,), (1,)))
            upstream[:, pl.ds(pl.multiple_of(c * 384, 128), 384)] = total
            return carry

        lax.fori_loop(0, 2, pull_up, 0)
        if layer == 1:
            fetch(SLOT_B, weights_into(slot_b, 0, "d"))
            fetch_saved(SLOPE, 0)
            fetch_saved(TURNED_MID, 0)
        if layer == 0:
            ready(MIDDLE)
        place_at()
        gain_sum, shift_sum, bias_sum = norm_back(middle, upstream, gain[layer, 1:2], gradient, rounded)
        sums[layer, 0:1, 768:1536] = gain_sum
        sums[layer, 1:2, 768:1536] = shift_sum
        sums[layer, 2:3, 0:768] = bias_sum
        if layer == 1:
            fetch_saved(MIDDLE, 0)
        name, w_qo = slots["q", layer]
        ready(name)
        ready(ATTENDED)
        place_at()
        turn_rows(rounded, left, k)
        weight_gradient(first + 2, left, lambda half, cols: attended[:, pl.ds(pl.multiple_of(half * 384, 128), 384)])

        if layer == 1:
            for copy in finals:
                copy.wait()

        def pull_out(half, carry):
            dattended[half] = mm(rounded[...], matrix(w_qo, half, *everything, pl.ds(1152, 384)), ((1,), (0,))).astype(BF16)
            return carry

        lax.fori_loop(0, 2, pull_out, 0)
        if layer == 1:
            fetch_saved(ATTENDED, 0)
        ready(PROJECT)
        scale = HEAD_DIM**-0.5

        def pair(j, carry):
            half = j // 3
            at = (j % 3) * 128
            prob_copy(layer, j).wait()

            @pl.when(j < 5)
            def _():
                prob_copy(layer, j + 1).start()

            lane = lax.broadcasted_iota(jnp.int32, (1, 128), 1) < 64
            columns = [pl.ds(pl.multiple_of(at + t * 384, 128), 128) for t in range(3)]
            query, key, value = (project[half, :, c] for c in columns)
            above = dattended[half, :, columns[0]]
            key_t = key.T
            dkeys, dvalues, dqueries = [], [], []
            for h in range(2):
                here = lane if h == 0 else jnp.logical_not(lane)
                prob = probs[j % 2, h]
                dprob = mm(jnp.where(here, value, jnp.zeros_like(value)), above, ((1,), (1,)))
                prob32 = prob.astype(F32)
                both = prob32 * dprob
                dscore = (both - prob32 * jnp.sum(both, axis=0, keepdims=True)).astype(BF16)
                dvalues.append(mm(prob, above, ((1,), (0,))))
                dkeys.append(mm(dscore, query, ((1,), (0,))))
                dqueries.append(mm(key_t[h * 64 : (h + 1) * 64], dscore, ((1,), (0,))))
            dproject[half, :, columns[0]] = (jnp.concatenate(dqueries, axis=0) * scale).T.astype(BF16)
            dproject[half, :, columns[1]] = (jnp.where(lane, dkeys[0], dkeys[1]) * scale).astype(BF16)
            dproject[half, :, columns[2]] = jnp.where(lane, dvalues[0], dvalues[1]).astype(BF16)
            return carry

        place_at(first + 2)
        lax.fori_loop(0, 3, pair, 0)
        place_at()
        lax.fori_loop(3, 6, pair, 0)
        if layer == 1:
            fetch_saved(PROJECT, 0)
            prob_copy(0, 0).start()
        ready(TURNED)
        place_at()
        for half in range(2):
            for t in (0, 2):
                sums[layer, 3:4, (t // 2) * 768 + half * 384 : (t // 2) * 768 + half * 384 + 384] = jnp.sum(
                    dproject[half, :, t * 384 : (t + 1) * 384].astype(F32), axis=0, keepdims=True
                )
        weight_gradient(first + 3, turned, lambda half, cols: dproject[half, :, cols])
        place_at(first + 3)

        def pull_qkv(c, carry):
            rest = (slice(None),) * 3
            total = mm(dproject[0], matrix(w_qo, 0, pl.ds(2 * c, 2), *rest, pl.ds(0, 1152)), ((1,), (1,)))
            total += mm(dproject[1], matrix(w_qo, 1, pl.ds(2 * c, 2), *rest, pl.ds(0, 1152)), ((1,), (1,)))
            upstream[:, pl.ds(pl.multiple_of(c * 384, 128), 384)] = total
            return carry

        lax.fori_loop(0, 2, pull_qkv, 0)
        if layer == 1:
            fetch(SLOT_A, weights_into(slot_a, 0, "u"))
            fetch_saved(TURNED, 0)
        ready(STREAM)
        place_at()
        gain_sum, shift_sum, _ = norm_back(stream, upstream, gain[layer, 0:1], gradient, rounded if layer == 1 else None)
        if layer == 1:
            sums[1, 0:1, 0:768] = gain_sum
            sums[1, 1:2, 0:768] = shift_sum
            fetch_saved(STREAM, 0)
        else:
            late[0:1] = gain_sum
            late[1:2] = shift_sum
    last = pltpu.make_async_copy(gradient, token_grad, last_sem)
    last.start()

    chains.at()
    last.wait()


def backward(whole, saved, first_grad, cotangent, lengths, gain, outb):
    rows, width = cotangent.shape
    widths = [w.shape[-1] for w in whole[:4]]
    any_spec = pl.BlockSpec(memory_space=pl.ANY)
    vmem_spec = pl.BlockSpec(memory_space=pltpu.VMEM)

    def blocks(*lead):
        return [pltpu.VMEM((*lead, 48, w), BF16) for w in widths]

    def arrival_shapes():
        sizes, shapes = {"y": 2, "z": 4, "x": 2}, []
        for _, _, columns, order in REDUCE_CHAINS:
            for phase in range(3):
                lead = [3] if order[phase] == "z" else []
                lead += [sizes[axis] for axis in "yzx" if axis in order[phase + 1 :]]
                shapes.append(pltpu.VMEM((*lead, 48, columns), BF16))
        return shapes

    wide = widths[2]
    small = (2, 8, wide)
    outs = pl.pallas_call(
        backward_kernel,
        out_shape=[jax.ShapeDtypeStruct((2, 48, w), F32) for w in widths]
        + [
            jax.ShapeDtypeStruct((rows, width), F32),
            jax.ShapeDtypeStruct(small, F32),
            jax.ShapeDtypeStruct((2, width), F32),
            jax.ShapeDtypeStruct((rows, width), BF16),
        ],
        in_specs=[any_spec] * (ITEM_COUNT + 18 + 2) + [pl.BlockSpec(memory_space=pltpu.SMEM), vmem_spec, vmem_spec],
        out_specs=[vmem_spec] * 4 + [any_spec, vmem_spec, vmem_spec, any_spec],
        scratch_shapes=[
            pltpu.VMEM((2, 4, 2, 2, 48, wide), BF16),
            pltpu.VMEM((2, 4, 2, 2, 48, wide), BF16),
            pltpu.VMEM((rows, width), F32),
            pltpu.VMEM((rows, width), F32),
            pltpu.VMEM((2, 4, 2, 48, rows), BF16),
            pltpu.VMEM((2, 4, 2, 48, rows), BF16),
            pltpu.VMEM((2, rows, widths[0]), BF16),
            pltpu.VMEM((rows, width), BF16),
            pltpu.VMEM((2, rows, wide), BF16),
            pltpu.VMEM((2, rows, wide), BF16),
            pltpu.VMEM((2, 2, rows, rows), BF16),
            pltpu.VMEM((rows, width), F32),
            pltpu.VMEM((rows, width), F32),
            pltpu.VMEM((rows, width), BF16),
            pltpu.VMEM((2, 4, 2, 48, rows), BF16),
            pltpu.VMEM((2, rows, width // 2), BF16),
            pltpu.VMEM((2, rows, widths[0]), BF16),
        ]
        + blocks(2, 4, 2)
        + [pltpu.VMEM((2, 4, 2, 48, wide), BF16), pltpu.VMEM((2, 4, 2, 48, wide), BF16)]
        + arrival_shapes()
        + [pltpu.VMEM(small[1:], F32)] * 4
        + [pltpu.VMEM((4, *small[1:]), F32), pltpu.VMEM((3, 2, width), F32), pltpu.VMEM((4, 2, width), F32)]
        + [
            pltpu.SemaphoreType.DMA((12, 2)),
            pltpu.SemaphoreType.DMA((2,)),
            pltpu.SemaphoreType.DMA((ITEM_COUNT, 2)),
            pltpu.SemaphoreType.DMA((ITEM_COUNT, 2)),
            pltpu.SemaphoreType.DMA((len(REDUCE_CHAINS), 5)),
            pltpu.SemaphoreType.DMA((len(REDUCE_CHAINS), 5)),
            pltpu.SemaphoreType.REGULAR((2,)),
            pltpu.SemaphoreType.DMA((13,)),
            pltpu.SemaphoreType.DMA((13,)),
            pltpu.SemaphoreType.DMA,
            pltpu.SemaphoreType.DMA((2,)),
        ],
        compiler_params=pltpu.CompilerParams(
            collective_id=1, has_side_effects=True, vmem_limit_bytes=63 * 2**20
        ),
        name="backward",
    )(*whole, *saved[0], *saved[1], first_grad, cotangent, lengths, gain, outb)
    return outs


def generic_body(dp_size, tokens, lengths, cotangent, norm_gain, norm_shift, qkv_weight, qv_bias,
         out_weight, up_weight, up_bias, down_weight, out_bias):
    part = lax.axis_index("tensor")
    layers = norm_gain.shape[0]
    rows, width = tokens.shape
    length = lax.dynamic_index_in_dim(lengths, part, keepdims=False)
    keep = jnp.arange(rows, dtype=jnp.int32) < length
    own = qkv_weight.shape[1]
    shards = []
    for layer in range(layers):
        shards += [
            qkv_weight[layer].reshape(own, -1),
            out_weight[layer].T,
            up_weight[layer],
            down_weight[layer].T,
        ]
    if False:
        full = [w.reshape(2, width, -1) for w in gather_weights(shards)]
    else:
        full = [
            lax.all_gather(s, ("tensor", "dp"), axis=0).reshape(2, width, -1) for s in shards
        ]
    qv_all = lax.all_gather(qv_bias, "tensor", axis=0)
    upb_all = lax.all_gather(up_bias, "tensor", axis=0)
    scale = HEAD_DIM**-0.5
    stream = tokens.astype(F32)
    saved = []
    for layer in range(layers):
        w_qkv, w_out, w_up, w_down = full[4 * layer : 4 * layer + 4]
        normed = layer_norm(stream, norm_gain[layer, 0], norm_shift[layer, 0]).astype(BF16)
        project = []
        for t in range(2):
            b = jnp.concatenate([qv_all[t, layer, 0], jnp.zeros_like(qv_all[t, layer, 0]), qv_all[t, layer, 1]])
            project.append((mm(normed, w_qkv[t], ((1,), (0,))) + b).astype(BF16))
        third = width // 2
        q, key, val = (
            heads(jnp.concatenate([project[t][:, j * third : (j + 1) * third] for t in range(2)], axis=1))
            for j in range(3)
        )
        scores = jnp.einsum("hqd,hkd->hqk", q, key, preferred_element_type=F32) * scale
        scores = jnp.where(keep[None, None, :], scores, -1e30)
        highest = jnp.max(scores, axis=-1, keepdims=True)
        exponent = jnp.exp(scores - highest)
        probs32 = exponent / jnp.sum(exponent, axis=-1, keepdims=True)
        probs = probs32.astype(BF16)
        attended = flat(jnp.einsum("hqk,hkd->hqd", probs, val, preferred_element_type=F32)).astype(BF16)
        branch = sum(mm(attended[:, t * third : (t + 1) * third], w_out[t], ((1,), (1,))) for t in range(2))
        middle = stream + branch + out_bias[layer, 0]
        normed_mid = layer_norm(middle, norm_gain[layer, 1], norm_shift[layer, 1]).astype(BF16)
        hidden = [mm(normed_mid, w_up[t], ((1,), (0,))) + upb_all[t, layer] for t in range(2)]
        activated = [gelu_exact(h).astype(BF16) for h in hidden]
        branch_mlp = sum(mm(activated[t], w_down[t], ((1,), (1,))) for t in range(2))
        saved.append((stream, middle, normed, q, key, val, probs, attended, normed_mid, hidden, activated))
        stream = middle + branch_mlp + out_bias[layer, 1]
    final = stream.astype(BF16)
    gradient = cotangent.astype(F32) * keep.astype(F32)[:, None]
    grads = [None] * (4 * layers)
    gain, shift, outb, qvb, upb = ([None] * layers for _ in range(5))
    for layer in reversed(range(layers)):
        stream_in, middle, normed, q, key, val, probs, attended, normed_mid, hidden, activated = saved[layer]
        w_qkv, w_out, w_up, w_down = full[4 * layer : 4 * layer + 4]
        third = width // 2
        bias_late = jnp.sum(gradient, axis=0)
        dout = gradient.astype(BF16)
        grads[4 * layer + 3] = jnp.stack([mm(dout, activated[t], ((0,), (0,))).astype(BF16) for t in range(2)])
        dhidden = []
        for t in range(2):
            dact = mm(dout, w_down[t], ((1,), (0,)))
            dhidden.append(jax.vjp(gelu_exact, hidden[t])[1](dact)[0].astype(BF16))
        upb[layer] = jnp.stack([jnp.sum(d.astype(F32), axis=0) for d in dhidden])
        grads[4 * layer + 2] = jnp.stack([mm(normed_mid, d, ((0,), (0,))).astype(BF16) for d in dhidden])
        dnormed_mid = sum(mm(dhidden[t], w_up[t], ((1,), (1,))) for t in range(2))
        pull = jax.vjp(layer_norm, middle, norm_gain[layer, 1], norm_shift[layer, 1])[1]
        dmid, gain_late, shift_late = pull(dnormed_mid)
        dmiddle = gradient + dmid
        bias_early = jnp.sum(dmiddle, axis=0)
        dbranch = dmiddle.astype(BF16)
        dout_t = mm(dbranch, attended, ((0,), (0,))).astype(BF16)
        grads[4 * layer + 1] = halves(dout_t)
        dattended = heads(jnp.concatenate([mm(dbranch, w_out[t], ((1,), (0,))) for t in range(2)], axis=1).astype(BF16))
        p = probs.astype(F32)
        dval = jnp.einsum("hqk,hqd->hkd", probs, dattended, preferred_element_type=F32)
        dprobs = jnp.einsum("hqd,hkd->hqk", dattended, val, preferred_element_type=F32)
        dscores = (p * (dprobs - jnp.sum(p * dprobs, axis=-1, keepdims=True))).astype(BF16)
        dquery = jnp.einsum("hqk,hkd->hqd", dscores, key, preferred_element_type=F32) * scale
        dkey = jnp.einsum("hqk,hqd->hkd", dscores, q, preferred_element_type=F32) * scale
        parts = [flat(a).astype(BF16) for a in (dquery, dkey, dval)]
        dproject = [
            jnp.concatenate([a[:, t * third : (t + 1) * third] for a in parts], axis=1) for t in range(2)
        ]
        qvb[layer] = jnp.stack([jnp.sum(parts[0].astype(F32), axis=0), jnp.sum(parts[2].astype(F32), axis=0)])
        grads[4 * layer] = jnp.stack([mm(normed, d, ((0,), (0,))).astype(BF16) for d in dproject])
        dnormed = sum(mm(dproject[t], w_qkv[t], ((1,), (1,))) for t in range(2))
        pull = jax.vjp(layer_norm, stream_in, norm_gain[layer, 0], norm_shift[layer, 0])[1]
        dfirst, gain_early, shift_early = pull(dnormed)
        gradient = dmiddle + dfirst
        gain[layer] = jnp.stack([gain_early, gain_late])
        shift[layer] = jnp.stack([shift_early, shift_late])
        outb[layer] = jnp.stack([bias_early, bias_late])
    if False:
        reduced = reduce_gradients([g.reshape(2, 4, 2, 2, 48, -1) for g in grads])
    else:
        reduced = [
            lax.psum_scatter(
                g.reshape(2 * dp_size, own, -1).astype(F32), ("tensor", "dp"), scatter_dimension=0
            )
            for g in grads
        ]
    g_gain, g_shift, g_outb, g_qvb, g_upb = lax.psum(
        (jnp.stack(gain), jnp.stack(shift), jnp.stack(outb), jnp.stack(qvb), jnp.stack(upb)),
        ("dp", "tensor"),
    )
    g_qvb = lax.dynamic_slice_in_dim(g_qvb, part * qv_bias.shape[2], qv_bias.shape[2], axis=2)
    g_upb = lax.dynamic_index_in_dim(g_upb, part, axis=1, keepdims=False)
    g_qkv = jnp.stack([reduced[4 * l].reshape(own, 3, -1) for l in range(layers)])
    g_out = jnp.stack([reduced[4 * l + 1].T for l in range(layers)])
    g_up = jnp.stack([reduced[4 * l + 2] for l in range(layers)])
    g_down = jnp.stack([reduced[4 * l + 3].T for l in range(layers)])
    return (final, gradient, g_gain, g_shift, g_qkv, g_qvb, g_out, g_up, g_upb, g_down, g_outb)


def finish_kernel(*refs):
    g_qkv, g_out, g_up, g_down, token_grad, sums, late, final = refs[:8]
    o_final, o_token, o_gain, o_shift, o_qkv, o_qvb, o_out, o_up, o_upb, o_down, o_outb = refs[8:19]
    (sem,) = refs[19:]
    y = lax.axis_index("tensor")
    width = late.shape[1]
    third = width // 2
    pairs = [(token_grad, o_token), (final, o_final), (g_up, o_up), (g_out, o_out), (g_down, o_down)]
    for layer in range(2):
        for t in range(3):
            pairs.append((g_qkv.at[layer, :, pl.ds(t * third, third)], o_qkv.at[layer, t]))
    moves = [pltpu.make_async_copy(source, target, sem.at[j]) for j, (source, target) in enumerate(pairs)]
    for copy in moves:
        copy.start()
    for layer in range(2):
        o_upb[layer : layer + 1] = sums[layer, pl.ds(4 + y, 1)]
        for j in range(2):
            at = slice(j * width, (j + 1) * width)
            here = pl.ds(pl.multiple_of(j * width + y * third, 128), third)
            o_outb[layer, j : j + 1] = sums[layer, 2:3, at]
            o_qvb[layer, j : j + 1] = sums[layer, 3:4, here]
            if layer == 0 and j == 0:
                o_gain[0, 0:1] = late[0:1]
                o_shift[0, 0:1] = late[1:2]
            else:
                o_gain[layer, j : j + 1] = sums[layer, 0:1, at]
                o_shift[layer, j : j + 1] = sums[layer, 1:2, at]
    for copy in moves:
        copy.wait()


def fused_body(tokens, lengths, cotangent, norm_gain, norm_shift, qkv_weight, qv_bias, out_weight, up_weight,
               up_bias, down_weight, out_bias):
    shards = (
        qkv_weight.transpose(0, 2, 1, 3),
        out_weight.transpose(0, 2, 1),
        up_weight,
        down_weight.transpose(0, 2, 1),
    )
    full, saved, first_grad = forward(
        shards, tokens, cotangent, lengths, norm_gain, norm_shift, out_bias, qv_bias, up_bias
    )
    reduced = backward(full, saved, first_grad, cotangent, lengths, norm_gain, out_bias)
    any_spec = pl.BlockSpec(memory_space=pl.ANY)
    vmem_spec = pl.BlockSpec(memory_space=pltpu.VMEM)

    def shape(array, kind=F32):
        return jax.ShapeDtypeStruct(array.shape, kind)

    outs = pl.pallas_call(
        finish_kernel,
        out_shape=(
            shape(tokens, BF16),
            shape(tokens),
            shape(norm_gain),
            shape(norm_shift),
            shape(shards[0]),
            shape(qv_bias),
            shape(shards[1]),
            shape(shards[2]),
            shape(up_bias),
            shape(shards[3]),
            shape(out_bias),
        ),
        in_specs=[vmem_spec] * 8,
        out_specs=(any_spec, any_spec, vmem_spec, vmem_spec, any_spec, vmem_spec, any_spec, any_spec, vmem_spec, any_spec, vmem_spec),
        scratch_shapes=[pltpu.SemaphoreType.DMA((11,))],
        name="finish",
    )(*reduced)
    final, token_grad, gain, shift, g_qkv, qvb, g_out, g_up, upb, g_down, outb = outs
    return (
        final,
        token_grad,
        gain,
        shift,
        g_qkv.transpose(0, 2, 1, 3),
        qvb,
        g_out.transpose(0, 2, 1),
        g_up,
        upb,
        g_down.transpose(0, 2, 1),
        outb,
    )


def solution(mesh):
    use_kernels = mesh.shape["dp"] == 16 and mesh.shape["tensor"] == 2
    return jax.shard_map(
        fused_body if use_kernels else functools.partial(generic_body, mesh.shape["dp"]),
        mesh=mesh,
        in_specs=(
            P(("dp", "tensor"), None),
            P("dp"),
            P(("dp", "tensor"), None),
            P(),
            P(),
            P(None, "dp", None, "tensor"),
            P(None, None, "tensor"),
            P(None, "tensor", "dp"),
            P(None, "dp", "tensor"),
            P(None, "tensor"),
            P(None, "tensor", "dp"),
            P(),
        ),
        out_specs=(
            P(("dp", "tensor"), None),
            P(("dp", "tensor"), None),
            P(),
            P(),
            P(None, "dp", None, "tensor"),
            P(None, None, "tensor"),
            P(None, "tensor", "dp"),
            P(None, "dp", "tensor"),
            P(None, "tensor"),
            P(None, "tensor", "dp"),
            P(),
        ),
        check_vma=False,
    )
```

```python
import functools

import jax
import jax.numpy as jnp
from jax import lax
from jax.experimental import pallas as pl
from jax.experimental.pallas import tpu as pltpu
from jax.sharding import PartitionSpec as P

HEAD_DIM = 64
EPSILON = 1e-06
MESH = pl.DeviceIdType.MESH
VMEM_LIMIT = 60 * 2**20
BF16 = jnp.bfloat16
F32 = jnp.float32
ITEM_COUNT = 8
GATHER_CHAINS = (
    (0, 0, 256, "zxy"),
    (0, 256, 256, "zyx"),
    (0, 512, 384, "zxy"),
    (0, 896, 256, "zyx"),
    (1, 0, 256, "zyx"),
    (1, 256, 128, "zxy"),
    (2, 0, 384, "zxy"),
    (2, 384, 384, "zyx"),
    (2, 768, 384, "zxy"),
    (2, 1152, 384, "zyx"),
    (3, 0, 384, "zxy"),
    (3, 384, 384, "zyx"),
    (3, 768, 384, "zxy"),
    (3, 1152, 384, "zyx"),
    (4, 0, 256, "xyz"),
    (4, 256, 256, "yxz"),
    (4, 512, 384, "zxy"),
    (4, 896, 256, "zyx"),
    (5, 0, 256, "zyx"),
    (5, 256, 128, "zxy"),
    (6, 0, 384, "xzy"),
    (6, 384, 384, "yzx"),
    (6, 768, 384, "zxy"),
    (6, 1152, 384, "zyx"),
    (7, 0, 384, "zxy"),
    (7, 384, 384, "zyx"),
    (7, 768, 384, "zxy"),
    (7, 1152, 384, "zyx"),
)
GATHER_TABLE = (
    (112, 160, 168, 120, 40, 48, 24, 8),
    (),
    (-113, 113, -169, -41, 41, 0, -121, 121, -161, -49, 49, 16, -114, -42, 42, -25, 25, 32, -122, -9, 9, 80, -50, 50, -43, 43, -1, 1, 56, -26, 26, -44, -17, 17, 72, -10, 10, -2, 2, -33, 33, 144, -81, 81, 88, -27, 27, -51, 51, -28, -57, 57, 64, -18, 18, -52, -3, 3, -73, 73, 104, -11, 11, -34, 34, -4, -145, 145, 96, -12, -82, -58, 58, 82, -89, 176, -65, 65, 136, -35, 35, -19, 89, 19, -36, -105, 128, -20),
    (-74, 74, 105, -97, 97, 152, -59, 59, -146, 146),
    (-177, 114, -66, 177, 66),
    (-60, -137, 169, -83, 137, 83, -129, 192, -153, 184, -75, 129, 75, -90, -98, 90, 98, -106),
    (),
    (-84, -76, -147, 106, 147, -115, 122, 115, -67, 67, -178, 153, 178, -148, -116, -138, -68),
    (-130, 138, 130, -170, 216),
    (-193, 161, -99, 99, -91, 170, 91, -185, 185, 200, -100, -92, -179, 179, -107, 193, 107, -154, 154, -180, -108, -123, 208, 123),
    (-131, 131, -139, 139, -124, -217, 217),
    (-186, 186, -132, -140),
    (-155, 155, -171, 171),
    (-162, 162, -218, 218, -156, -194, 194),
    (-172, -201, 201, -209, 209, -187, 187, -163, 163),
    (),
    (-188, -219, 219, -164),
    (-195, 195, -210, 210, -220, -202, 202),
    (-196,),
    (-211, 211, -203, 203),
    (-212, -204),
)


REDUCE_CHAINS = (
    (0, 0, 384, "yxz"),
    (0, 384, 384, "xyz"),
    (0, 768, 384, "yzx"),
    (0, 1152, 384, "xzy"),
    (1, 0, 384, "yxz"),
    (1, 384, 384, "xyz"),
    (1, 768, 384, "yzx"),
    (1, 1152, 384, "xzy"),
    (2, 0, 256, "xyz"),
    (2, 256, 128, "yxz"),
    (3, 0, 256, "yxz"),
    (3, 256, 256, "xyz"),
    (3, 512, 384, "yxz"),
    (3, 896, 256, "xyz"),
    (4, 0, 384, "yxz"),
    (4, 384, 384, "xyz"),
    (4, 768, 384, "yzx"),
    (4, 1152, 384, "xzy"),
    (5, 0, 384, "yxz"),
    (5, 384, 384, "xyz"),
    (5, 768, 384, "yxz"),
    (5, 1152, 384, "xyz"),
    (6, 0, 256, "xyz"),
    (6, 256, 128, "yxz"),
    (7, 0, 256, "yxz"),
    (7, 256, 256, "xyz"),
    (7, 512, 384, "yxz"),
    (7, 896, 256, "xyz"),
)
REDUCE_TABLE = (
    (),
    (8, 24, 16, 0),
    (),
    (),
    (),
    (56, 32, -9, 40, -17, 48, 17),
    (-1, 9, -25, 1, 25),
    (),
    (-18, -33, 72, -57, 18, 57),
    (-26, -41, 33, -49, 41, 49),
    (-2, 64, 2, -10, 26, -19),
    (104, -73, 80, -58, 10, -34, 73, -42, 58, -27, 96),
    (-65, 88, -50, 34, -3, 42),
    (-81, 65, -105, 81, -59, 105, -74, 50),
    (-11, 74),
    (-35, -89, 136, -97, 128),
    (-82, 97, 82, -43, -66, 112, 66, -51, 120, -75, -106, 89, 106),
    (-137, 152, -129, 144, -83, 137),
    (-98, 168, -67, 129, -107, 98, -113, 160, -90, -121, 113, 121),
    (),
    (-138, 90, -145, 184),
    (-153, 145, -130),
    (-161, 138, -169, 176, -99, -91, -122, 153, 122),
    (224, -114, 161, 114, -185, 192, -139, 208, -146, 185, 146),
    (-123, -154, 169, 154, -225, -177, 225, -115, -162, 130, 162),
    (232, -193, 177, -186, 193, -147, 186),
    (-226, 216, -131, 200, -233, -155, -209, 226, -194, 233, 194, -163, -170, 170, -187, -178, 178, -195, -227, 227, -217, 209, 217, -171, -201, 201, -234, 234, -218, 218, -179, -210, 210, -202, -235, -228, 235, 228, -219, 202, -229, -211, -236, -203),
)


def places():
    dp = lax.axis_index("dp")
    y = lax.axis_index("tensor")
    return dp // 4, (dp // 2) % 2, dp % 2, y


def partners(z, x, k, y):
    def at(z_, x_, k_, y_):
        return {"dp": (z_ * 2 + x_) * 2 + k_, "tensor": y_}

    along_z = [at((z + step) % 4, x, k, y) for step in (1, 2, 3)]
    return along_z + [at(z, 1 - x, k, y), at(z, x, k, 1 - y), at(z, x, 1 - k, y)]


def greet(peers):
    barrier = pltpu.get_barrier_semaphore()
    for peer in peers:
        pl.semaphore_signal(barrier, inc=1, device_id=peer, device_id_type=MESH)
    pl.semaphore_wait(barrier, len(peers))


def layer_norm(inputs, gain_row, shift_row):
    centered = inputs - jnp.mean(inputs, axis=-1, keepdims=True)
    variance = jnp.mean(centered * centered, axis=-1, keepdims=True)
    return centered * lax.rsqrt(variance + EPSILON) * gain_row + shift_row


def gelu_exact(values):
    return jax.nn.gelu(values, approximate=False)


def mm(left, right, contract):
    return lax.dot_general(left, right, (contract, ((), ())), preferred_element_type=F32)


def halves(array):
    return jnp.stack(jnp.split(array, 2, axis=1))


def heads(array):
    return array.reshape(array.shape[0], -1, HEAD_DIM).transpose(1, 0, 2)


def flat(array):
    return array.transpose(1, 0, 2).reshape(array.shape[1], -1)


class Chains:
    def __init__(self, table, copies, arrived):
        self.table, self.copies, self.arrived = table, copies, arrived
        self.live, self.spot = {}, 0

    def act(self, code):
        if code >= 0:
            key = divmod(code, 8)
            self.live[key] = self.copies(*key)
            for copy in self.live[key]:
                copy.start()
        else:
            key = divmod(-code - 1, 8)
            for copy in self.live.pop(key):
                copy.wait()
            self.arrived(*key)

    def at(self):
        for code in self.table[self.spot]:
            self.act(code)
        self.spot += 1


def axis_index_of(axis, own, order, count):
    return slice(None) if axis in order[:count] else own


def gather_chains(shards, held, send, recv, local, peers, place):
    z, x, k, y = place
    mine = {}
    for layer in range(2):
        for kind in range(4):
            i = 4 * layer + kind
            target = held[i].at[y, z, x, k]
            if kind == 0:
                mine[i] = [
                    pltpu.make_async_copy(shards[0].at[layer, t], target.at[:, pl.ds(t * 384, 384)], local.at[i, t])
                    for t in range(3)
                ]
            else:
                mine[i] = [pltpu.make_async_copy(shards[kind].at[layer], target, local.at[i, 0])]
            for copy in mine[i]:
                copy.start()

    def put(i):
        for copy in mine.pop(i, ()):
            copy.wait()

    def copies(c, phase):
        i, first, width, order = GATHER_CHAINS[c]
        b, cols = held[i], pl.ds(first, width)
        put(i)

        def remote(source, target, slot, peer):
            return pltpu.make_async_remote_copy(
                source, target, send.at[c, slot], recv.at[c, slot], device_id=peers[peer], device_id_type=MESH
            )

        if phase == 3:
            ref = b.at[:, :, :, k, :, cols]
            return [remote(ref, ref, 5, 5)]
        at = [axis_index_of(axis, own_at, order, phase) for axis, own_at in (("y", y), ("z", z), ("x", x))]
        target = b.at[(*at, k, slice(None), cols)]
        if order[phase] == "z":
            return [remote(target, target, j, j) for j in range(3)]
        return [remote(target, target, 3, 3) if order[phase] == "x" else remote(target, target, 4, 4)]

    return Chains(GATHER_TABLE, copies, lambda c, phase: None)


def matrix(ref, *lead):
    value = ref[lead] if lead else ref[...]
    return value.reshape(-1, value.shape[-1])


def norm_rows(source, gain_row, shift_row, target):
    def block(t, carry):
        rows = pl.ds(pl.multiple_of(t * 128, 128), 128)
        target[rows, :] = layer_norm(source[rows, :], gain_row, shift_row).astype(BF16)
        return carry

    lax.fori_loop(0, source.shape[0] // 128, block, 0)


def turn_rows(source, target, k):
    for c in range(2):
        turned = source[:, c * 384 : (c + 1) * 384].T
        for j in range(8):
            block = c * 8 + j
            target[(block + k) % 2, block // 4, (block // 2) % 2] = turned[j * 48 : (j + 1) * 48]


def forward_kernel(*refs):
    n = ITEM_COUNT
    it = iter(refs)

    def take(count):
        return [next(it) for _ in range(count)]

    shards = take(4)
    tokens, cotangent, lengths, gain, shift, outb, qvb, upb = take(8)
    whole = take(n)
    saved = [take(9) for _ in range(2)]
    (first_grad,) = take(1)
    held = take(n)
    (stream, middle, normed, turned, turned_mid, project, attended, active, slope, probs, qv_all, up_all) = take(12)
    (grad, to_core, from_core) = take(3)
    send, recv, local, out_sem, core_send, core_recv, small_send, small_recv, whole_sem, grad_sem = take(10)
    place = z, x, k, y = places()
    peers = partners(z, x, k, y)
    chains = gather_chains(shards, held, send, recv, local, peers, place)
    qv_all[y] = qvb[...]
    up_all[y] = upb[...]
    greet(peers)
    chains.at()
    small = [
        pltpu.make_async_remote_copy(
            ref.at[y], ref.at[y], small_send.at[j], small_recv.at[j], device_id=peers[4], device_id_type=MESH
        )
        for j, ref in enumerate((qv_all, up_all))
    ]
    for copy in small:
        copy.start()
    stream[...] = tokens[...].astype(F32)
    length = lengths[y]
    rows = stream.shape[0]
    outgoing = {}

    def save(layer, slot, ref):
        copy = pltpu.make_async_copy(ref, saved[layer][slot], out_sem.at[layer, slot])
        copy.start()
        outgoing[slot] = copy

    def settle(slot):
        if slot in outgoing:
            outgoing.pop(slot).wait()

    back = []

    def keep_weight(i):
        copy = pltpu.make_async_copy(held[i], whole[i], whole_sem.at[i])
        copy.start()
        back.append(copy)

    everything = (slice(None),) * 4
    for layer in range(2):
        w_qkv, w_out, w_up, w_down = held[4 * layer : 4 * layer + 4]
        chains.at()
        settle(2)
        norm_rows(stream, gain[layer, 0:1], shift[layer, 0:1], normed)
        turn_rows(normed, turned, k)
        save(layer, 0, stream)
        save(layer, 2, turned)
        if layer == 0:
            for copy in small:
                copy.wait()
        settle(4)
        for half in range(2):
            chains.at()
            if half == 0:
                keep_weight(4 * layer)

            def third(t, carry):
                cols = pl.ds(pl.multiple_of(t * 384, 128), 384)
                part = mm(normed[...], matrix(w_qkv, half, *everything, cols), ((1,), (0,)))
                bias = jnp.where(t == 1, 0.0, qv_all[half, layer, pl.ds(t // 2, 1)])
                project[half, :, cols] = (part + bias).astype(BF16)
                return carry

            lax.fori_loop(0, 3, third, 0)
        save(layer, 4, project)
        settle(5)

        def pair(j, carry):
            half = j // 3
            at = (j % 3) * 128
            lane = lax.broadcasted_iota(jnp.int32, (1, 128), 1) < 64
            query = project[half, :, pl.ds(pl.multiple_of(at, 128), 128)]
            key = project[half, :, pl.ds(pl.multiple_of(at + 384, 128), 128)]
            value = project[half, :, pl.ds(pl.multiple_of(at + 768, 128), 128)]
            value_t = value.T
            hidden_key = lax.broadcasted_iota(jnp.int32, (rows, 1), 0) >= length
            both = []
            slot = j % 2
            for h in range(2):
                here = lane if h == 0 else jnp.logical_not(lane)
                some = jnp.where(here, key, jnp.zeros_like(key)) * jnp.asarray(HEAD_DIM**-0.5, BF16)
                scores = mm(some, query, ((1,), (1,)))
                scores = jnp.where(hidden_key, -1e30, scores)
                exponent = jnp.exp(scores - jnp.max(scores, axis=0, keepdims=True))
                prob = (exponent * (1.0 / jnp.sum(exponent, axis=0, keepdims=True))).astype(BF16)
                probs[j, h] = prob
                both.append(mm(value_t[h * 64 : (h + 1) * 64], prob, ((1,), (0,))))
            block = jnp.concatenate(both, axis=0).T
            attended[:, pl.ds(pl.multiple_of(j * 128, 128), 128)] = block.astype(BF16)
            return carry

        settle(6)
        chains.at()
        lax.fori_loop(0, 6, pair, 0)
        save(layer, 5, attended)
        save(layer, 6, probs)
        chains.at()
        keep_weight(4 * layer + 1)
        settle(1)

        def mix(c, carry):
            cols = pl.ds(pl.multiple_of(c * 384, 128), 384)
            total = stream[:, cols] + outb[layer, 0:1, cols]
            for half in range(2):
                total += mm(attended[:, half * 384 : (half + 1) * 384], matrix(w_out, half, pl.ds(2 * c, 2)), ((1,), (1,)))
            middle[:, cols] = total
            return carry

        lax.fori_loop(0, 2, mix, 0)
        save(layer, 1, middle)
        chains.at()
        settle(3)
        norm_rows(middle, gain[layer, 1:2], shift[layer, 1:2], normed)
        turn_rows(normed, turned_mid, k)
        save(layer, 3, turned_mid)
        settle(7)
        settle(8)

        def unit(t, carry):
            half = t // 3
            cols = pl.ds(pl.multiple_of((t % 3) * 512, 128), 512)
            hidden = mm(normed[...], matrix(w_up, half, *everything, cols), ((1,), (0,)))
            hidden = hidden + up_all[half, layer : layer + 1, cols]
            cdf = 0.5 * (1.0 + lax.erf(hidden * (0.5**0.5)))
            density = jnp.exp(-0.5 * hidden * hidden) * 0.3989422804014327
            active[half, :, cols] = (hidden * cdf).astype(BF16)
            slope[half, :, cols] = (cdf + hidden * density).astype(BF16)
            return carry

        for t0 in range(0, 6, 3):
            chains.at()
            if t0 == 0:
                keep_weight(4 * layer + 2)
            lax.fori_loop(t0, t0 + 3, unit, 0)
        save(layer, 7, active)
        save(layer, 8, slope)
        chains.at()
        if layer == 1:
            break
        keep_weight(3)
        settle(0)

        def close(c, carry):
            cols = pl.ds(pl.multiple_of(c * 384, 128), 384)
            total = middle[:, cols] + outb[layer, 1:2, cols]
            for half in range(2):
                total += mm(active[half], matrix(w_down, half, pl.ds(2 * c, 2)), ((1,), (1,)))
            stream[:, cols] = total
            return carry

        lax.fori_loop(0, 2, close, 0)

    keep = lax.broadcasted_iota(jnp.int32, (rows, 1), 0) < length
    normed[...] = jnp.where(keep, cotangent[...], jnp.zeros_like(cotangent[...]))
    settle(2)
    turn_rows(normed, turned, k)
    def across(half):
        return pltpu.make_async_remote_copy(
            to_core.at[half], from_core.at[half], core_send.at[half], core_recv.at[half],
            device_id=peers[5], device_id_type=MESH,
        )

    def first_half(half, carry):
        def chunk(t, inner):
            cols = pl.ds(pl.multiple_of(t * 512, 128), 512)
            value = mm(turned[...].reshape(768, rows), active[half, :, cols], ((1,), (0,))).astype(BF16)
            grad[half, :, :, :, cols] = value[:384].reshape(4, 2, 48, 512)
            to_core[half, :, :, :, cols] = value[384:].reshape(4, 2, 48, 512)
            return inner

        lax.fori_loop(0, 3, chunk, 0)
        across(half).start()
        return carry

    lax.fori_loop(0, 2, first_half, 0)
    chains.at()
    for half in range(2):
        across(half).wait()

    def join(t, carry):
        at = (t // 8, (t // 2) % 4, t % 2)
        grad[at] = grad[at] + from_core[at]
        return carry

    lax.fori_loop(0, 16, join, 0)
    back.append(pltpu.make_async_copy(grad, first_grad, grad_sem))
    back[-1].start()
    chains.at()
    keep_weight(7)
    for slot in list(outgoing):
        settle(slot)
    for copy in back:
        copy.wait()


def forward(shards, tokens, cotangent, lengths, gain, shift, outb, qvb, upb):
    rows, width = tokens.shape
    qkv, out, up, down = shards
    widths = [3 * qkv.shape[3], out.shape[2], up.shape[2], down.shape[2]] * 2
    full = [(2, 4, 2, 2, 48, w) for w in widths]
    layer_saves = [
        ((rows, width), F32),
        ((rows, width), F32),
        ((2, 4, 2, 48, rows), BF16),
        ((2, 4, 2, 48, rows), BF16),
        ((2, rows, widths[0]), BF16),
        ((rows, width), BF16),
        ((6, 2, rows, rows), BF16),
        ((2, rows, widths[2]), BF16),
        ((2, rows, widths[2]), BF16),
    ]
    any_spec = pl.BlockSpec(memory_space=pl.ANY)
    vmem_spec = pl.BlockSpec(memory_space=pltpu.VMEM)
    out_shape = (
        [jax.ShapeDtypeStruct(f, BF16) for f in full]
        + [jax.ShapeDtypeStruct(s, t) for s, t in layer_saves * 2]
        + [jax.ShapeDtypeStruct((2, 4, 2, 48, widths[3]), BF16)]
    )
    by_slot = {j: pltpu.VMEM(*layer_saves[j]) for j in range(9)}
    outs = pl.pallas_call(
        forward_kernel,
        out_shape=out_shape,
        in_specs=[any_spec] * 4 + [vmem_spec] * 2 + [pl.BlockSpec(memory_space=pltpu.SMEM)] + [vmem_spec] * 5,
        out_specs=[any_spec] * (ITEM_COUNT + 19),
        scratch_shapes=[pltpu.VMEM(f, BF16) for f in full]
        + [
            by_slot[0],
            by_slot[1],
            pltpu.VMEM((rows, width), BF16),
            by_slot[2],
            by_slot[3],
            by_slot[4],
            by_slot[5],
            by_slot[7],
            by_slot[8],
            by_slot[6],
            pltpu.VMEM((2, *qvb.shape), F32),
            pltpu.VMEM((2, *upb.shape), F32),
            pltpu.VMEM((2, 4, 2, 48, widths[3]), BF16),
            pltpu.VMEM((2, 4, 2, 48, widths[3]), BF16),
            pltpu.VMEM((2, 4, 2, 48, widths[3]), BF16),
            pltpu.SemaphoreType.DMA((len(GATHER_CHAINS), 6)),
            pltpu.SemaphoreType.DMA((len(GATHER_CHAINS), 6)),
            pltpu.SemaphoreType.DMA((ITEM_COUNT, 3)),
            pltpu.SemaphoreType.DMA((2, 9)),
            pltpu.SemaphoreType.DMA((2,)),
            pltpu.SemaphoreType.DMA((2,)),
            pltpu.SemaphoreType.DMA((2,)),
            pltpu.SemaphoreType.DMA((2,)),
            pltpu.SemaphoreType.DMA((ITEM_COUNT,)),
            pltpu.SemaphoreType.DMA,
        ],
        compiler_params=pltpu.CompilerParams(
            collective_id=0, has_side_effects=True, vmem_limit_bytes=VMEM_LIMIT
        ),
        name="forward",
    )(*shards, tokens, cotangent, lengths, gain, shift, outb, qvb, upb)
    return outs[:ITEM_COUNT], [outs[ITEM_COUNT + 9 * l : ITEM_COUNT + 9 * l + 9] for l in range(2)], outs[-1]


def norm_back(source, upstream, gain_row, gradient, rounded):
    def block(t, sums):
        rows = pl.ds(pl.multiple_of(t * 128, 128), 128)
        inputs = source[rows, :]
        centered = inputs - jnp.mean(inputs, axis=-1, keepdims=True)
        rate = lax.rsqrt(jnp.mean(centered * centered, axis=-1, keepdims=True) + EPSILON)
        unit = centered * rate
        above = upstream[rows, :]
        pull = above * gain_row
        along = jnp.mean(pull * unit, axis=-1, keepdims=True)
        total = gradient[rows, :] + rate * (pull - jnp.mean(pull, axis=-1, keepdims=True) - unit * along)
        gradient[rows, :] = total
        if rounded is not None:
            rounded[rows, :] = total.astype(BF16)
        return (
            sums[0] + jnp.sum(above * unit, axis=0, keepdims=True),
            sums[1] + jnp.sum(above, axis=0, keepdims=True),
            sums[2] + jnp.sum(total, axis=0, keepdims=True),
        )

    zero = jnp.zeros((1, source.shape[1]), F32)
    return lax.fori_loop(0, source.shape[0] // 128, block, (zero, zero, zero))


def backward_kernel(*refs):
    n = ITEM_COUNT
    it = iter(refs)

    def take(count):
        return [next(it) for _ in range(count)]

    whole = take(n)
    saved = [take(9) for _ in range(2)]
    first_grad, cotangent, lengths, gain, outb = take(5)
    out_q, out_o, out_u, out_d, token_grad, sums, late, final = take(8)
    outs = (out_q, out_o, out_u, out_d)
    (slot_a, slot_b, stream, middle, turned, turned_mid, project, attended, active, slope, probs) = take(11)
    (gradient, upstream, rounded, left, dattended, dproject) = take(6)
    held = take(4)
    (to_core, from_core) = take(2)
    arrivals = [take(3) for _ in REDUCE_CHAINS]
    small_c, small_x, small_y, small_b, small_z, late_in, late_z = take(7)
    (fetch_sem, prob_sem, core_send, core_recv, send, recv, credit, small_send, small_recv, last_sem, final_sem) = take(11)
    place = z, x, k, y = places()
    peers = partners(z, x, k, y)
    rows = stream.shape[0]

    fetches = {}

    def fetch(name, pairs):
        fetches[name] = [pltpu.make_async_copy(s, t, fetch_sem.at[name, j]) for j, (s, t) in enumerate(pairs)]
        for copy in fetches[name]:
            copy.start()

    def ready(name):
        for copy in fetches.pop(name):
            copy.wait()

    def weights_into(slot, layer, kind):
        w_qkv, w_out, w_up, w_down = whole[4 * layer : 4 * layer + 4]
        if kind == "d":
            return [(w_down, slot)]
        if kind == "u":
            return [(w_up, slot)]
        lead = (slice(None),) * 5
        return [(w_qkv, slot.at[(*lead, pl.ds(0, 1152))]), (w_out, slot.at[(*lead, pl.ds(1152, 384))])]

    SLOT_A, SLOT_B, STREAM, MIDDLE, TURNED, TURNED_MID, PROJECT, ATTENDED, ACTIVE, SLOPE, COT, GRAD = range(12)
    buffers = {
        STREAM: (stream, 0),
        MIDDLE: (middle, 1),
        TURNED: (turned, 2),
        TURNED_MID: (turned_mid, 3),
        PROJECT: (project, 4),
        ATTENDED: (attended, 5),
        ACTIVE: (active, 7),
        SLOPE: (slope, 8),
    }

    def fetch_saved(name, layer):
        target, index = buffers[name]
        fetch(name, [(saved[layer][index], target)])

    def prob_copy(layer, j):
        return pltpu.make_async_copy(saved[layer][6].at[j], probs.at[j % 2], prob_sem.at[j % 2])

    fetch(GRAD, [(first_grad, held[3])])
    fetch(COT, [(cotangent, rounded)])
    fetch(SLOT_A, weights_into(slot_a, 1, "d"))
    for name in (SLOPE, MIDDLE, TURNED_MID):
        fetch_saved(name, 1)
    fetch(SLOT_B, weights_into(slot_b, 1, "u"))
    for name in (ATTENDED, PROJECT, TURNED, STREAM):
        fetch_saved(name, 1)
    fetch_saved(ACTIVE, 0)
    prob_copy(1, 0).start()
    slots = {("d", 1): (SLOT_A, slot_a), ("u", 1): (SLOT_B, slot_b), ("q", 1): (SLOT_A, slot_a),
             ("d", 0): (SLOT_B, slot_b), ("u", 0): (SLOT_A, slot_a), ("q", 0): (SLOT_B, slot_b)}
    greet(peers)

    kinds = [(1, 3), (1, 2), (1, 1), (1, 0), (0, 3), (0, 2), (0, 1), (0, 0)]

    def core_copy(r, half):
        width = held[kinds[r][1]].shape[-1]
        at = (half, slice(None), slice(None), slice(None), pl.ds(0, width))
        return pltpu.make_async_remote_copy(
            to_core.at[at], from_core.at[at], core_send.at[r, half], core_recv.at[r, half],
            device_id=peers[5], device_id_type=MESH,
        )

    def take_core(r):
        b = held[kinds[r][1]]
        width = b.shape[-1]
        for half in range(2):
            core_copy(r, half).wait()

        def block(t, carry):
            at = (t // 8, (t // 2) % 4, t % 2)
            b[at] = b[at] + from_core[(*at, slice(None), pl.ds(0, width))]
            return carry

        lax.fori_loop(0, 16, block, 0)
        if r < n - 1:
            for half in range(2):
                pl.semaphore_signal(credit.at[half], inc=1, device_id=peers[5], device_id_type=MESH)

    def rest_of(order, phase):
        return [(axis, size) for axis, size in (("y", 2), ("z", 4), ("x", 2)) if axis in order[phase + 1 :]]

    def copies(c, phase):
        r, first, width, order = REDUCE_CHAINS[c]
        b, cols = held[kinds[r][1]], pl.ds(first, width)
        target = arrivals[c][phase]
        left_over = order[phase + 1 :]

        def block(axis, there):
            at = []
            for name, own_at in (("y", y), ("z", z), ("x", x)):
                at.append(there if name == axis else slice(None) if name in left_over else own_at)
            return b.at[(*at, slice(None), cols)]

        def remote(source, there, slot, peer):
            return pltpu.make_async_remote_copy(
                source, there, send.at[c, slot], recv.at[c, slot], device_id=peers[peer], device_id_type=MESH
            )

        if order[phase] == "z":
            return [remote(block("z", (z + 1 + j) % 4), target.at[j], j, j) for j in range(3)]
        if order[phase] == "x":
            return [remote(block("x", 1 - x), target, 3, 3)]
        return [remote(block("y", 1 - y), target, 4, 4)]

    def arrived(c, phase):
        r, first, width, order = REDUCE_CHAINS[c]
        layer, kind = kinds[r]
        b, cols = held[kind], pl.ds(first, width)
        source = arrivals[c][phase]
        rest = rest_of(order, phase)
        count = 1
        for _, size in rest:
            count *= size

        def total(t):
            at, inner, stride = {}, [], 1
            for axis, size in reversed(rest):
                at[axis] = (t // stride) % size
                stride *= size
            inner = [at[axis] for axis, _ in rest]
            spot = (at.get("y", y), at.get("z", z), at.get("x", x), slice(None), cols)
            value = b[spot].astype(F32)
            if order[phase] == "z":
                for j in range(3):
                    value += source[(j, *inner)].astype(F32)
            else:
                value += source[tuple(inner)].astype(F32) if inner else source[...].astype(F32)
            return spot, value

        if not rest:
            outs[kind][layer, :, cols] = total(0)[1]
        else:

            def block(t, carry):
                spot, value = total(t)
                b[spot] = value.astype(BF16)
                return carry

            lax.fori_loop(0, count, block, 0)

    early, late_at = len(REDUCE_CHAINS), len(REDUCE_CHAINS) + 1

    def small_copies(c, phase):
        def remote(source, target, slot, peer):
            return pltpu.make_async_remote_copy(
                source, target, small_send.at[slot], small_recv.at[slot], device_id=peers[peer], device_id_type=MESH
            )

        if c == early:
            if phase == 0:
                return [remote(sums.at[1 - k], small_c, 0, 5)]
            if phase == 3:
                small_z[z] = sums[k]
                return [remote(sums.at[k], small_z.at[z], 3 + j, j) for j in range(3)]
            target, slot, peer = ((small_x, 1, 3), (small_y, 2, 4), None, (small_b, 6, 5))[phase - 1]
            return [remote(sums.at[k], target, slot, peer)]
        if phase == 3:
            late_z[z] = late[...]
            return [remote(late, late_z.at[z], 10 + j, j) for j in range(3)]
        return [remote(late, late_in.at[phase], 7 + phase, (5, 3, 4)[phase])]

    def small_arrived(c, phase):
        if c == early:
            if phase == 4:
                sums[1 - k] = small_b[...]
            elif phase == 3:
                sums[k] = (small_z[0] + small_z[1]) + (small_z[2] + small_z[3])
            else:
                sums[k] += (small_c, small_x, small_y)[phase][...]
        elif phase == 3:
            late[...] = (late_z[0] + late_z[1]) + (late_z[2] + late_z[3])
        else:
            late[...] += late_in[phase]

    def any_copies(c, phase):
        return copies(c, phase) if c < early else small_copies(c, phase)

    def any_arrived(c, phase):
        return arrived(c, phase) if c < early else small_arrived(c, phase)

    chains = Chains(REDUCE_TABLE, any_copies, any_arrived)

    def weight_gradient(r, lhs, rhs):
        b = held[kinds[r][1]]
        width = b.shape[-1]
        size = 512 if width % 512 == 0 else 384

        def one(half, carry):
            def chunk(t, inner):
                cols = pl.ds(pl.multiple_of(t * size, 128), size)
                value = mm(lhs[...].reshape(768, rows), rhs(half, cols), ((1,), (0,))).astype(BF16)
                b[half, :, :, :, cols] = value[:384].reshape(4, 2, 48, size)
                to_core[half, :, :, :, cols] = value[384:].reshape(4, 2, 48, size)
                return inner

            lax.fori_loop(0, width // size, chunk, 0)
            if r > 1:
                pl.semaphore_wait(credit.at[half], 1)
            core_copy(r, half).start()
            return carry

        lax.fori_loop(0, 2, one, 0)

    sums[0, 0:2, 0:768] = jnp.zeros((2, 768), F32)
    sums[:, 6:8, :] = jnp.zeros((2, 2, 1536), F32)
    chains.at()
    ready(GRAD)
    chains.at()
    ready(COT)
    keep = lax.broadcasted_iota(jnp.int32, (rows, 1), 0) < lengths[y]
    gradient[...] = jnp.where(keep, rounded[...].astype(F32), 0.0)
    rounded[...] = gradient[...].astype(BF16)
    everything = (slice(None),) * 4

    def place_at(*taken):
        for r in taken:
            take_core(r)
        chains.at()

    for layer in (1, 0):
        first = 0 if layer == 1 else 4
        place_at()
        sums[layer, 2:3, 768:1536] = jnp.sum(gradient[...], axis=0, keepdims=True)
        name, w_down = slots["d", layer]
        if layer == 0:
            turn_rows(rounded, left, k)
            ready(ACTIVE)
            place_at()
            weight_gradient(first, left, lambda half, cols: active[half, :, cols])
        ready(name)
        ready(SLOPE)
        place_at(*([first] if first else []))

        def unit(t, carry):
            half = t // 3
            cols = pl.ds(pl.multiple_of((t % 3) * 512, 128), 512)
            dact = mm(rounded[...], matrix(w_down, half, *everything, cols), ((1,), (0,)))
            dhidden = (dact * slope[half, :, cols].astype(F32)).astype(BF16)
            slope[half, :, cols] = dhidden
            sums[layer, pl.ds(4 + half, 1), cols] = jnp.sum(dhidden.astype(F32), axis=0, keepdims=True)
            return carry

        lax.fori_loop(0, 6, unit, 0)
        if layer == 1:
            fetch(SLOT_A, weights_into(slot_a, 1, "q"))
        else:
            fetch(SLOT_B, weights_into(slot_b, 0, "q"))
            fetch_saved(ACTIVE, 1)
        name, w_up = slots["u", layer]
        ready(name)
        ready(TURNED_MID)
        place_at()
        weight_gradient(first + 1, turned_mid, lambda half, cols: slope[half, :, cols])
        place_at(first + 1)

        def pull_up(c, carry):
            total = mm(slope[0], matrix(w_up, 0, pl.ds(2 * c, 2)), ((1,), (1,)))
            total += mm(slope[1], matrix(w_up, 1, pl.ds(2 * c, 2)), ((1,), (1,)))
            upstream[:, pl.ds(pl.multiple_of(c * 384, 128), 384)] = total
            return carry

        lax.fori_loop(0, 2, pull_up, 0)
        if layer == 1:
            fetch(SLOT_B, weights_into(slot_b, 0, "d"))
            fetch_saved(SLOPE, 0)
            fetch_saved(TURNED_MID, 0)
        else:
            fetch(SLOT_A, weights_into(slot_a, 1, "d"))
        ready(MIDDLE)
        place_at()
        gain_sum, shift_sum, bias_sum = norm_back(middle, upstream, gain[layer, 1:2], gradient, rounded)
        sums[layer, 0:1, 768:1536] = gain_sum
        sums[layer, 1:2, 768:1536] = shift_sum
        sums[layer, 2:3, 0:768] = bias_sum
        fetch_saved(MIDDLE, 1 - layer)
        name, w_qo = slots["q", layer]
        ready(name)
        ready(ATTENDED)
        place_at()
        turn_rows(rounded, left, k)
        weight_gradient(first + 2, left, lambda half, cols: attended[:, pl.ds(pl.multiple_of(half * 384, 128), 384)])

        def pull_out(half, carry):
            dattended[half] = mm(rounded[...], matrix(w_qo, half, *everything, pl.ds(1152, 384)), ((1,), (0,))).astype(BF16)
            return carry

        lax.fori_loop(0, 2, pull_out, 0)
        if layer == 1:
            fetch_saved(ATTENDED, 0)
        ready(PROJECT)
        scale = HEAD_DIM**-0.5

        def pair(j, carry):
            half = j // 3
            at = (j % 3) * 128
            prob_copy(layer, j).wait()

            @pl.when(j < 5)
            def _():
                prob_copy(layer, j + 1).start()

            lane = lax.broadcasted_iota(jnp.int32, (1, 128), 1) < 64
            columns = [pl.ds(pl.multiple_of(at + t * 384, 128), 128) for t in range(3)]
            query, key, value = (project[half, :, c] for c in columns)
            above = dattended[half, :, columns[0]]
            key_t = key.T
            dkeys, dvalues, dqueries = [], [], []
            for h in range(2):
                here = lane if h == 0 else jnp.logical_not(lane)
                prob = probs[j % 2, h]
                dprob = mm(jnp.where(here, value, jnp.zeros_like(value)), above, ((1,), (1,)))
                prob32 = prob.astype(F32)
                both = prob32 * dprob
                dscore = (both - prob32 * jnp.sum(both, axis=0, keepdims=True)).astype(BF16)
                dvalues.append(mm(prob, above, ((1,), (0,))))
                dkeys.append(mm(dscore, query, ((1,), (0,))))
                dqueries.append(mm(key_t[h * 64 : (h + 1) * 64], dscore, ((1,), (0,))))
            dproject[half, :, columns[0]] = (jnp.concatenate(dqueries, axis=0) * scale).T.astype(BF16)
            dproject[half, :, columns[1]] = (jnp.where(lane, dkeys[0], dkeys[1]) * scale).astype(BF16)
            dproject[half, :, columns[2]] = jnp.where(lane, dvalues[0], dvalues[1]).astype(BF16)
            return carry

        place_at(first + 2)
        lax.fori_loop(0, 3, pair, 0)
        place_at()
        lax.fori_loop(3, 6, pair, 0)
        if layer == 1:
            fetch_saved(PROJECT, 0)
            prob_copy(0, 0).start()
        ready(TURNED)
        place_at()
        for half in range(2):
            for t in (0, 2):
                sums[layer, 3:4, (t // 2) * 768 + half * 384 : (t // 2) * 768 + half * 384 + 384] = jnp.sum(
                    dproject[half, :, t * 384 : (t + 1) * 384].astype(F32), axis=0, keepdims=True
                )
        weight_gradient(first + 3, turned, lambda half, cols: dproject[half, :, cols])
        place_at(first + 3)

        def pull_qkv(c, carry):
            rest = (slice(None),) * 3
            total = mm(dproject[0], matrix(w_qo, 0, pl.ds(2 * c, 2), *rest, pl.ds(0, 1152)), ((1,), (1,)))
            total += mm(dproject[1], matrix(w_qo, 1, pl.ds(2 * c, 2), *rest, pl.ds(0, 1152)), ((1,), (1,)))
            upstream[:, pl.ds(pl.multiple_of(c * 384, 128), 384)] = total
            return carry

        lax.fori_loop(0, 2, pull_qkv, 0)
        if layer == 1:
            fetch(SLOT_A, weights_into(slot_a, 0, "u"))
            fetch_saved(TURNED, 0)
        ready(STREAM)
        place_at()
        gain_sum, shift_sum, _ = norm_back(stream, upstream, gain[layer, 0:1], gradient, rounded if layer == 1 else None)
        if layer == 1:
            sums[1, 0:1, 0:768] = gain_sum
            sums[1, 1:2, 0:768] = shift_sum
            fetch_saved(STREAM, 0)
        else:
            late[0:1] = gain_sum
            late[1:2] = shift_sum
    last = pltpu.make_async_copy(gradient, token_grad, last_sem)
    last.start()

    ready(SLOT_A)
    ready(ACTIVE)
    ready(MIDDLE)

    def close(c, carry):
        cols = pl.ds(pl.multiple_of(c * 384, 128), 384)
        total = middle[:, cols] + outb[1, 1:2, cols]
        for half in range(2):
            total += mm(active[half], matrix(slot_a, half, pl.ds(2 * c, 2)), ((1,), (1,)))
        dattended[c] = total.astype(BF16)
        return carry

    chains.at()
    lax.fori_loop(0, 2, close, 0)
    finals = [
        pltpu.make_async_copy(dattended.at[c], final.at[:, pl.ds(c * 384, 384)], final_sem.at[c]) for c in range(2)
    ]
    for copy in finals:
        copy.start()
    chains.at()
    last.wait()
    for copy in finals:
        copy.wait()


def backward(whole, saved, first_grad, cotangent, lengths, gain, outb):
    rows, width = cotangent.shape
    widths = [w.shape[-1] for w in whole[:4]]
    any_spec = pl.BlockSpec(memory_space=pl.ANY)
    vmem_spec = pl.BlockSpec(memory_space=pltpu.VMEM)

    def blocks(*lead):
        return [pltpu.VMEM((*lead, 48, w), BF16) for w in widths]

    def arrival_shapes():
        sizes, shapes = {"y": 2, "z": 4, "x": 2}, []
        for _, _, columns, order in REDUCE_CHAINS:
            for phase in range(3):
                lead = [3] if order[phase] == "z" else []
                lead += [sizes[axis] for axis in "yzx" if axis in order[phase + 1 :]]
                shapes.append(pltpu.VMEM((*lead, 48, columns), BF16))
        return shapes

    wide = widths[2]
    small = (2, 8, wide)
    outs = pl.pallas_call(
        backward_kernel,
        out_shape=[jax.ShapeDtypeStruct((2, 48, w), F32) for w in widths]
        + [
            jax.ShapeDtypeStruct((rows, width), F32),
            jax.ShapeDtypeStruct(small, F32),
            jax.ShapeDtypeStruct((2, width), F32),
            jax.ShapeDtypeStruct((rows, width), BF16),
        ],
        in_specs=[any_spec] * (ITEM_COUNT + 18 + 2) + [pl.BlockSpec(memory_space=pltpu.SMEM), vmem_spec, vmem_spec],
        out_specs=[vmem_spec] * 4 + [any_spec, vmem_spec, vmem_spec, any_spec],
        scratch_shapes=[
            pltpu.VMEM((2, 4, 2, 2, 48, wide), BF16),
            pltpu.VMEM((2, 4, 2, 2, 48, wide), BF16),
            pltpu.VMEM((rows, width), F32),
            pltpu.VMEM((rows, width), F32),
            pltpu.VMEM((2, 4, 2, 48, rows), BF16),
            pltpu.VMEM((2, 4, 2, 48, rows), BF16),
            pltpu.VMEM((2, rows, widths[0]), BF16),
            pltpu.VMEM((rows, width), BF16),
            pltpu.VMEM((2, rows, wide), BF16),
            pltpu.VMEM((2, rows, wide), BF16),
            pltpu.VMEM((2, 2, rows, rows), BF16),
            pltpu.VMEM((rows, width), F32),
            pltpu.VMEM((rows, width), F32),
            pltpu.VMEM((rows, width), BF16),
            pltpu.VMEM((2, 4, 2, 48, rows), BF16),
            pltpu.VMEM((2, rows, width // 2), BF16),
            pltpu.VMEM((2, rows, widths[0]), BF16),
        ]
        + blocks(2, 4, 2)
        + [pltpu.VMEM((2, 4, 2, 48, wide), BF16), pltpu.VMEM((2, 4, 2, 48, wide), BF16)]
        + arrival_shapes()
        + [pltpu.VMEM(small[1:], F32)] * 4
        + [pltpu.VMEM((4, *small[1:]), F32), pltpu.VMEM((3, 2, width), F32), pltpu.VMEM((4, 2, width), F32)]
        + [
            pltpu.SemaphoreType.DMA((12, 2)),
            pltpu.SemaphoreType.DMA((2,)),
            pltpu.SemaphoreType.DMA((ITEM_COUNT, 2)),
            pltpu.SemaphoreType.DMA((ITEM_COUNT, 2)),
            pltpu.SemaphoreType.DMA((len(REDUCE_CHAINS), 5)),
            pltpu.SemaphoreType.DMA((len(REDUCE_CHAINS), 5)),
            pltpu.SemaphoreType.REGULAR((2,)),
            pltpu.SemaphoreType.DMA((13,)),
            pltpu.SemaphoreType.DMA((13,)),
            pltpu.SemaphoreType.DMA,
            pltpu.SemaphoreType.DMA((2,)),
        ],
        compiler_params=pltpu.CompilerParams(
            collective_id=1, has_side_effects=True, vmem_limit_bytes=63 * 2**20
        ),
        name="backward",
    )(*whole, *saved[0], *saved[1], first_grad, cotangent, lengths, gain, outb)
    return outs


def generic_body(dp_size, tokens, lengths, cotangent, norm_gain, norm_shift, qkv_weight, qv_bias,
         out_weight, up_weight, up_bias, down_weight, out_bias):
    part = lax.axis_index("tensor")
    layers = norm_gain.shape[0]
    rows, width = tokens.shape
    length = lax.dynamic_index_in_dim(lengths, part, keepdims=False)
    keep = jnp.arange(rows, dtype=jnp.int32) < length
    own = qkv_weight.shape[1]
    shards = []
    for layer in range(layers):
        shards += [
            qkv_weight[layer].reshape(own, -1),
            out_weight[layer].T,
            up_weight[layer],
            down_weight[layer].T,
        ]
    if False:
        full = [w.reshape(2, width, -1) for w in gather_weights(shards)]
    else:
        full = [
            lax.all_gather(s, ("tensor", "dp"), axis=0).reshape(2, width, -1) for s in shards
        ]
    qv_all = lax.all_gather(qv_bias, "tensor", axis=0)
    upb_all = lax.all_gather(up_bias, "tensor", axis=0)
    scale = HEAD_DIM**-0.5
    stream = tokens.astype(F32)
    saved = []
    for layer in range(layers):
        w_qkv, w_out, w_up, w_down = full[4 * layer : 4 * layer + 4]
        normed = layer_norm(stream, norm_gain[layer, 0], norm_shift[layer, 0]).astype(BF16)
        project = []
        for t in range(2):
            b = jnp.concatenate([qv_all[t, layer, 0], jnp.zeros_like(qv_all[t, layer, 0]), qv_all[t, layer, 1]])
            project.append((mm(normed, w_qkv[t], ((1,), (0,))) + b).astype(BF16))
        third = width // 2
        q, key, val = (
            heads(jnp.concatenate([project[t][:, j * third : (j + 1) * third] for t in range(2)], axis=1))
            for j in range(3)
        )
        scores = jnp.einsum("hqd,hkd->hqk", q, key, preferred_element_type=F32) * scale
        scores = jnp.where(keep[None, None, :], scores, -1e30)
        highest = jnp.max(scores, axis=-1, keepdims=True)
        exponent = jnp.exp(scores - highest)
        probs32 = exponent / jnp.sum(exponent, axis=-1, keepdims=True)
        probs = probs32.astype(BF16)
        attended = flat(jnp.einsum("hqk,hkd->hqd", probs, val, preferred_element_type=F32)).astype(BF16)
        branch = sum(mm(attended[:, t * third : (t + 1) * third], w_out[t], ((1,), (1,))) for t in range(2))
        middle = stream + branch + out_bias[layer, 0]
        normed_mid = layer_norm(middle, norm_gain[layer, 1], norm_shift[layer, 1]).astype(BF16)
        hidden = [mm(normed_mid, w_up[t], ((1,), (0,))) + upb_all[t, layer] for t in range(2)]
        activated = [gelu_exact(h).astype(BF16) for h in hidden]
        branch_mlp = sum(mm(activated[t], w_down[t], ((1,), (1,))) for t in range(2))
        saved.append((stream, middle, normed, q, key, val, probs, attended, normed_mid, hidden, activated))
        stream = middle + branch_mlp + out_bias[layer, 1]
    final = stream.astype(BF16)
    gradient = cotangent.astype(F32) * keep.astype(F32)[:, None]
    grads = [None] * (4 * layers)
    gain, shift, outb, qvb, upb = ([None] * layers for _ in range(5))
    for layer in reversed(range(layers)):
        stream_in, middle, normed, q, key, val, probs, attended, normed_mid, hidden, activated = saved[layer]
        w_qkv, w_out, w_up, w_down = full[4 * layer : 4 * layer + 4]
        third = width // 2
        bias_late = jnp.sum(gradient, axis=0)
        dout = gradient.astype(BF16)
        grads[4 * layer + 3] = jnp.stack([mm(dout, activated[t], ((0,), (0,))).astype(BF16) for t in range(2)])
        dhidden = []
        for t in range(2):
            dact = mm(dout, w_down[t], ((1,), (0,)))
            dhidden.append(jax.vjp(gelu_exact, hidden[t])[1](dact)[0].astype(BF16))
        upb[layer] = jnp.stack([jnp.sum(d.astype(F32), axis=0) for d in dhidden])
        grads[4 * layer + 2] = jnp.stack([mm(normed_mid, d, ((0,), (0,))).astype(BF16) for d in dhidden])
        dnormed_mid = sum(mm(dhidden[t], w_up[t], ((1,), (1,))) for t in range(2))
        pull = jax.vjp(layer_norm, middle, norm_gain[layer, 1], norm_shift[layer, 1])[1]
        dmid, gain_late, shift_late = pull(dnormed_mid)
        dmiddle = gradient + dmid
        bias_early = jnp.sum(dmiddle, axis=0)
        dbranch = dmiddle.astype(BF16)
        dout_t = mm(dbranch, attended, ((0,), (0,))).astype(BF16)
        grads[4 * layer + 1] = halves(dout_t)
        dattended = heads(jnp.concatenate([mm(dbranch, w_out[t], ((1,), (0,))) for t in range(2)], axis=1).astype(BF16))
        p = probs.astype(F32)
        dval = jnp.einsum("hqk,hqd->hkd", probs, dattended, preferred_element_type=F32)
        dprobs = jnp.einsum("hqd,hkd->hqk", dattended, val, preferred_element_type=F32)
        dscores = (p * (dprobs - jnp.sum(p * dprobs, axis=-1, keepdims=True))).astype(BF16)
        dquery = jnp.einsum("hqk,hkd->hqd", dscores, key, preferred_element_type=F32) * scale
        dkey = jnp.einsum("hqk,hqd->hkd", dscores, q, preferred_element_type=F32) * scale
        parts = [flat(a).astype(BF16) for a in (dquery, dkey, dval)]
        dproject = [
            jnp.concatenate([a[:, t * third : (t + 1) * third] for a in parts], axis=1) for t in range(2)
        ]
        qvb[layer] = jnp.stack([jnp.sum(parts[0].astype(F32), axis=0), jnp.sum(parts[2].astype(F32), axis=0)])
        grads[4 * layer] = jnp.stack([mm(normed, d, ((0,), (0,))).astype(BF16) for d in dproject])
        dnormed = sum(mm(dproject[t], w_qkv[t], ((1,), (1,))) for t in range(2))
        pull = jax.vjp(layer_norm, stream_in, norm_gain[layer, 0], norm_shift[layer, 0])[1]
        dfirst, gain_early, shift_early = pull(dnormed)
        gradient = dmiddle + dfirst
        gain[layer] = jnp.stack([gain_early, gain_late])
        shift[layer] = jnp.stack([shift_early, shift_late])
        outb[layer] = jnp.stack([bias_early, bias_late])
    if False:
        reduced = reduce_gradients([g.reshape(2, 4, 2, 2, 48, -1) for g in grads])
    else:
        reduced = [
            lax.psum_scatter(
                g.reshape(2 * dp_size, own, -1).astype(F32), ("tensor", "dp"), scatter_dimension=0
            )
            for g in grads
        ]
    g_gain, g_shift, g_outb, g_qvb, g_upb = lax.psum(
        (jnp.stack(gain), jnp.stack(shift), jnp.stack(outb), jnp.stack(qvb), jnp.stack(upb)),
        ("dp", "tensor"),
    )
    g_qvb = lax.dynamic_slice_in_dim(g_qvb, part * qv_bias.shape[2], qv_bias.shape[2], axis=2)
    g_upb = lax.dynamic_index_in_dim(g_upb, part, axis=1, keepdims=False)
    g_qkv = jnp.stack([reduced[4 * l].reshape(own, 3, -1) for l in range(layers)])
    g_out = jnp.stack([reduced[4 * l + 1].T for l in range(layers)])
    g_up = jnp.stack([reduced[4 * l + 2] for l in range(layers)])
    g_down = jnp.stack([reduced[4 * l + 3].T for l in range(layers)])
    return (final, gradient, g_gain, g_shift, g_qkv, g_qvb, g_out, g_up, g_upb, g_down, g_outb)


def finish_kernel(*refs):
    g_qkv, g_out, g_up, g_down, token_grad, sums, late, final = refs[:8]
    o_final, o_token, o_gain, o_shift, o_qkv, o_qvb, o_out, o_up, o_upb, o_down, o_outb = refs[8:19]
    (sem,) = refs[19:]
    y = lax.axis_index("tensor")
    width = late.shape[1]
    third = width // 2
    pairs = [(token_grad, o_token), (final, o_final), (g_up, o_up), (g_out, o_out), (g_down, o_down)]
    for layer in range(2):
        for t in range(3):
            pairs.append((g_qkv.at[layer, :, pl.ds(t * third, third)], o_qkv.at[layer, t]))
    moves = [pltpu.make_async_copy(source, target, sem.at[j]) for j, (source, target) in enumerate(pairs)]
    for copy in moves:
        copy.start()
    for layer in range(2):
        o_upb[layer : layer + 1] = sums[layer, pl.ds(4 + y, 1)]
        for j in range(2):
            at = slice(j * width, (j + 1) * width)
            here = pl.ds(pl.multiple_of(j * width + y * third, 128), third)
            o_outb[layer, j : j + 1] = sums[layer, 2:3, at]
            o_qvb[layer, j : j + 1] = sums[layer, 3:4, here]
            if layer == 0 and j == 0:
                o_gain[0, 0:1] = late[0:1]
                o_shift[0, 0:1] = late[1:2]
            else:
                o_gain[layer, j : j + 1] = sums[layer, 0:1, at]
                o_shift[layer, j : j + 1] = sums[layer, 1:2, at]
    for copy in moves:
        copy.wait()


def fused_body(tokens, lengths, cotangent, norm_gain, norm_shift, qkv_weight, qv_bias, out_weight, up_weight,
               up_bias, down_weight, out_bias):
    shards = (
        qkv_weight.transpose(0, 2, 1, 3),
        out_weight.transpose(0, 2, 1),
        up_weight,
        down_weight.transpose(0, 2, 1),
    )
    full, saved, first_grad = forward(
        shards, tokens, cotangent, lengths, norm_gain, norm_shift, out_bias, qv_bias, up_bias
    )
    reduced = backward(full, saved, first_grad, cotangent, lengths, norm_gain, out_bias)
    any_spec = pl.BlockSpec(memory_space=pl.ANY)
    vmem_spec = pl.BlockSpec(memory_space=pltpu.VMEM)

    def shape(array, kind=F32):
        return jax.ShapeDtypeStruct(array.shape, kind)

    outs = pl.pallas_call(
        finish_kernel,
        out_shape=(
            shape(tokens, BF16),
            shape(tokens),
            shape(norm_gain),
            shape(norm_shift),
            shape(shards[0]),
            shape(qv_bias),
            shape(shards[1]),
            shape(shards[2]),
            shape(up_bias),
            shape(shards[3]),
            shape(out_bias),
        ),
        in_specs=[vmem_spec] * 8,
        out_specs=(any_spec, any_spec, vmem_spec, vmem_spec, any_spec, vmem_spec, any_spec, any_spec, vmem_spec, any_spec, vmem_spec),
        scratch_shapes=[pltpu.SemaphoreType.DMA((11,))],
        name="finish",
    )(*reduced)
    final, token_grad, gain, shift, g_qkv, qvb, g_out, g_up, upb, g_down, outb = outs
    return (
        final,
        token_grad,
        gain,
        shift,
        g_qkv.transpose(0, 2, 1, 3),
        qvb,
        g_out.transpose(0, 2, 1),
        g_up,
        upb,
        g_down.transpose(0, 2, 1),
        outb,
    )


def solution(mesh):
    use_kernels = mesh.shape["dp"] == 16 and mesh.shape["tensor"] == 2
    return jax.shard_map(
        fused_body if use_kernels else functools.partial(generic_body, mesh.shape["dp"]),
        mesh=mesh,
        in_specs=(
            P(("dp", "tensor"), None),
            P("dp"),
            P(("dp", "tensor"), None),
            P(),
            P(),
            P(None, "dp", None, "tensor"),
            P(None, None, "tensor"),
            P(None, "tensor", "dp"),
            P(None, "dp", "tensor"),
            P(None, "tensor"),
            P(None, "tensor", "dp"),
            P(),
        ),
        out_specs=(
            P(("dp", "tensor"), None),
            P(("dp", "tensor"), None),
            P(),
            P(),
            P(None, "dp", None, "tensor"),
            P(None, None, "tensor"),
            P(None, "tensor", "dp"),
            P(None, "dp", "tensor"),
            P(None, "tensor"),
            P(None, "tensor", "dp"),
            P(),
        ),
        check_vma=False,
    )
```

```python
import functools

import jax
import jax.numpy as jnp
from jax import lax
from jax.experimental import pallas as pl
from jax.experimental.pallas import tpu as pltpu
from jax.sharding import PartitionSpec as P

HEAD_DIM = 64
EPSILON = 1e-06
MESH = pl.DeviceIdType.MESH
VMEM_LIMIT = 60 * 2**20
BF16 = jnp.bfloat16
F32 = jnp.float32
ITEM_COUNT = 8
GATHER_CHAINS = (
    (0, 0, 256, "zxy"),
    (0, 256, 256, "zyx"),
    (0, 512, 384, "zxy"),
    (0, 896, 256, "zyx"),
    (1, 0, 256, "zyx"),
    (1, 256, 128, "zxy"),
    (2, 0, 384, "zxy"),
    (2, 384, 384, "zyx"),
    (2, 768, 384, "zxy"),
    (2, 1152, 384, "zyx"),
    (3, 0, 384, "zxy"),
    (3, 384, 384, "zyx"),
    (3, 768, 384, "zxy"),
    (3, 1152, 384, "zyx"),
    (4, 0, 256, "xyz"),
    (4, 256, 256, "yxz"),
    (4, 512, 384, "zxy"),
    (4, 896, 256, "zyx"),
    (5, 0, 256, "zyx"),
    (5, 256, 128, "zxy"),
    (6, 0, 384, "xzy"),
    (6, 384, 384, "yzx"),
    (6, 768, 384, "zxy"),
    (6, 1152, 384, "zyx"),
    (7, 0, 384, "zxy"),
    (7, 384, 384, "zyx"),
    (7, 768, 384, "zxy"),
    (7, 1152, 384, "zyx"),
)
GATHER_TABLE = (
    (112, 160, 168, 120, 40, 48, 24, 8),
    (),
    (-113, 113, -169, -41, 41, 0, -121, 121, -161, -49, 49, 16, -114, -42, 42, -25, 25, 32, -122, -9, 9, 80, -50, 50, -43, 43, -1, 1, 56, -26, 26, -44, -17, 17, 72, -10, 10, -2, 2, -33, 33, 144, -81, 81, 88, -27, 27, -51, 51, -28, -57, 57, 64, -18, 18, -52, -3, 3, -73, 73, 104, -11, 11, -34, 34, -4, -145, 145, 96, -12, -82, -58, 58, 82, -89, 176, -65, 65, 136, -35, 35, -19, 89, 19, -36, -105, 128, -20),
    (-74, 74, 105, -97, 97, 152, -59, 59, -146, 146),
    (-177, 114, -66, 177, 66),
    (-60, -137, 169, -83, 137, 83, -129, 192, -153, 184, -75, 129, 75, -90, -98, 90, 98, -106),
    (),
    (-84, -76, -147, 106, 147, -115, 122, 115, -67, 67, -178, 153, 178, -148, -116, -138, -68),
    (-130, 138, 130, -170, 216),
    (-193, 161, -99, 99, -91, 170, 91, -185, 185, 200, -100, -92, -179, 179, -107, 193, 107, -154, 154, -180, -108, -123, 208, 123),
    (-131, 131, -139, 139, -124, -217, 217),
    (-186, 186, -132, -140),
    (-155, 155, -171, 171),
    (-162, 162, -218, 218, -156, -194, 194),
    (-172, -201, 201, -209, 209, -187, 187, -163, 163),
    (),
    (-188, -219, 219, -164),
    (-195, 195, -210, 210, -220, -202, 202),
    (-196,),
    (-211, 211, -203, 203),
    (-212, -204),
)


REDUCE_CHAINS = (
    (0, 0, 384, "yzx"),
    (0, 384, 384, "xzy"),
    (0, 768, 384, "yxz"),
    (0, 1152, 384, "xyz"),
    (1, 0, 384, "yxz"),
    (1, 384, 384, "xyz"),
    (1, 768, 384, "yzx"),
    (1, 1152, 384, "xzy"),
    (2, 0, 256, "xyz"),
    (2, 256, 128, "yxz"),
    (3, 0, 256, "yxz"),
    (3, 256, 256, "xyz"),
    (3, 512, 384, "yxz"),
    (3, 896, 256, "xyz"),
    (4, 0, 384, "yxz"),
    (4, 384, 384, "xyz"),
    (4, 768, 384, "yzx"),
    (4, 1152, 384, "xzy"),
    (5, 0, 384, "yxz"),
    (5, 384, 384, "xyz"),
    (5, 768, 384, "yxz"),
    (5, 1152, 384, "xyz"),
    (6, 0, 256, "xyz"),
    (6, 256, 128, "yxz"),
    (7, 0, 256, "yxz"),
    (7, 256, 256, "xyz"),
    (7, 512, 384, "yxz"),
    (7, 896, 256, "xyz"),
)
REDUCE_TABLE = (
    (),
    (24, 8, 0, 16),
    (),
    (),
    (),
    (56, 32, -1, 48, 1, -25, 40),
    (-9, 9, -17, 17, 25),
    (-2,),
    (-33, 72, -57, 33, 57),
    (-10, -41, 2, -49, 41, 49),
    (-18, 64, 18, -26, 10, -73),
    (80, -58, 26, -34, 73, -3, 88, -42, 58, -11, 96),
    (-65, 104, -50, 34, -74, 50, -19, 74, -81, 65),
    (-59, -89, 81, 89, -27, 42),
    (),
    (-35, -105, 136, -75, -97, 112, -51, 120),
    (-66, 128, 66, -82, 97, 82, -43, -90, 105, 90),
    (-137, 168, -113, 144, -67, 137),
    (-83, -121, 113, -91, -129, 121, 129, -106, 160, 106, -98, 152),
    (),
    (-138, 98, -145, 138, -169, 145),
    (-122, 169, -114, 176, -130, 114),
    (-107, 122, -161, 184, -99, -153, 161, -139, 153),
    (224, -115, -146, 200, 146, -170, 208, 170),
    (-185, 192, -123, -177, 185, -225, -154, 177, 154, -162, 225, -147, 162),
    (232, -171),
    (-201, 130, -209, 201, -186, 209, 186, -233, -226, 233, -155, -193, 226, -131, 193, -163, -178, 178, -187, -202, 202, -210, 216, 210, -234, 234, -227, -179, 227, -194, -235, -203, 235, -217, 217, -211, 194, -218, -228, 218, 228, -236, -229, -195, -219),
)


def places():
    dp = lax.axis_index("dp")
    y = lax.axis_index("tensor")
    return dp // 4, (dp // 2) % 2, dp % 2, y


def partners(z, x, k, y):
    def at(z_, x_, k_, y_):
        return {"dp": (z_ * 2 + x_) * 2 + k_, "tensor": y_}

    along_z = [at((z + step) % 4, x, k, y) for step in (1, 2, 3)]
    return along_z + [at(z, 1 - x, k, y), at(z, x, k, 1 - y), at(z, x, 1 - k, y)]


def greet(peers):
    barrier = pltpu.get_barrier_semaphore()
    for peer in peers:
        pl.semaphore_signal(barrier, inc=1, device_id=peer, device_id_type=MESH)
    pl.semaphore_wait(barrier, len(peers))


def layer_norm(inputs, gain_row, shift_row):
    centered = inputs - jnp.mean(inputs, axis=-1, keepdims=True)
    variance = jnp.mean(centered * centered, axis=-1, keepdims=True)
    return centered * lax.rsqrt(variance + EPSILON) * gain_row + shift_row


def gelu_exact(values):
    return jax.nn.gelu(values, approximate=False)


def mm(left, right, contract):
    return lax.dot_general(left, right, (contract, ((), ())), preferred_element_type=F32)


def halves(array):
    return jnp.stack(jnp.split(array, 2, axis=1))


def heads(array):
    return array.reshape(array.shape[0], -1, HEAD_DIM).transpose(1, 0, 2)


def flat(array):
    return array.transpose(1, 0, 2).reshape(array.shape[1], -1)


class Chains:
    def __init__(self, table, copies, arrived):
        self.table, self.copies, self.arrived = table, copies, arrived
        self.live, self.spot = {}, 0

    def act(self, code):
        if code >= 0:
            key = divmod(code, 8)
            self.live[key] = self.copies(*key)
            for copy in self.live[key]:
                copy.start()
        else:
            key = divmod(-code - 1, 8)
            for copy in self.live.pop(key):
                copy.wait()
            self.arrived(*key)

    def at(self):
        for code in self.table[self.spot]:
            self.act(code)
        self.spot += 1


def axis_index_of(axis, own, order, count):
    return slice(None) if axis in order[:count] else own


def gather_chains(shards, held, send, recv, local, peers, place):
    z, x, k, y = place
    mine = {}
    for layer in range(2):
        for kind in range(4):
            i = 4 * layer + kind
            target = held[i].at[y, z, x, k]
            if kind == 0:
                mine[i] = [
                    pltpu.make_async_copy(shards[0].at[layer, t], target.at[:, pl.ds(t * 384, 384)], local.at[i, t])
                    for t in range(3)
                ]
            else:
                mine[i] = [pltpu.make_async_copy(shards[kind].at[layer], target, local.at[i, 0])]
            for copy in mine[i]:
                copy.start()

    def put(i):
        for copy in mine.pop(i, ()):
            copy.wait()

    def copies(c, phase):
        i, first, width, order = GATHER_CHAINS[c]
        b, cols = held[i], pl.ds(first, width)
        put(i)

        def remote(source, target, slot, peer):
            return pltpu.make_async_remote_copy(
                source, target, send.at[c, slot], recv.at[c, slot], device_id=peers[peer], device_id_type=MESH
            )

        if phase == 3:
            ref = b.at[:, :, :, k, :, cols]
            return [remote(ref, ref, 5, 5)]
        at = [axis_index_of(axis, own_at, order, phase) for axis, own_at in (("y", y), ("z", z), ("x", x))]
        target = b.at[(*at, k, slice(None), cols)]
        if order[phase] == "z":
            return [remote(target, target, j, j) for j in range(3)]
        return [remote(target, target, 3, 3) if order[phase] == "x" else remote(target, target, 4, 4)]

    return Chains(GATHER_TABLE, copies, lambda c, phase: None)


def matrix(ref, *lead):
    value = ref[lead] if lead else ref[...]
    return value.reshape(-1, value.shape[-1])


def norm_rows(source, gain_row, shift_row, target):
    def block(t, carry):
        rows = pl.ds(pl.multiple_of(t * 128, 128), 128)
        target[rows, :] = layer_norm(source[rows, :], gain_row, shift_row).astype(BF16)
        return carry

    lax.fori_loop(0, source.shape[0] // 128, block, 0)


def turn_rows(source, target, k):
    for c in range(2):
        turned = source[:, c * 384 : (c + 1) * 384].T
        for j in range(8):
            block = c * 8 + j
            target[(block + k) % 2, block // 4, (block // 2) % 2] = turned[j * 48 : (j + 1) * 48]


def forward_kernel(*refs):
    n = ITEM_COUNT
    it = iter(refs)

    def take(count):
        return [next(it) for _ in range(count)]

    shards = take(4)
    tokens, cotangent, lengths, gain, shift, outb, qvb, upb = take(8)
    whole = take(n)
    saved = [take(9) for _ in range(2)]
    (first_grad,) = take(1)
    held = take(n)
    (stream, middle, normed, turned, turned_mid, project, attended, active, slope, probs, qv_all, up_all) = take(12)
    (grad, to_core, from_core) = take(3)
    send, recv, local, out_sem, core_send, core_recv, small_send, small_recv, whole_sem, grad_sem = take(10)
    place = z, x, k, y = places()
    peers = partners(z, x, k, y)
    chains = gather_chains(shards, held, send, recv, local, peers, place)
    qv_all[y] = qvb[...]
    up_all[y] = upb[...]
    greet(peers)
    chains.at()
    small = [
        pltpu.make_async_remote_copy(
            ref.at[y], ref.at[y], small_send.at[j], small_recv.at[j], device_id=peers[4], device_id_type=MESH
        )
        for j, ref in enumerate((qv_all, up_all))
    ]
    for copy in small:
        copy.start()
    stream[...] = tokens[...].astype(F32)
    length = lengths[y]
    rows = stream.shape[0]
    outgoing = {}

    def save(layer, slot, ref):
        copy = pltpu.make_async_copy(ref, saved[layer][slot], out_sem.at[layer, slot])
        copy.start()
        outgoing[slot] = copy

    def settle(slot):
        if slot in outgoing:
            outgoing.pop(slot).wait()

    back = []

    def keep_weight(i):
        copy = pltpu.make_async_copy(held[i], whole[i], whole_sem.at[i])
        copy.start()
        back.append(copy)

    everything = (slice(None),) * 4
    for layer in range(2):
        w_qkv, w_out, w_up, w_down = held[4 * layer : 4 * layer + 4]
        chains.at()
        settle(2)
        norm_rows(stream, gain[layer, 0:1], shift[layer, 0:1], normed)
        turn_rows(normed, turned, k)
        save(layer, 0, stream)
        save(layer, 2, turned)
        if layer == 0:
            for copy in small:
                copy.wait()
        settle(4)
        for half in range(2):
            chains.at()
            if half == 0:
                keep_weight(4 * layer)

            def third(t, carry):
                cols = pl.ds(pl.multiple_of(t * 384, 128), 384)
                part = mm(normed[...], matrix(w_qkv, half, *everything, cols), ((1,), (0,)))
                bias = jnp.where(t == 1, 0.0, qv_all[half, layer, pl.ds(t // 2, 1)])
                project[half, :, cols] = (part + bias).astype(BF16)
                return carry

            lax.fori_loop(0, 3, third, 0)
        save(layer, 4, project)
        settle(5)

        def pair(j, carry):
            half = j // 3
            at = (j % 3) * 128
            lane = lax.broadcasted_iota(jnp.int32, (1, 128), 1) < 64
            query = project[half, :, pl.ds(pl.multiple_of(at, 128), 128)]
            key = project[half, :, pl.ds(pl.multiple_of(at + 384, 128), 128)]
            value = project[half, :, pl.ds(pl.multiple_of(at + 768, 128), 128)]
            value_t = value.T
            hidden_key = lax.broadcasted_iota(jnp.int32, (rows, 1), 0) >= length
            both = []
            slot = j % 2
            for h in range(2):
                here = lane if h == 0 else jnp.logical_not(lane)
                some = jnp.where(here, key, jnp.zeros_like(key)) * jnp.asarray(HEAD_DIM**-0.5, BF16)
                scores = mm(some, query, ((1,), (1,)))
                scores = jnp.where(hidden_key, -1e30, scores)
                exponent = jnp.exp(scores - jnp.max(scores, axis=0, keepdims=True))
                prob = (exponent * (1.0 / jnp.sum(exponent, axis=0, keepdims=True))).astype(BF16)
                probs[j, h] = prob
                both.append(mm(value_t[h * 64 : (h + 1) * 64], prob, ((1,), (0,))))
            block = jnp.concatenate(both, axis=0).T
            attended[:, pl.ds(pl.multiple_of(j * 128, 128), 128)] = block.astype(BF16)
            return carry

        settle(6)
        chains.at()
        lax.fori_loop(0, 6, pair, 0)
        save(layer, 5, attended)
        save(layer, 6, probs)
        chains.at()
        keep_weight(4 * layer + 1)
        settle(1)

        def mix(c, carry):
            cols = pl.ds(pl.multiple_of(c * 384, 128), 384)
            total = stream[:, cols] + outb[layer, 0:1, cols]
            for half in range(2):
                total += mm(attended[:, half * 384 : (half + 1) * 384], matrix(w_out, half, pl.ds(2 * c, 2)), ((1,), (1,)))
            middle[:, cols] = total
            return carry

        lax.fori_loop(0, 2, mix, 0)
        save(layer, 1, middle)
        chains.at()
        settle(3)
        norm_rows(middle, gain[layer, 1:2], shift[layer, 1:2], normed)
        turn_rows(normed, turned_mid, k)
        save(layer, 3, turned_mid)
        settle(7)
        settle(8)

        def unit(t, carry):
            half = t // 3
            cols = pl.ds(pl.multiple_of((t % 3) * 512, 128), 512)
            hidden = mm(normed[...], matrix(w_up, half, *everything, cols), ((1,), (0,)))
            hidden = hidden + up_all[half, layer : layer + 1, cols]
            cdf = 0.5 * (1.0 + lax.erf(hidden * (0.5**0.5)))
            density = jnp.exp(-0.5 * hidden * hidden) * 0.3989422804014327
            active[half, :, cols] = (hidden * cdf).astype(BF16)
            slope[half, :, cols] = (cdf + hidden * density).astype(BF16)
            return carry

        for t0 in range(0, 6, 3):
            chains.at()
            if t0 == 0:
                keep_weight(4 * layer + 2)
            lax.fori_loop(t0, t0 + 3, unit, 0)
        save(layer, 7, active)
        save(layer, 8, slope)
        chains.at()
        if layer == 1:
            break
        keep_weight(3)
        settle(0)

        def close(c, carry):
            cols = pl.ds(pl.multiple_of(c * 384, 128), 384)
            total = middle[:, cols] + outb[layer, 1:2, cols]
            for half in range(2):
                total += mm(active[half], matrix(w_down, half, pl.ds(2 * c, 2)), ((1,), (1,)))
            stream[:, cols] = total
            return carry

        lax.fori_loop(0, 2, close, 0)

    keep = lax.broadcasted_iota(jnp.int32, (rows, 1), 0) < length
    normed[...] = jnp.where(keep, cotangent[...], jnp.zeros_like(cotangent[...]))
    settle(2)
    turn_rows(normed, turned, k)
    def across(half):
        return pltpu.make_async_remote_copy(
            to_core.at[half], from_core.at[half], core_send.at[half], core_recv.at[half],
            device_id=peers[5], device_id_type=MESH,
        )

    def first_half(half, carry):
        def chunk(t, inner):
            cols = pl.ds(pl.multiple_of(t * 512, 128), 512)
            value = mm(turned[...].reshape(768, rows), active[half, :, cols], ((1,), (0,))).astype(BF16)
            grad[half, :, :, :, cols] = value[:384].reshape(4, 2, 48, 512)
            to_core[half, :, :, :, cols] = value[384:].reshape(4, 2, 48, 512)
            return inner

        lax.fori_loop(0, 3, chunk, 0)
        across(half).start()
        return carry

    lax.fori_loop(0, 2, first_half, 0)
    chains.at()
    for half in range(2):
        across(half).wait()

    def join(t, carry):
        at = (t // 8, (t // 2) % 4, t % 2)
        grad[at] = grad[at] + from_core[at]
        return carry

    lax.fori_loop(0, 16, join, 0)
    back.append(pltpu.make_async_copy(grad, first_grad, grad_sem))
    back[-1].start()
    chains.at()
    keep_weight(7)
    for slot in list(outgoing):
        settle(slot)
    for copy in back:
        copy.wait()


def forward(shards, tokens, cotangent, lengths, gain, shift, outb, qvb, upb):
    rows, width = tokens.shape
    qkv, out, up, down = shards
    widths = [3 * qkv.shape[3], out.shape[2], up.shape[2], down.shape[2]] * 2
    full = [(2, 4, 2, 2, 48, w) for w in widths]
    layer_saves = [
        ((rows, width), F32),
        ((rows, width), F32),
        ((2, 4, 2, 48, rows), BF16),
        ((2, 4, 2, 48, rows), BF16),
        ((2, rows, widths[0]), BF16),
        ((rows, width), BF16),
        ((6, 2, rows, rows), BF16),
        ((2, rows, widths[2]), BF16),
        ((2, rows, widths[2]), BF16),
    ]
    any_spec = pl.BlockSpec(memory_space=pl.ANY)
    vmem_spec = pl.BlockSpec(memory_space=pltpu.VMEM)
    out_shape = (
        [jax.ShapeDtypeStruct(f, BF16) for f in full]
        + [jax.ShapeDtypeStruct(s, t) for s, t in layer_saves * 2]
        + [jax.ShapeDtypeStruct((2, 4, 2, 48, widths[3]), BF16)]
    )
    by_slot = {j: pltpu.VMEM(*layer_saves[j]) for j in range(9)}
    outs = pl.pallas_call(
        forward_kernel,
        out_shape=out_shape,
        in_specs=[any_spec] * 4 + [vmem_spec] * 2 + [pl.BlockSpec(memory_space=pltpu.SMEM)] + [vmem_spec] * 5,
        out_specs=[any_spec] * (ITEM_COUNT + 19),
        scratch_shapes=[pltpu.VMEM(f, BF16) for f in full]
        + [
            by_slot[0],
            by_slot[1],
            pltpu.VMEM((rows, width), BF16),
            by_slot[2],
            by_slot[3],
            by_slot[4],
            by_slot[5],
            by_slot[7],
            by_slot[8],
            by_slot[6],
            pltpu.VMEM((2, *qvb.shape), F32),
            pltpu.VMEM((2, *upb.shape), F32),
            pltpu.VMEM((2, 4, 2, 48, widths[3]), BF16),
            pltpu.VMEM((2, 4, 2, 48, widths[3]), BF16),
            pltpu.VMEM((2, 4, 2, 48, widths[3]), BF16),
            pltpu.SemaphoreType.DMA((len(GATHER_CHAINS), 6)),
            pltpu.SemaphoreType.DMA((len(GATHER_CHAINS), 6)),
            pltpu.SemaphoreType.DMA((ITEM_COUNT, 3)),
            pltpu.SemaphoreType.DMA((2, 9)),
            pltpu.SemaphoreType.DMA((2,)),
            pltpu.SemaphoreType.DMA((2,)),
            pltpu.SemaphoreType.DMA((2,)),
            pltpu.SemaphoreType.DMA((2,)),
            pltpu.SemaphoreType.DMA((ITEM_COUNT,)),
            pltpu.SemaphoreType.DMA,
        ],
        compiler_params=pltpu.CompilerParams(
            collective_id=0, has_side_effects=True, vmem_limit_bytes=VMEM_LIMIT
        ),
        name="forward",
    )(*shards, tokens, cotangent, lengths, gain, shift, outb, qvb, upb)
    return outs[:ITEM_COUNT], [outs[ITEM_COUNT + 9 * l : ITEM_COUNT + 9 * l + 9] for l in range(2)], outs[-1]


def norm_back(source, upstream, gain_row, gradient, rounded):
    def block(t, sums):
        rows = pl.ds(pl.multiple_of(t * 128, 128), 128)
        inputs = source[rows, :]
        centered = inputs - jnp.mean(inputs, axis=-1, keepdims=True)
        rate = lax.rsqrt(jnp.mean(centered * centered, axis=-1, keepdims=True) + EPSILON)
        unit = centered * rate
        above = upstream[rows, :]
        pull = above * gain_row
        along = jnp.mean(pull * unit, axis=-1, keepdims=True)
        total = gradient[rows, :] + rate * (pull - jnp.mean(pull, axis=-1, keepdims=True) - unit * along)
        gradient[rows, :] = total
        if rounded is not None:
            rounded[rows, :] = total.astype(BF16)
        return (
            sums[0] + jnp.sum(above * unit, axis=0, keepdims=True),
            sums[1] + jnp.sum(above, axis=0, keepdims=True),
            sums[2] + jnp.sum(total, axis=0, keepdims=True),
        )

    zero = jnp.zeros((1, source.shape[1]), F32)
    return lax.fori_loop(0, source.shape[0] // 128, block, (zero, zero, zero))


def backward_kernel(*refs):
    n = ITEM_COUNT
    it = iter(refs)

    def take(count):
        return [next(it) for _ in range(count)]

    whole = take(n)
    saved = [take(9) for _ in range(2)]
    first_grad, cotangent, lengths, gain, outb = take(5)
    out_q, out_o, out_u, out_d, token_grad, sums, late, final = take(8)
    outs = (out_q, out_o, out_u, out_d)
    (slot_a, slot_b, stream, middle, turned, turned_mid, project, attended, active, slope, probs) = take(11)
    (gradient, upstream, rounded, left, dattended, dproject) = take(6)
    held = take(4)
    (to_core, from_core) = take(2)
    arrivals = [take(3) for _ in REDUCE_CHAINS]
    small_c, small_x, small_y, small_b, small_z, late_in, late_z = take(7)
    (fetch_sem, prob_sem, core_send, core_recv, send, recv, credit, small_send, small_recv, last_sem, final_sem) = take(11)
    place = z, x, k, y = places()
    peers = partners(z, x, k, y)
    rows = stream.shape[0]

    fetches = {}

    def fetch(name, pairs):
        fetches[name] = [pltpu.make_async_copy(s, t, fetch_sem.at[name, j]) for j, (s, t) in enumerate(pairs)]
        for copy in fetches[name]:
            copy.start()

    def ready(name):
        for copy in fetches.pop(name):
            copy.wait()

    def weights_into(slot, layer, kind):
        w_qkv, w_out, w_up, w_down = whole[4 * layer : 4 * layer + 4]
        if kind == "d":
            return [(w_down, slot)]
        if kind == "u":
            return [(w_up, slot)]
        lead = (slice(None),) * 5
        return [(w_qkv, slot.at[(*lead, pl.ds(0, 1152))]), (w_out, slot.at[(*lead, pl.ds(1152, 384))])]

    SLOT_A, SLOT_B, STREAM, MIDDLE, TURNED, TURNED_MID, PROJECT, ATTENDED, ACTIVE, SLOPE, COT, GRAD = range(12)
    buffers = {
        STREAM: (stream, 0),
        MIDDLE: (middle, 1),
        TURNED: (turned, 2),
        TURNED_MID: (turned_mid, 3),
        PROJECT: (project, 4),
        ATTENDED: (attended, 5),
        ACTIVE: (active, 7),
        SLOPE: (slope, 8),
    }

    def fetch_saved(name, layer):
        target, index = buffers[name]
        fetch(name, [(saved[layer][index], target)])

    def prob_copy(layer, j):
        return pltpu.make_async_copy(saved[layer][6].at[j], probs.at[j % 2], prob_sem.at[j % 2])

    fetch(GRAD, [(first_grad, held[3])])
    fetch(COT, [(cotangent, rounded)])
    fetch(SLOT_A, weights_into(slot_a, 1, "d"))
    for name in (SLOPE, MIDDLE, TURNED_MID):
        fetch_saved(name, 1)
    fetch(SLOT_B, weights_into(slot_b, 1, "u"))
    for name in (ATTENDED, PROJECT, TURNED, STREAM):
        fetch_saved(name, 1)
    fetch_saved(ACTIVE, 0)
    prob_copy(1, 0).start()
    slots = {("d", 1): (SLOT_A, slot_a), ("u", 1): (SLOT_B, slot_b), ("q", 1): (SLOT_A, slot_a),
             ("d", 0): (SLOT_B, slot_b), ("u", 0): (SLOT_A, slot_a), ("q", 0): (SLOT_B, slot_b)}
    greet(peers)

    kinds = [(1, 3), (1, 2), (1, 1), (1, 0), (0, 3), (0, 2), (0, 1), (0, 0)]

    def core_copy(r, half):
        width = held[kinds[r][1]].shape[-1]
        at = (half, slice(None), slice(None), slice(None), pl.ds(0, width))
        return pltpu.make_async_remote_copy(
            to_core.at[at], from_core.at[at], core_send.at[r, half], core_recv.at[r, half],
            device_id=peers[5], device_id_type=MESH,
        )

    def take_core(r):
        b = held[kinds[r][1]]
        width = b.shape[-1]
        for half in range(2):
            core_copy(r, half).wait()

        def block(t, carry):
            at = (t // 8, (t // 2) % 4, t % 2)
            b[at] = b[at] + from_core[(*at, slice(None), pl.ds(0, width))]
            return carry

        lax.fori_loop(0, 16, block, 0)
        if r < n - 1:
            for half in range(2):
                pl.semaphore_signal(credit.at[half], inc=1, device_id=peers[5], device_id_type=MESH)

    def rest_of(order, phase):
        return [(axis, size) for axis, size in (("y", 2), ("z", 4), ("x", 2)) if axis in order[phase + 1 :]]

    def copies(c, phase):
        r, first, width, order = REDUCE_CHAINS[c]
        b, cols = held[kinds[r][1]], pl.ds(first, width)
        target = arrivals[c][phase]
        left_over = order[phase + 1 :]

        def block(axis, there):
            at = []
            for name, own_at in (("y", y), ("z", z), ("x", x)):
                at.append(there if name == axis else slice(None) if name in left_over else own_at)
            return b.at[(*at, slice(None), cols)]

        def remote(source, there, slot, peer):
            return pltpu.make_async_remote_copy(
                source, there, send.at[c, slot], recv.at[c, slot], device_id=peers[peer], device_id_type=MESH
            )

        if order[phase] == "z":
            return [remote(block("z", (z + 1 + j) % 4), target.at[j], j, j) for j in range(3)]
        if order[phase] == "x":
            return [remote(block("x", 1 - x), target, 3, 3)]
        return [remote(block("y", 1 - y), target, 4, 4)]

    def arrived(c, phase):
        r, first, width, order = REDUCE_CHAINS[c]
        layer, kind = kinds[r]
        b, cols = held[kind], pl.ds(first, width)
        source = arrivals[c][phase]
        rest = rest_of(order, phase)
        count = 1
        for _, size in rest:
            count *= size

        def total(t):
            at, inner, stride = {}, [], 1
            for axis, size in reversed(rest):
                at[axis] = (t // stride) % size
                stride *= size
            inner = [at[axis] for axis, _ in rest]
            spot = (at.get("y", y), at.get("z", z), at.get("x", x), slice(None), cols)
            value = b[spot].astype(F32)
            if order[phase] == "z":
                for j in range(3):
                    value += source[(j, *inner)].astype(F32)
            else:
                value += source[tuple(inner)].astype(F32) if inner else source[...].astype(F32)
            return spot, value

        if not rest:
            outs[kind][layer, :, cols] = total(0)[1]
        else:

            def block(t, carry):
                spot, value = total(t)
                b[spot] = value.astype(BF16)
                return carry

            lax.fori_loop(0, count, block, 0)

    early, late_at = len(REDUCE_CHAINS), len(REDUCE_CHAINS) + 1

    def small_copies(c, phase):
        def remote(source, target, slot, peer):
            return pltpu.make_async_remote_copy(
                source, target, small_send.at[slot], small_recv.at[slot], device_id=peers[peer], device_id_type=MESH
            )

        if c == early:
            if phase == 0:
                return [remote(sums.at[1 - k], small_c, 0, 5)]
            if phase == 3:
                small_z[z] = sums[k]
                return [remote(sums.at[k], small_z.at[z], 3 + j, j) for j in range(3)]
            target, slot, peer = ((small_x, 1, 3), (small_y, 2, 4), None, (small_b, 6, 5))[phase - 1]
            return [remote(sums.at[k], target, slot, peer)]
        if phase == 3:
            late_z[z] = late[...]
            return [remote(late, late_z.at[z], 10 + j, j) for j in range(3)]
        return [remote(late, late_in.at[phase], 7 + phase, (5, 3, 4)[phase])]

    def small_arrived(c, phase):
        if c == early:
            if phase == 4:
                sums[1 - k] = small_b[...]
            elif phase == 3:
                sums[k] = (small_z[0] + small_z[1]) + (small_z[2] + small_z[3])
            else:
                sums[k] += (small_c, small_x, small_y)[phase][...]
        elif phase == 3:
            late[...] = (late_z[0] + late_z[1]) + (late_z[2] + late_z[3])
        else:
            late[...] += late_in[phase]

    def any_copies(c, phase):
        return copies(c, phase) if c < early else small_copies(c, phase)

    def any_arrived(c, phase):
        return arrived(c, phase) if c < early else small_arrived(c, phase)

    chains = Chains(REDUCE_TABLE, any_copies, any_arrived)

    def weight_gradient(r, lhs, rhs):
        b = held[kinds[r][1]]
        width = b.shape[-1]
        size = 512 if width % 512 == 0 else 384

        def one(half, carry):
            def chunk(t, inner):
                cols = pl.ds(pl.multiple_of(t * size, 128), size)
                value = mm(lhs[...].reshape(768, rows), rhs(half, cols), ((1,), (0,))).astype(BF16)
                b[half, :, :, :, cols] = value[:384].reshape(4, 2, 48, size)
                to_core[half, :, :, :, cols] = value[384:].reshape(4, 2, 48, size)
                return inner

            lax.fori_loop(0, width // size, chunk, 0)
            if r > 1:
                pl.semaphore_wait(credit.at[half], 1)
            core_copy(r, half).start()
            return carry

        lax.fori_loop(0, 2, one, 0)

    sums[0, 0:2, 0:768] = jnp.zeros((2, 768), F32)
    sums[:, 6:8, :] = jnp.zeros((2, 2, 1536), F32)
    chains.at()
    ready(GRAD)
    chains.at()
    ready(COT)
    keep = lax.broadcasted_iota(jnp.int32, (rows, 1), 0) < lengths[y]
    gradient[...] = jnp.where(keep, rounded[...].astype(F32), 0.0)
    rounded[...] = gradient[...].astype(BF16)
    everything = (slice(None),) * 4

    def place_at(*taken):
        for r in taken:
            take_core(r)
        chains.at()

    for layer in (1, 0):
        first = 0 if layer == 1 else 4
        place_at()
        sums[layer, 2:3, 768:1536] = jnp.sum(gradient[...], axis=0, keepdims=True)
        name, w_down = slots["d", layer]
        if layer == 0:
            turn_rows(rounded, left, k)
            ready(ACTIVE)
            place_at()
            weight_gradient(first, left, lambda half, cols: active[half, :, cols])
        ready(name)
        ready(SLOPE)
        place_at(*([first] if first else []))

        def unit(t, carry):
            half = t // 3
            cols = pl.ds(pl.multiple_of((t % 3) * 512, 128), 512)
            dact = mm(rounded[...], matrix(w_down, half, *everything, cols), ((1,), (0,)))
            dhidden = (dact * slope[half, :, cols].astype(F32)).astype(BF16)
            slope[half, :, cols] = dhidden
            sums[layer, pl.ds(4 + half, 1), cols] = jnp.sum(dhidden.astype(F32), axis=0, keepdims=True)
            return carry

        lax.fori_loop(0, 6, unit, 0)
        if layer == 1:
            fetch(SLOT_A, weights_into(slot_a, 1, "q"))
        else:
            fetch(SLOT_B, weights_into(slot_b, 0, "q"))
            fetch_saved(ACTIVE, 1)
        name, w_up = slots["u", layer]
        ready(name)
        ready(TURNED_MID)
        place_at()
        weight_gradient(first + 1, turned_mid, lambda half, cols: slope[half, :, cols])
        place_at(first + 1)

        def pull_up(c, carry):
            total = mm(slope[0], matrix(w_up, 0, pl.ds(2 * c, 2)), ((1,), (1,)))
            total += mm(slope[1], matrix(w_up, 1, pl.ds(2 * c, 2)), ((1,), (1,)))
            upstream[:, pl.ds(pl.multiple_of(c * 384, 128), 384)] = total
            return carry

        lax.fori_loop(0, 2, pull_up, 0)
        if layer == 1:
            fetch(SLOT_B, weights_into(slot_b, 0, "d"))
            fetch_saved(SLOPE, 0)
            fetch_saved(TURNED_MID, 0)
        else:
            fetch(SLOT_A, weights_into(slot_a, 1, "d"))
        ready(MIDDLE)
        place_at()
        gain_sum, shift_sum, bias_sum = norm_back(middle, upstream, gain[layer, 1:2], gradient, rounded)
        sums[layer, 0:1, 768:1536] = gain_sum
        sums[layer, 1:2, 768:1536] = shift_sum
        sums[layer, 2:3, 0:768] = bias_sum
        fetch_saved(MIDDLE, 1 - layer)
        name, w_qo = slots["q", layer]
        ready(name)
        ready(ATTENDED)
        place_at()
        turn_rows(rounded, left, k)
        weight_gradient(first + 2, left, lambda half, cols: attended[:, pl.ds(pl.multiple_of(half * 384, 128), 384)])

        def pull_out(half, carry):
            dattended[half] = mm(rounded[...], matrix(w_qo, half, *everything, pl.ds(1152, 384)), ((1,), (0,))).astype(BF16)
            return carry

        lax.fori_loop(0, 2, pull_out, 0)
        if layer == 1:
            fetch_saved(ATTENDED, 0)
        ready(PROJECT)
        scale = HEAD_DIM**-0.5

        def pair(j, carry):
            half = j // 3
            at = (j % 3) * 128
            prob_copy(layer, j).wait()

            @pl.when(j < 5)
            def _():
                prob_copy(layer, j + 1).start()

            lane = lax.broadcasted_iota(jnp.int32, (1, 128), 1) < 64
            columns = [pl.ds(pl.multiple_of(at + t * 384, 128), 128) for t in range(3)]
            query, key, value = (project[half, :, c] for c in columns)
            above = dattended[half, :, columns[0]]
            key_t = key.T
            dkeys, dvalues, dqueries = [], [], []
            for h in range(2):
                here = lane if h == 0 else jnp.logical_not(lane)
                prob = probs[j % 2, h]
                dprob = mm(jnp.where(here, value, jnp.zeros_like(value)), above, ((1,), (1,)))
                prob32 = prob.astype(F32)
                both = prob32 * dprob
                dscore = (both - prob32 * jnp.sum(both, axis=0, keepdims=True)).astype(BF16)
                dvalues.append(mm(prob, above, ((1,), (0,))))
                dkeys.append(mm(dscore, query, ((1,), (0,))))
                dqueries.append(mm(key_t[h * 64 : (h + 1) * 64], dscore, ((1,), (0,))))
            dproject[half, :, columns[0]] = (jnp.concatenate(dqueries, axis=0) * scale).T.astype(BF16)
            dproject[half, :, columns[1]] = (jnp.where(lane, dkeys[0], dkeys[1]) * scale).astype(BF16)
            dproject[half, :, columns[2]] = jnp.where(lane, dvalues[0], dvalues[1]).astype(BF16)
            return carry

        place_at(first + 2)
        lax.fori_loop(0, 3, pair, 0)
        place_at()
        lax.fori_loop(3, 6, pair, 0)
        if layer == 1:
            fetch_saved(PROJECT, 0)
            prob_copy(0, 0).start()
        ready(TURNED)
        place_at()
        for half in range(2):
            for t in (0, 2):
                sums[layer, 3:4, (t // 2) * 768 + half * 384 : (t // 2) * 768 + half * 384 + 384] = jnp.sum(
                    dproject[half, :, t * 384 : (t + 1) * 384].astype(F32), axis=0, keepdims=True
                )
        weight_gradient(first + 3, turned, lambda half, cols: dproject[half, :, cols])
        place_at(first + 3)

        def pull_qkv(c, carry):
            rest = (slice(None),) * 3
            total = mm(dproject[0], matrix(w_qo, 0, pl.ds(2 * c, 2), *rest, pl.ds(0, 1152)), ((1,), (1,)))
            total += mm(dproject[1], matrix(w_qo, 1, pl.ds(2 * c, 2), *rest, pl.ds(0, 1152)), ((1,), (1,)))
            upstream[:, pl.ds(pl.multiple_of(c * 384, 128), 384)] = total
            return carry

        lax.fori_loop(0, 2, pull_qkv, 0)
        if layer == 1:
            fetch(SLOT_A, weights_into(slot_a, 0, "u"))
            fetch_saved(TURNED, 0)
        ready(STREAM)
        place_at()
        gain_sum, shift_sum, _ = norm_back(stream, upstream, gain[layer, 0:1], gradient, rounded if layer == 1 else None)
        if layer == 1:
            sums[1, 0:1, 0:768] = gain_sum
            sums[1, 1:2, 0:768] = shift_sum
            fetch_saved(STREAM, 0)
        else:
            late[0:1] = gain_sum
            late[1:2] = shift_sum
    last = pltpu.make_async_copy(gradient, token_grad, last_sem)
    last.start()

    ready(SLOT_A)
    ready(ACTIVE)
    ready(MIDDLE)

    def close(c, carry):
        cols = pl.ds(pl.multiple_of(c * 384, 128), 384)
        total = middle[:, cols] + outb[1, 1:2, cols]
        for half in range(2):
            total += mm(active[half], matrix(slot_a, half, pl.ds(2 * c, 2)), ((1,), (1,)))
        dattended[c] = total.astype(BF16)
        return carry

    chains.at()
    lax.fori_loop(0, 2, close, 0)
    finals = [
        pltpu.make_async_copy(dattended.at[c], final.at[:, pl.ds(c * 384, 384)], final_sem.at[c]) for c in range(2)
    ]
    for copy in finals:
        copy.start()
    chains.at()
    last.wait()
    for copy in finals:
        copy.wait()


def backward(whole, saved, first_grad, cotangent, lengths, gain, outb):
    rows, width = cotangent.shape
    widths = [w.shape[-1] for w in whole[:4]]
    any_spec = pl.BlockSpec(memory_space=pl.ANY)
    vmem_spec = pl.BlockSpec(memory_space=pltpu.VMEM)

    def blocks(*lead):
        return [pltpu.VMEM((*lead, 48, w), BF16) for w in widths]

    def arrival_shapes():
        sizes, shapes = {"y": 2, "z": 4, "x": 2}, []
        for _, _, columns, order in REDUCE_CHAINS:
            for phase in range(3):
                lead = [3] if order[phase] == "z" else []
                lead += [sizes[axis] for axis in "yzx" if axis in order[phase + 1 :]]
                shapes.append(pltpu.VMEM((*lead, 48, columns), BF16))
        return shapes

    wide = widths[2]
    small = (2, 8, wide)
    outs = pl.pallas_call(
        backward_kernel,
        out_shape=[jax.ShapeDtypeStruct((2, 48, w), F32) for w in widths]
        + [
            jax.ShapeDtypeStruct((rows, width), F32),
            jax.ShapeDtypeStruct(small, F32),
            jax.ShapeDtypeStruct((2, width), F32),
            jax.ShapeDtypeStruct((rows, width), BF16),
        ],
        in_specs=[any_spec] * (ITEM_COUNT + 18 + 2) + [pl.BlockSpec(memory_space=pltpu.SMEM), vmem_spec, vmem_spec],
        out_specs=[vmem_spec] * 4 + [any_spec, vmem_spec, vmem_spec, any_spec],
        scratch_shapes=[
            pltpu.VMEM((2, 4, 2, 2, 48, wide), BF16),
            pltpu.VMEM((2, 4, 2, 2, 48, wide), BF16),
            pltpu.VMEM((rows, width), F32),
            pltpu.VMEM((rows, width), F32),
            pltpu.VMEM((2, 4, 2, 48, rows), BF16),
            pltpu.VMEM((2, 4, 2, 48, rows), BF16),
            pltpu.VMEM((2, rows, widths[0]), BF16),
            pltpu.VMEM((rows, width), BF16),
            pltpu.VMEM((2, rows, wide), BF16),
            pltpu.VMEM((2, rows, wide), BF16),
            pltpu.VMEM((2, 2, rows, rows), BF16),
            pltpu.VMEM((rows, width), F32),
            pltpu.VMEM((rows, width), F32),
            pltpu.VMEM((rows, width), BF16),
            pltpu.VMEM((2, 4, 2, 48, rows), BF16),
            pltpu.VMEM((2, rows, width // 2), BF16),
            pltpu.VMEM((2, rows, widths[0]), BF16),
        ]
        + blocks(2, 4, 2)
        + [pltpu.VMEM((2, 4, 2, 48, wide), BF16), pltpu.VMEM((2, 4, 2, 48, wide), BF16)]
        + arrival_shapes()
        + [pltpu.VMEM(small[1:], F32)] * 4
        + [pltpu.VMEM((4, *small[1:]), F32), pltpu.VMEM((3, 2, width), F32), pltpu.VMEM((4, 2, width), F32)]
        + [
            pltpu.SemaphoreType.DMA((12, 2)),
            pltpu.SemaphoreType.DMA((2,)),
            pltpu.SemaphoreType.DMA((ITEM_COUNT, 2)),
            pltpu.SemaphoreType.DMA((ITEM_COUNT, 2)),
            pltpu.SemaphoreType.DMA((len(REDUCE_CHAINS), 5)),
            pltpu.SemaphoreType.DMA((len(REDUCE_CHAINS), 5)),
            pltpu.SemaphoreType.REGULAR((2,)),
            pltpu.SemaphoreType.DMA((13,)),
            pltpu.SemaphoreType.DMA((13,)),
            pltpu.SemaphoreType.DMA,
            pltpu.SemaphoreType.DMA((2,)),
        ],
        compiler_params=pltpu.CompilerParams(
            collective_id=1, has_side_effects=True, vmem_limit_bytes=63 * 2**20
        ),
        name="backward",
    )(*whole, *saved[0], *saved[1], first_grad, cotangent, lengths, gain, outb)
    return outs


def generic_body(dp_size, tokens, lengths, cotangent, norm_gain, norm_shift, qkv_weight, qv_bias,
         out_weight, up_weight, up_bias, down_weight, out_bias):
    part = lax.axis_index("tensor")
    layers = norm_gain.shape[0]
    rows, width = tokens.shape
    length = lax.dynamic_index_in_dim(lengths, part, keepdims=False)
    keep = jnp.arange(rows, dtype=jnp.int32) < length
    own = qkv_weight.shape[1]
    shards = []
    for layer in range(layers):
        shards += [
            qkv_weight[layer].reshape(own, -1),
            out_weight[layer].T,
            up_weight[layer],
            down_weight[layer].T,
        ]
    if False:
        full = [w.reshape(2, width, -1) for w in gather_weights(shards)]
    else:
        full = [
            lax.all_gather(s, ("tensor", "dp"), axis=0).reshape(2, width, -1) for s in shards
        ]
    qv_all = lax.all_gather(qv_bias, "tensor", axis=0)
    upb_all = lax.all_gather(up_bias, "tensor", axis=0)
    scale = HEAD_DIM**-0.5
    stream = tokens.astype(F32)
    saved = []
    for layer in range(layers):
        w_qkv, w_out, w_up, w_down = full[4 * layer : 4 * layer + 4]
        normed = layer_norm(stream, norm_gain[layer, 0], norm_shift[layer, 0]).astype(BF16)
        project = []
        for t in range(2):
            b = jnp.concatenate([qv_all[t, layer, 0], jnp.zeros_like(qv_all[t, layer, 0]), qv_all[t, layer, 1]])
            project.append((mm(normed, w_qkv[t], ((1,), (0,))) + b).astype(BF16))
        third = width // 2
        q, key, val = (
            heads(jnp.concatenate([project[t][:, j * third : (j + 1) * third] for t in range(2)], axis=1))
            for j in range(3)
        )
        scores = jnp.einsum("hqd,hkd->hqk", q, key, preferred_element_type=F32) * scale
        scores = jnp.where(keep[None, None, :], scores, -1e30)
        highest = jnp.max(scores, axis=-1, keepdims=True)
        exponent = jnp.exp(scores - highest)
        probs32 = exponent / jnp.sum(exponent, axis=-1, keepdims=True)
        probs = probs32.astype(BF16)
        attended = flat(jnp.einsum("hqk,hkd->hqd", probs, val, preferred_element_type=F32)).astype(BF16)
        branch = sum(mm(attended[:, t * third : (t + 1) * third], w_out[t], ((1,), (1,))) for t in range(2))
        middle = stream + branch + out_bias[layer, 0]
        normed_mid = layer_norm(middle, norm_gain[layer, 1], norm_shift[layer, 1]).astype(BF16)
        hidden = [mm(normed_mid, w_up[t], ((1,), (0,))) + upb_all[t, layer] for t in range(2)]
        activated = [gelu_exact(h).astype(BF16) for h in hidden]
        branch_mlp = sum(mm(activated[t], w_down[t], ((1,), (1,))) for t in range(2))
        saved.append((stream, middle, normed, q, key, val, probs, attended, normed_mid, hidden, activated))
        stream = middle + branch_mlp + out_bias[layer, 1]
    final = stream.astype(BF16)
    gradient = cotangent.astype(F32) * keep.astype(F32)[:, None]
    grads = [None] * (4 * layers)
    gain, shift, outb, qvb, upb = ([None] * layers for _ in range(5))
    for layer in reversed(range(layers)):
        stream_in, middle, normed, q, key, val, probs, attended, normed_mid, hidden, activated = saved[layer]
        w_qkv, w_out, w_up, w_down = full[4 * layer : 4 * layer + 4]
        third = width // 2
        bias_late = jnp.sum(gradient, axis=0)
        dout = gradient.astype(BF16)
        grads[4 * layer + 3] = jnp.stack([mm(dout, activated[t], ((0,), (0,))).astype(BF16) for t in range(2)])
        dhidden = []
        for t in range(2):
            dact = mm(dout, w_down[t], ((1,), (0,)))
            dhidden.append(jax.vjp(gelu_exact, hidden[t])[1](dact)[0].astype(BF16))
        upb[layer] = jnp.stack([jnp.sum(d.astype(F32), axis=0) for d in dhidden])
        grads[4 * layer + 2] = jnp.stack([mm(normed_mid, d, ((0,), (0,))).astype(BF16) for d in dhidden])
        dnormed_mid = sum(mm(dhidden[t], w_up[t], ((1,), (1,))) for t in range(2))
        pull = jax.vjp(layer_norm, middle, norm_gain[layer, 1], norm_shift[layer, 1])[1]
        dmid, gain_late, shift_late = pull(dnormed_mid)
        dmiddle = gradient + dmid
        bias_early = jnp.sum(dmiddle, axis=0)
        dbranch = dmiddle.astype(BF16)
        dout_t = mm(dbranch, attended, ((0,), (0,))).astype(BF16)
        grads[4 * layer + 1] = halves(dout_t)
        dattended = heads(jnp.concatenate([mm(dbranch, w_out[t], ((1,), (0,))) for t in range(2)], axis=1).astype(BF16))
        p = probs.astype(F32)
        dval = jnp.einsum("hqk,hqd->hkd", probs, dattended, preferred_element_type=F32)
        dprobs = jnp.einsum("hqd,hkd->hqk", dattended, val, preferred_element_type=F32)
        dscores = (p * (dprobs - jnp.sum(p * dprobs, axis=-1, keepdims=True))).astype(BF16)
        dquery = jnp.einsum("hqk,hkd->hqd", dscores, key, preferred_element_type=F32) * scale
        dkey = jnp.einsum("hqk,hqd->hkd", dscores, q, preferred_element_type=F32) * scale
        parts = [flat(a).astype(BF16) for a in (dquery, dkey, dval)]
        dproject = [
            jnp.concatenate([a[:, t * third : (t + 1) * third] for a in parts], axis=1) for t in range(2)
        ]
        qvb[layer] = jnp.stack([jnp.sum(parts[0].astype(F32), axis=0), jnp.sum(parts[2].astype(F32), axis=0)])
        grads[4 * layer] = jnp.stack([mm(normed, d, ((0,), (0,))).astype(BF16) for d in dproject])
        dnormed = sum(mm(dproject[t], w_qkv[t], ((1,), (1,))) for t in range(2))
        pull = jax.vjp(layer_norm, stream_in, norm_gain[layer, 0], norm_shift[layer, 0])[1]
        dfirst, gain_early, shift_early = pull(dnormed)
        gradient = dmiddle + dfirst
        gain[layer] = jnp.stack([gain_early, gain_late])
        shift[layer] = jnp.stack([shift_early, shift_late])
        outb[layer] = jnp.stack([bias_early, bias_late])
    if False:
        reduced = reduce_gradients([g.reshape(2, 4, 2, 2, 48, -1) for g in grads])
    else:
        reduced = [
            lax.psum_scatter(
                g.reshape(2 * dp_size, own, -1).astype(F32), ("tensor", "dp"), scatter_dimension=0
            )
            for g in grads
        ]
    g_gain, g_shift, g_outb, g_qvb, g_upb = lax.psum(
        (jnp.stack(gain), jnp.stack(shift), jnp.stack(outb), jnp.stack(qvb), jnp.stack(upb)),
        ("dp", "tensor"),
    )
    g_qvb = lax.dynamic_slice_in_dim(g_qvb, part * qv_bias.shape[2], qv_bias.shape[2], axis=2)
    g_upb = lax.dynamic_index_in_dim(g_upb, part, axis=1, keepdims=False)
    g_qkv = jnp.stack([reduced[4 * l].reshape(own, 3, -1) for l in range(layers)])
    g_out = jnp.stack([reduced[4 * l + 1].T for l in range(layers)])
    g_up = jnp.stack([reduced[4 * l + 2] for l in range(layers)])
    g_down = jnp.stack([reduced[4 * l + 3].T for l in range(layers)])
    return (final, gradient, g_gain, g_shift, g_qkv, g_qvb, g_out, g_up, g_upb, g_down, g_outb)


def finish_kernel(*refs):
    g_qkv, g_out, g_up, g_down, token_grad, sums, late, final = refs[:8]
    o_final, o_token, o_gain, o_shift, o_qkv, o_qvb, o_out, o_up, o_upb, o_down, o_outb = refs[8:19]
    (sem,) = refs[19:]
    y = lax.axis_index("tensor")
    width = late.shape[1]
    third = width // 2
    pairs = [(token_grad, o_token), (final, o_final), (g_up, o_up), (g_out, o_out), (g_down, o_down)]
    for layer in range(2):
        for t in range(3):
            pairs.append((g_qkv.at[layer, :, pl.ds(t * third, third)], o_qkv.at[layer, t]))
    moves = [pltpu.make_async_copy(source, target, sem.at[j]) for j, (source, target) in enumerate(pairs)]
    for copy in moves:
        copy.start()
    for layer in range(2):
        o_upb[layer : layer + 1] = sums[layer, pl.ds(4 + y, 1)]
        for j in range(2):
            at = slice(j * width, (j + 1) * width)
            here = pl.ds(pl.multiple_of(j * width + y * third, 128), third)
            o_outb[layer, j : j + 1] = sums[layer, 2:3, at]
            o_qvb[layer, j : j + 1] = sums[layer, 3:4, here]
            if layer == 0 and j == 0:
                o_gain[0, 0:1] = late[0:1]
                o_shift[0, 0:1] = late[1:2]
            else:
                o_gain[layer, j : j + 1] = sums[layer, 0:1, at]
                o_shift[layer, j : j + 1] = sums[layer, 1:2, at]
    for copy in moves:
        copy.wait()


def fused_body(tokens, lengths, cotangent, norm_gain, norm_shift, qkv_weight, qv_bias, out_weight, up_weight,
               up_bias, down_weight, out_bias):
    shards = (
        qkv_weight.transpose(0, 2, 1, 3),
        out_weight.transpose(0, 2, 1),
        up_weight,
        down_weight.transpose(0, 2, 1),
    )
    full, saved, first_grad = forward(
        shards, tokens, cotangent, lengths, norm_gain, norm_shift, out_bias, qv_bias, up_bias
    )
    reduced = backward(full, saved, first_grad, cotangent, lengths, norm_gain, out_bias)
    any_spec = pl.BlockSpec(memory_space=pl.ANY)
    vmem_spec = pl.BlockSpec(memory_space=pltpu.VMEM)

    def shape(array, kind=F32):
        return jax.ShapeDtypeStruct(array.shape, kind)

    outs = pl.pallas_call(
        finish_kernel,
        out_shape=(
            shape(tokens, BF16),
            shape(tokens),
            shape(norm_gain),
            shape(norm_shift),
            shape(shards[0]),
            shape(qv_bias),
            shape(shards[1]),
            shape(shards[2]),
            shape(up_bias),
            shape(shards[3]),
            shape(out_bias),
        ),
        in_specs=[vmem_spec] * 8,
        out_specs=(any_spec, any_spec, vmem_spec, vmem_spec, any_spec, vmem_spec, any_spec, any_spec, vmem_spec, any_spec, vmem_spec),
        scratch_shapes=[pltpu.SemaphoreType.DMA((11,))],
        name="finish",
    )(*reduced)
    final, token_grad, gain, shift, g_qkv, qvb, g_out, g_up, upb, g_down, outb = outs
    return (
        final,
        token_grad,
        gain,
        shift,
        g_qkv.transpose(0, 2, 1, 3),
        qvb,
        g_out.transpose(0, 2, 1),
        g_up,
        upb,
        g_down.transpose(0, 2, 1),
        outb,
    )


def solution(mesh):
    use_kernels = mesh.shape["dp"] == 16 and mesh.shape["tensor"] == 2
    return jax.shard_map(
        fused_body if use_kernels else functools.partial(generic_body, mesh.shape["dp"]),
        mesh=mesh,
        in_specs=(
            P(("dp", "tensor"), None),
            P("dp"),
            P(("dp", "tensor"), None),
            P(),
            P(),
            P(None, "dp", None, "tensor"),
            P(None, None, "tensor"),
            P(None, "tensor", "dp"),
            P(None, "dp", "tensor"),
            P(None, "tensor"),
            P(None, "tensor", "dp"),
            P(),
        ),
        out_specs=(
            P(("dp", "tensor"), None),
            P(("dp", "tensor"), None),
            P(),
            P(),
            P(None, "dp", None, "tensor"),
            P(None, None, "tensor"),
            P(None, "tensor", "dp"),
            P(None, "dp", "tensor"),
            P(None, "tensor"),
            P(None, "tensor", "dp"),
            P(),
        ),
        check_vma=False,
    )
```
